32 devices in a mesh: groups: 2 (over y), servers: 4 (over z), heads: 4 (over x, core).
Axes of the slice: x: 2, y: 2, z: 4, core: 2. Of those that a mesh axis runs over, the one named last changes fastest.
Arguments:
- grad_out: bfloat16 [4096, 2048], P(('groups', 'servers')), parts along dimension 0, may hold values from -6 to 6
- out_weight: bfloat16 [2048, 4096], P(None, 'heads'), may hold values from -0.125 to 0.125
- queries: bfloat16 [4096, 4096], P(('groups', 'servers'), 'heads'), parts along dimension 0, may hold values from -2.5 to 2.5
- attn_out: bfloat16 [4096, 4096], P(('groups', 'servers'), 'heads'), parts along dimension 0, may hold values from -4 to 4
- lse: float32 [32, 4096], P('heads', ('groups', 'servers')), parts along dimension 1, may hold values from 5 to 6.5
- keys: bfloat16 [4096, 512], P(('groups', 'servers'), 'heads'), parts along dimension 0, may hold values from -2.5 to 2.5
- values: bfloat16 [4096, 512], P(('groups', 'servers'), 'heads'), parts along dimension 0, may hold values from -4 to 4
- prefix_keys: bfloat16 [256, 512], P(('groups', 'servers'), 'heads'), parts along dimension 0, may hold values from -2.5 to 2.5
- prefix_values: bfloat16 [256, 512], P(('groups', 'servers'), 'heads'), parts along dimension 0, may hold values from -4 to 4
- fork_owner: int32 [128, 1], P('groups'), parts along dimension 0, may hold values from 0 to 3; in each aligned block of 16 rows (0 to 15, 16 to 31, ...) at most 8 rows name the same one
- fork_root: int32 [128], P('groups'), parts along dimension 0, may hold values from 0 to 3
- fork_offset: int32 [128], P('groups'), parts along dimension 0, may hold values from 1 to 64
Outputs:
- grad_queries: bfloat16 [4096, 4096], P(('groups', 'servers'), 'heads'), parts along dimension 0
- grad_keys: bfloat16 [4096, 512], P(('groups', 'servers'), 'heads'), parts along dimension 0
- grad_values: bfloat16 [4096, 512], P(('groups', 'servers'), 'heads'), parts along dimension 0
- prefix_grad_keys: bfloat16 [256, 512], P(('groups', 'servers'), 'heads'), parts along dimension 0
- prefix_grad_values: bfloat16 [256, 512], P(('groups', 'servers'), 'heads'), parts along dimension 0
The draws below stay inside these ranges and needn't reach their ends.
There are 2 independent parts, one for each index of `groups`. The reference program is written for one: setup_inputs(seed, part) draws one part's arguments, and reference() takes and returns one part's arrays. A program takes and returns all parts, laid end to end along the dimension named above; an argument that names none is the same for every part. Nothing has to cross between parts.
Inputs may be any that keep to these rules, and one draw needn't show every extreme that they name: `fork_owner`: row g names the owner of the rollout that continuation g forks from. Among the continuations of one owner (aligned blocks of 16 rows) no owner is named more than 8 times.
All inputs are finite; a program needn't handle non-finite values.
Results may differ from the reference program's by a relative error of at most 0.0061.
Values may be sent and summed in bfloat16 or wider, within the bound.
No kernel may reach another device: no remote copies, remote signals or barrier semaphores. Data moves between devices by JAX's collectives and lax.ppermute only.
A program may use at most 128 MiB of HBM per device.

```python
import math
import jax
import jax.numpy as jnp
import numpy as np
from jax import lax

DM = 2048
HQ = 32
KVH = 4
HD = 128
CH_DEV = 16
ROOTS_DEV = 4
RLEN = 64
CLEN = 16
TOK_DEV = 512
TOKENS = 2048
PREFIX = 128
NCH = 64
MOST = 8
N_SERVERS = 4


def plant(values, stream_key, least, largest):
    place = [jax.random.randint(jax.random.fold_in(stream_key, axis), (), 0, length) for axis, length in enumerate(values.shape)]
    widest = values.shape.index(max(values.shape))
    neighbour = place[:widest] + [(place[widest] + 1) % values.shape[widest]] + place[widest + 1:]
    return values.at[tuple(place)].set(least).at[tuple(neighbour)].set(largest)


def levels(rng, dims, cuts, least, largest):
    gain, own = 1.0, jax.random.fold_in(rng, 6)
    for position, blocks in cuts:
        heights = jnp.exp(jax.random.uniform(jax.random.fold_in(own, position), (blocks,), jnp.float32, least / len(cuts), largest / len(cuts)))
        gain = gain * jnp.repeat(heights, dims[position] // blocks).reshape([-1 if axis == position else 1 for axis in range(len(dims))])
    return gain


def shared_out(rng, own, number, rows, count, top, reach, skew):
    order = jax.random.permutation(rng, count)
    heavy_load, usual = shares(count, rows * top, reach, skew, True), shares(count, rows * top, reach, skew, False)
    places = jnp.arange(count)

    def named(lengths, turn):
        used = int((lengths > 0).sum())
        fixed = max(1, used // 4)
        moved = fixed + (places - fixed + turn * (used - fixed)) % max(1, count - fixed)
        return jnp.zeros((count,), jnp.int32).at[order[jnp.where(places < fixed, places, moved)]].set(jnp.asarray(lengths, jnp.int32))

    lengths = jnp.where(number % 4 == 0, named(heavy_load, number // 4), named(usual, number - number // 4 - 1))
    mixed = jax.random.permutation(jax.random.fold_in(own, 3), count)
    giver, receiver = mixed[0:count // 2 * 2:2], mixed[1:count // 2 * 2:2]
    room = jnp.minimum(lengths[giver] - 1, reach - lengths[receiver]) // 2
    room = jnp.where((giver == order[0]) | (receiver == order[0]) | (lengths[receiver] == 0), 0, jnp.maximum(room, 0))
    moved = jax.random.randint(jax.random.fold_in(own, 4), (count // 2,), 0, 1 << 20) % (room + 1)
    lengths = lengths.at[giver].add(-moved).at[receiver].add(moved)
    labels = jnp.searchsorted(jnp.cumsum(lengths), jnp.arange(rows * top), side="right").astype(jnp.int32)
    listing = labels.reshape(top, rows).T
    listing = listing[jax.random.permutation(jax.random.fold_in(own, 1), rows)]
    turn = jax.random.randint(jax.random.fold_in(own, 2), (rows, 1), 0, top)
    return jnp.take_along_axis(listing, (jnp.arange(top)[None, :] + turn) % top, axis=1)


def shares(amount, total, limit, skew, full):
    loads = [(1 << 20) // math.isqrt(rank ** skew) + 1 for rank in range(1, amount + 1)]
    largest = limit if full else min(limit, max(-(-total // amount), total * loads[0] // sum(loads)))
    least = 1 if total - largest >= amount - 1 else 0
    holding, spare = [largest] + [least] * (amount - 1), total - largest - least * (amount - 1)
    while spare > 0:
        movable = [i for i in range(1, amount) if holding[i] < largest] or [i for i in range(1, amount) if holding[i] < limit]
        whole, budget = sum([loads[i] for i in movable]), spare
        for i in movable:
            extra = min(limit - holding[i], max(1, budget * loads[i] // whole), spare)
            holding[i] = holding[i] + extra
            spare = spare - extra
    return np.array(holding)


def scatter_about(own_key, extent, scale, limit, cuts=(), kind=jnp.bfloat16):
    array = scale * jax.random.normal(own_key, extent, jnp.float32)
    if cuts:
        array = array * levels(own_key, extent, cuts, -0.22, 0.18)
    return jnp.clip(array, -limit, limit).astype(kind)


def setup_inputs(seed: int = 0, part: int = 0) -> dict:
    key_of = jax.random.split(jax.random.key(seed), 13)
    part_splits = jax.random.split(jax.random.fold_in(key_of[12], part), 13)
    grad_out = scatter_about(part_splits[0], (TOKENS, DM), 1.0, 6.0, ((0, 4),))
    out_weight = scatter_about(key_of[1], (DM, HQ * HD), DM ** -0.5, 0.125, ((1, 4),))
    queries = scatter_about(part_splits[2], (TOKENS, HQ * HD), 1.0, 2.5, ((0, 4), (1, 4)))
    attn_out = scatter_about(part_splits[3], (TOKENS, HQ * HD), 1.0, 4.0, ((0, 4), (1, 4)))
    lse = jnp.clip(5.0 + 1.5 * jax.random.uniform(part_splits[4], (HQ, TOKENS), jnp.float32) ** levels(part_splits[4], (HQ, TOKENS), ((0, 4), (1, 4)), -0.2, 0.2), 5.0, 6.5)
    keys = scatter_about(part_splits[5], (TOKENS, KVH * HD), 1.0, 2.5, ((0, 4), (1, 4)))
    values = scatter_about(part_splits[6], (TOKENS, KVH * HD), 1.0, 4.0, ((0, 4), (1, 4)))
    prefix_keys = scatter_about(part_splits[7], (PREFIX, KVH * HD), 1.0, 2.5, ((0, 4), (1, 4)))
    prefix_values = scatter_about(part_splits[8], (PREFIX, KVH * HD), 1.0, 4.0, ((0, 4), (1, 4)))
    fork_owner_keys = jax.random.split(jax.random.fold_in(part_splits[9], 1), NCH // CH_DEV)
    fork_owner_turns = jax.random.permutation(jax.random.fold_in(part_splits[9], 3), NCH // CH_DEV)
    fork_owner = jax.vmap(lambda own, number: shared_out(jax.random.fold_in(part_splits[9], 2), own, number, CH_DEV, N_SERVERS, 1, MOST, 2))(fork_owner_keys, fork_owner_turns).reshape((NCH, 1))
    fork_root = plant(jax.random.randint(part_splits[10], (NCH,), 0, ROOTS_DEV), jax.random.fold_in(part_splits[10], 1), 0, ROOTS_DEV - 1).astype(jnp.int32)
    fork_offset = plant(jax.random.randint(part_splits[11], (NCH,), 1, RLEN + 1), jax.random.fold_in(part_splits[11], 1), 1, RLEN).astype(jnp.int32)
    return dict(grad_out=grad_out, out_weight=out_weight, queries=queries, attn_out=attn_out, lse=lse, keys=keys, values=values, prefix_keys=prefix_keys, prefix_values=prefix_values, fork_owner=fork_owner, fork_root=fork_root, fork_offset=fork_offset)


def one_head(query_rows, out_rows, lse_row, delta_row, key_rows, value_rows, allowed, scaling):
    contract = (((1,), (1,)), ((), ()))
    across = (((0,), (0,)), ((), ()))
    query_wide = query_rows.astype(jnp.float32)
    out_wide = out_rows.astype(jnp.float32)
    key_wide = key_rows.astype(jnp.float32)
    value_wide = value_rows.astype(jnp.float32)
    scores = lax.dot_general(query_wide, key_wide, contract, preferred_element_type=jnp.float32) * scaling
    weights = jnp.where(allowed, jnp.exp(scores - lse_row[:, None]), jnp.float32(0.0))
    weights_low = weights.astype(jnp.bfloat16)
    weight_grads = lax.dot_general(out_wide, value_wide, contract, preferred_element_type=jnp.float32)
    score_grads = (weights * (weight_grads - delta_row[:, None])).astype(jnp.bfloat16)
    score_wide = score_grads.astype(jnp.float32)
    grad_value = lax.dot_general(weights_low.astype(jnp.float32), out_wide, across, preferred_element_type=jnp.float32)
    grad_query = jnp.dot(score_wide, key_wide, preferred_element_type=jnp.float32) * scaling
    grad_key = lax.dot_general(score_wide, query_wide, across, preferred_element_type=jnp.float32) * scaling
    return grad_query, grad_key, grad_value


def group_grads(query_heads, out_heads, lse_rows, delta_rows, key_heads, value_heads, allowed):
    group_size = query_heads.shape[1] // key_heads.shape[1]
    scaling = query_heads.shape[2] ** -0.5
    keys_wide = jnp.repeat(key_heads, group_size, axis=1)
    values_wide = jnp.repeat(value_heads, group_size, axis=1)
    mapped = jax.vmap(one_head, in_axes=(1, 1, 0, 0, 1, 1, None, None), out_axes=(1, 1, 1))
    grad_query, grad_key, grad_value = mapped(query_heads, out_heads, lse_rows, delta_rows, keys_wide, values_wide, allowed, scaling)
    key_count = key_heads.shape[0]
    grad_key = grad_key.reshape(key_count, key_heads.shape[1], group_size, -1).sum(axis=2)
    grad_value = grad_value.reshape(key_count, key_heads.shape[1], group_size, -1).sum(axis=2)
    return grad_query, grad_key, grad_value


def segment_rows(source, offset, pieces, length):
    return source[offset:offset + pieces * length].reshape((pieces, length) + source.shape[1:])


def segment_columns(source, offset, pieces, length):
    return jnp.swapaxes(source[:, offset:offset + pieces * length].reshape(source.shape[0], pieces, length), 0, 1)


def reference(grad_out, out_weight, queries, attn_out, lse, keys, values, prefix_keys, prefix_values, fork_owner, fork_root, fork_offset):
    out_grad = jnp.dot(grad_out, out_weight, preferred_element_type=jnp.float32).astype(jnp.bfloat16)
    tokens_all = out_grad.shape[0]
    out_heads = out_grad.reshape(tokens_all, HQ, HD)
    query_heads = queries.reshape(tokens_all, HQ, HD)
    output_heads = attn_out.reshape(tokens_all, HQ, HD)
    delta_rows = jnp.einsum("thd,thd->ht", out_heads.astype(jnp.float32), output_heads.astype(jnp.float32))
    key_heads = keys.reshape(tokens_all, KVH, HD)
    value_heads = values.reshape(tokens_all, KVH, HD)
    prompt_keys = prefix_keys.reshape(PREFIX, KVH, HD)
    prompt_values = prefix_values.reshape(PREFIX, KVH, HD)
    root_rows = ROOTS_DEV * RLEN
    child_rows = CH_DEV * CLEN
    positions = jnp.arange(RLEN, dtype=jnp.int32)
    base_rows = (fork_owner[:, 0] * TOK_DEV + fork_root * RLEN).astype(jnp.int32)
    parent_index = base_rows[:, None] + positions[None, :]
    root_tril = jnp.tril(jnp.ones((RLEN, RLEN), dtype=jnp.bool_))
    child_tril = jnp.tril(jnp.ones((CLEN, CLEN), dtype=jnp.bool_))
    all_open = jnp.ones((1, 1), dtype=jnp.bool_)
    segment_map = jax.vmap(group_grads, in_axes=(0, 0, 0, 0, 0, 0, None))
    parent_map = jax.vmap(group_grads, in_axes=(0, 0, 0, 0, 0, 0, 0))

    def owner_step(totals, owner):
        pre_keys_acc, pre_values_acc, branch_keys_acc, branch_values_acc = totals
        start = (owner * TOK_DEV).astype(jnp.int32)
        owner_query = lax.dynamic_slice_in_dim(query_heads, start, TOK_DEV, 0)
        owner_out = lax.dynamic_slice_in_dim(out_heads, start, TOK_DEV, 0)
        owner_lse = lax.dynamic_slice_in_dim(lse, start, TOK_DEV, 1)
        owner_delta = lax.dynamic_slice_in_dim(delta_rows, start, TOK_DEV, 1)
        owner_keys = lax.dynamic_slice_in_dim(key_heads, start, TOK_DEV, 0)
        owner_values = lax.dynamic_slice_in_dim(value_heads, start, TOK_DEV, 0)
        pre_query_grad, pre_key_grad, pre_value_grad = group_grads(owner_query, owner_out, owner_lse, owner_delta, prompt_keys, prompt_values, all_open)
        root_query_grad, root_key_grad, root_value_grad = segment_map(
            segment_rows(owner_query, 0, ROOTS_DEV, RLEN), segment_rows(owner_out, 0, ROOTS_DEV, RLEN),
            segment_columns(owner_lse, 0, ROOTS_DEV, RLEN), segment_columns(owner_delta, 0, ROOTS_DEV, RLEN),
            segment_rows(owner_keys, 0, ROOTS_DEV, RLEN), segment_rows(owner_values, 0, ROOTS_DEV, RLEN), root_tril)
        child_query = segment_rows(owner_query, root_rows, CH_DEV, CLEN)
        child_out = segment_rows(owner_out, root_rows, CH_DEV, CLEN)
        child_lse = segment_columns(owner_lse, root_rows, CH_DEV, CLEN)
        child_delta = segment_columns(owner_delta, root_rows, CH_DEV, CLEN)
        child_query_grad, child_key_grad, child_value_grad = segment_map(
            child_query, child_out, child_lse, child_delta,
            segment_rows(owner_keys, root_rows, CH_DEV, CLEN), segment_rows(owner_values, root_rows, CH_DEV, CLEN), child_tril)
        first_child = (owner * CH_DEV).astype(jnp.int32)
        owner_index = lax.dynamic_slice_in_dim(parent_index, first_child, CH_DEV, 0)
        owner_offsets = lax.dynamic_slice_in_dim(fork_offset, first_child, CH_DEV, 0)
        parent_keys = key_heads[owner_index]
        parent_values = value_heads[owner_index]
        parent_open = positions[None, None, :] < owner_offsets[:, None, None]
        parent_query_grad, parent_key_grad, parent_value_grad = parent_map(
            child_query, child_out, child_lse, child_delta, parent_keys, parent_values, parent_open)
        grad_query = pre_query_grad + jnp.concatenate([
            root_query_grad.reshape(root_rows, HQ, HD),
            (child_query_grad + parent_query_grad).reshape(child_rows, HQ, HD)], axis=0)
        local_keys = jnp.concatenate([root_key_grad.reshape(root_rows, KVH, HD), child_key_grad.reshape(child_rows, KVH, HD)], axis=0)
        local_values = jnp.concatenate([root_value_grad.reshape(root_rows, KVH, HD), child_value_grad.reshape(child_rows, KVH, HD)], axis=0)
        branch_keys_acc = lax.dynamic_update_slice_in_dim(branch_keys_acc, lax.dynamic_slice_in_dim(branch_keys_acc, start, TOK_DEV, 0) + local_keys, start, 0)
        branch_values_acc = lax.dynamic_update_slice_in_dim(branch_values_acc, lax.dynamic_slice_in_dim(branch_values_acc, start, TOK_DEV, 0) + local_values, start, 0)
        flat_index = owner_index.reshape(-1)
        branch_keys_acc = branch_keys_acc.at[flat_index].add(parent_key_grad.reshape(-1, KVH, HD))
        branch_values_acc = branch_values_acc.at[flat_index].add(parent_value_grad.reshape(-1, KVH, HD))
        totals = (pre_keys_acc + pre_key_grad, pre_values_acc + pre_value_grad, branch_keys_acc, branch_values_acc)
        return totals, grad_query.astype(jnp.bfloat16)

    initial = (jnp.zeros((PREFIX, KVH, HD), jnp.float32), jnp.zeros((PREFIX, KVH, HD), jnp.float32),
               jnp.zeros((tokens_all, KVH, HD), jnp.float32), jnp.zeros((tokens_all, KVH, HD), jnp.float32))
    totals, query_grads = lax.scan(owner_step, initial, jnp.arange(N_SERVERS, dtype=jnp.int32))
    grad_queries = query_grads.reshape(tokens_all, HQ * HD)
    grad_keys = totals[2].reshape(tokens_all, KVH * HD).astype(jnp.bfloat16)
    grad_values = totals[3].reshape(tokens_all, KVH * HD).astype(jnp.bfloat16)
    prefix_grad_keys = totals[0].reshape(PREFIX, KVH * HD).astype(jnp.bfloat16)
    prefix_grad_values = totals[1].reshape(PREFIX, KVH * HD).astype(jnp.bfloat16)
    return grad_queries, grad_keys, grad_values, prefix_grad_keys, prefix_grad_values
```

```python
import jax
import jax.numpy as jnp
from jax import lax
from jax.experimental import pallas as pl
from jax.experimental.pallas import tpu as pltpu
from jax.sharding import PartitionSpec as P

HD = 128
CH_DEV = 16
ROOTS_DEV = 4
RLEN = 64
CLEN = 16
ROOT_ROWS = ROOTS_DEV * RLEN
BLOCK = 64
PER = BLOCK // CLEN
SCALE = HD ** (-0.5)
NT = (((1,), (1,)), ((), ()))
NN = (((1,), (0,)), ((), ()))
TN = (((0,), (0,)), ((), ()))
F32 = jnp.float32
BF16 = jnp.bfloat16
VMEM = pl.BlockSpec(memory_space=pltpu.VMEM)
SMEM = pl.BlockSpec(memory_space=pltpu.SMEM)


def dot(left, right, numbers):
    return lax.dot_general(left, right, numbers, preferred_element_type=F32)


def out_grad_body(grad_ref, weight_ref, attn_ref, out_ref, delta_ref, columns_ref):
    step = pl.program_id(0)
    wide = jnp.dot(grad_ref[...], weight_ref[...], preferred_element_type=F32).astype(BF16)
    out_ref[...] = wide
    products = wide.astype(F32) * attn_ref[...].astype(F32)
    per_step = products.shape[1] // HD
    lane = lax.broadcasted_iota(jnp.int32, columns_ref.shape, 1)

    @pl.when(step == 0)
    def _():
        columns_ref[...] = jnp.zeros(columns_ref.shape, F32)

    columns = columns_ref[...]
    for head in range(per_step):
        total = jnp.sum(products[:, head * HD : (head + 1) * HD], axis=1, keepdims=True)
        columns = jnp.where(lane == step * per_step + head, total, columns)
    columns_ref[...] = columns

    @pl.when(step == pl.num_programs(0) - 1)
    def _():
        delta_ref[...] = jnp.transpose(columns)[: delta_ref.shape[0]]


def out_grad_call(grad_out, out_weight, attn_out):
    rows, model = grad_out.shape
    cols = out_weight.shape[1]
    heads = cols // HD
    width = 2 * HD
    return pl.pallas_call(
        out_grad_body,
        grid=(cols // width,),
        in_specs=[
            pl.BlockSpec((rows, model), lambda i: (0, 0)),
            pl.BlockSpec((model, width), lambda i: (0, i)),
            pl.BlockSpec((rows, width), lambda i: (0, i)),
        ],
        out_specs=[
            pl.BlockSpec((rows, width), lambda i: (0, i)),
            pl.BlockSpec((heads, rows), lambda i: (0, 0)),
        ],
        out_shape=[
            jax.ShapeDtypeStruct((rows, cols), BF16),
            jax.ShapeDtypeStruct((heads, rows), F32),
        ],
        scratch_shapes=[pltpu.VMEM((rows, HD), F32)],
        name="out_grad",
    )(grad_out, out_weight, attn_out)


def stacked(ref, start, heads):
    return jnp.concatenate(
        [ref[start : start + BLOCK, head * HD : (head + 1) * HD] for head in range(heads)], axis=0
    )


def row_of(ref, start, heads):
    return jnp.concatenate([ref[head : head + 1, start : start + BLOCK] for head in range(heads)], axis=1)


def pair_grads(key_part, value_part, query, out, lse, delta, allowed):
    scores = dot(key_part, query, NT) * SCALE
    weights = jnp.exp(scores - lse)
    if allowed is not None:
        weights = jnp.where(allowed, weights, 0.0)
    weight_grads = dot(value_part, out, NT)
    score_grads = (weights * (weight_grads - delta)).astype(BF16)
    value_grad = dot(weights.astype(BF16), out, NN)
    key_grad = dot(score_grads, query, NN) * SCALE
    query_grad = dot(score_grads, key_part, TN)
    return query_grad, key_grad, value_grad


def attend_body(shard_count, part_rows, prompt_rows, extra_prompt, *refs):
    (slot_ref, limit_ref, q_ref, out_ref, lse_ref, delta_ref, key_ref, value_ref) = refs[:8]
    shards = refs[8 : 8 + shard_count]
    refs = refs[8 + shard_count :]
    if extra_prompt:
        extra_ref, refs = refs[0], refs[1:]
    (gq_ref, child_ref, keys_out, values_out, prompt_out, *send_refs) = refs[: 5 + len(refs) - 5 - 3]
    pool_ref, sums_ref, prompt_ref = refs[-3:]
    heads = lse_ref.shape[0]
    tokens = q_ref.shape[0]
    cols = heads * BLOCK
    pool_at = 0
    for shard in shards:
        pool_ref[pool_at : pool_at + shard.shape[0]] = shard[...]
        pool_at += shard.shape[0]
    pool_shards = pool_at // part_rows
    own = prompt_rows
    for index in range(pool_shards):
        at = index * part_rows + 2 * ROOT_ROWS
        prompt_ref[0, index * own : (index + 1) * own] = pool_ref[at : at + own]
        prompt_ref[1, index * own : (index + 1) * own] = pool_ref[at + own : at + 2 * own]
    if extra_prompt:
        prompt_ref[0, pool_shards * own : (pool_shards + 1) * own] = extra_ref[0:own]
        prompt_ref[1, pool_shards * own : (pool_shards + 1) * own] = extra_ref[own : 2 * own]
    sums_ref[...] = jnp.zeros(sums_ref.shape, F32)
    prompt_count = prompt_ref.shape[1]
    chunk = 128
    key_index = lax.broadcasted_iota(jnp.int32, (BLOCK, cols), 0)
    token_index = lax.broadcasted_iota(jnp.int32, (BLOCK, cols), 1) % BLOCK
    root_allowed = key_index <= token_index
    child_allowed = root_allowed & (key_index // CLEN == token_index // CLEN)
    in_child = token_index // CLEN
    prompt_keys = [jnp.zeros((chunk, HD), F32) for _ in range(prompt_count // chunk)]
    prompt_values = [jnp.zeros((chunk, HD), F32) for _ in range(prompt_count // chunk)]
    for block in range(tokens // BLOCK):
        start = block * BLOCK
        query = stacked(q_ref, start, heads)
        out = stacked(out_ref, start, heads)
        lse = row_of(lse_ref, start, heads)
        delta = row_of(delta_ref, start, heads)
        in_root = start < ROOT_ROWS
        total, key_grad, value_grad = pair_grads(
            key_ref[start : start + BLOCK],
            value_ref[start : start + BLOCK],
            query,
            out,
            lse,
            delta,
            root_allowed if in_root else child_allowed,
        )
        keys_out[start : start + BLOCK] = key_grad
        values_out[start : start + BLOCK] = value_grad
        for part in range(prompt_count // chunk):
            query_grad, key_grad, value_grad = pair_grads(
                prompt_ref[0, part * chunk : (part + 1) * chunk],
                prompt_ref[1, part * chunk : (part + 1) * chunk],
                query,
                out,
                lse,
                delta,
                None,
            )
            total = total + query_grad
            prompt_keys[part] = prompt_keys[part] + key_grad
            prompt_values[part] = prompt_values[part] + value_grad
        if not in_root:
            first = (start - ROOT_ROWS) // CLEN
            bases = [pl.multiple_of(slot_ref[first + k], BLOCK) for k in range(PER)]
            key_part = jnp.concatenate([pool_ref[pl.ds(at, RLEN)] for at in bases], axis=0)
            value_part = jnp.concatenate([pool_ref[pl.ds(at + ROOT_ROWS, RLEN)] for at in bases], axis=0)
            allowed = jnp.concatenate(
                [(key_index < limit_ref[first + k]) & (in_child == k) for k in range(PER)], axis=0
            )
            query_grad, key_grad, value_grad = pair_grads(
                key_part, value_part, query, out, lse, delta, allowed
            )
            total = total + query_grad
            for k in range(PER):
                at = bases[k]
                rows = slice(k * RLEN, (k + 1) * RLEN)
                sums_ref[pl.ds(at, RLEN)] = sums_ref[pl.ds(at, RLEN)] + key_grad[rows]
                sums_ref[pl.ds(at + ROOT_ROWS, RLEN)] = (
                    sums_ref[pl.ds(at + ROOT_ROWS, RLEN)] + value_grad[rows]
                )
        total = total * SCALE
        for head in range(heads):
            piece = total[head * BLOCK : (head + 1) * BLOCK]
            if in_root:
                gq_ref[start : start + BLOCK, head * HD : (head + 1) * HD] = piece.astype(BF16)
            else:
                child_ref[start - ROOT_ROWS : start - ROOT_ROWS + BLOCK, head * HD : (head + 1) * HD] = piece
    key_all = jnp.concatenate(prompt_keys, axis=0)
    value_all = jnp.concatenate(prompt_values, axis=0)
    for index in range(pool_shards):
        at = index * part_rows + 2 * ROOT_ROWS
        sums_ref[at : at + own] = key_all[index * own : (index + 1) * own]
        sums_ref[at + own : at + 2 * own] = value_all[index * own : (index + 1) * own]
    if extra_prompt:
        keys_out[0:ROOT_ROWS] = keys_out[0:ROOT_ROWS] + sums_ref[0:ROOT_ROWS]
        values_out[0:ROOT_ROWS] = values_out[0:ROOT_ROWS] + sums_ref[ROOT_ROWS : 2 * ROOT_ROWS]
        prompt_out[...] = sums_ref[2 * ROOT_ROWS : part_rows]
        for index in range(1, pool_shards):
            send_refs[index - 1][...] = sums_ref[index * part_rows : (index + 1) * part_rows].astype(BF16)
        send_refs[-1][0:own] = key_all[pool_shards * own :].astype(BF16)
        send_refs[-1][own : 2 * own] = value_all[pool_shards * own :].astype(BF16)
    else:
        prompt_out[...] = jnp.zeros(prompt_out.shape, F32)
        send_refs[0][...] = sums_ref[...]


def attend_call(slots, limits, queries, out_grad, lse, delta, keys, values, shards, extra, prompt_rows):
    tokens, width = queries.shape
    part_rows = 2 * ROOT_ROWS + 2 * prompt_rows
    pool_rows = sum(shard.shape[0] for shard in shards)
    pool_shards = pool_rows // part_rows
    extra_prompt = extra is not None
    prompt_count = (pool_shards + (1 if extra_prompt else 0)) * prompt_rows
    shapes = [
        jax.ShapeDtypeStruct((tokens, width), BF16),
        jax.ShapeDtypeStruct((tokens - ROOT_ROWS, width), F32),
        jax.ShapeDtypeStruct((tokens, HD), F32),
        jax.ShapeDtypeStruct((tokens, HD), F32),
        jax.ShapeDtypeStruct((2 * prompt_rows, HD), F32),
    ]
    if extra_prompt:
        shapes += [jax.ShapeDtypeStruct((part_rows, HD), BF16)] * (pool_shards - 1)
        shapes += [jax.ShapeDtypeStruct((2 * prompt_rows, HD), BF16)]
    else:
        shapes += [jax.ShapeDtypeStruct((pool_rows, HD), F32)]
    operands = [slots, limits, queries, out_grad, lse, delta, keys, values, *shards]
    if extra_prompt:
        operands.append(extra)

    def body(*refs):
        attend_body(len(shards), part_rows, prompt_rows, extra_prompt, *refs)

    return pl.pallas_call(
        body,
        in_specs=[SMEM, SMEM] + [VMEM] * (len(operands) - 2),
        out_specs=[VMEM] * len(shapes),
        out_shape=shapes,
        scratch_shapes=[
            pltpu.VMEM((pool_rows, HD), BF16),
            pltpu.VMEM((pool_rows, HD), F32),
            pltpu.VMEM((2, prompt_count, HD), BF16),
        ],
        name="attend",
    )(*operands)


def far_body(base_ref, limit_ref, q_ref, out_ref, lse_ref, delta_ref, shard_ref, child_ref, prompt_ref, gq_in, send_ref, gq_ref):
    heads = lse_ref.shape[0]
    cols = heads * BLOCK
    key_index = lax.broadcasted_iota(jnp.int32, (ROOT_ROWS, cols), 0)
    in_child = (lax.broadcasted_iota(jnp.int32, (1, cols), 1) % BLOCK) // CLEN
    key_part = shard_ref[0:ROOT_ROWS]
    value_part = shard_ref[ROOT_ROWS : 2 * ROOT_ROWS]
    key_total = jnp.zeros((ROOT_ROWS, HD), F32)
    value_total = jnp.zeros((ROOT_ROWS, HD), F32)
    for block in range(child_ref.shape[0] // BLOCK):
        start = block * BLOCK
        first = start // CLEN
        low = jnp.zeros((1, cols), jnp.int32)
        high = jnp.zeros((1, cols), jnp.int32)
        for k in range(PER):
            low = jnp.where(in_child == k, base_ref[first + k], low)
            high = jnp.where(in_child == k, base_ref[first + k] + limit_ref[first + k], high)
        allowed = (key_index >= low) & (key_index < high)
        query_grad, key_grad, value_grad = pair_grads(
            key_part,
            value_part,
            stacked(q_ref, ROOT_ROWS + start, heads),
            stacked(out_ref, ROOT_ROWS + start, heads),
            row_of(lse_ref, ROOT_ROWS + start, heads),
            row_of(delta_ref, ROOT_ROWS + start, heads),
            allowed,
        )
        key_total = key_total + key_grad
        value_total = value_total + value_grad
        query_grad = query_grad * SCALE
        for head in range(heads):
            columns = slice(head * HD, (head + 1) * HD)
            gq_ref[start : start + BLOCK, columns] = (
                child_ref[start : start + BLOCK, columns] + query_grad[head * BLOCK : (head + 1) * BLOCK]
            ).astype(BF16)
    send_ref[0:ROOT_ROWS] = key_total.astype(BF16)
    send_ref[ROOT_ROWS : 2 * ROOT_ROWS] = value_total.astype(BF16)
    send_ref[2 * ROOT_ROWS :] = prompt_ref[...]


def far_call(bases, limits, queries, out_grad, lse, delta, shard, child, prompt, gq):
    tokens, width = queries.shape
    return pl.pallas_call(
        far_body,
        grid=(1,),
        in_specs=[SMEM, SMEM] + [VMEM] * 7 + [pl.BlockSpec(memory_space=pl.ANY)],
        out_specs=[VMEM, pl.BlockSpec((tokens - ROOT_ROWS, width), lambda i: (1, 0))],
        out_shape=[jax.ShapeDtypeStruct(shard.shape, BF16), jax.ShapeDtypeStruct(gq.shape, BF16)],
        input_output_aliases={9: 1},
        name="attend_far",
    )(bases, limits, queries, out_grad, lse, delta, shard, child, prompt, gq)


def finish_body(key_ref, value_ref, prompt_ref, *refs):
    parts = refs[:-4]
    keys_out, values_out, prefix_keys_out, prefix_values_out = refs[-4:]
    own = prefix_keys_out.shape[0]
    total = parts[0][...].astype(F32)
    for part in parts[1:]:
        total = total + part[...].astype(F32)
    keys_out[0:ROOT_ROWS] = (key_ref[0:ROOT_ROWS] + total[0:ROOT_ROWS]).astype(BF16)
    keys_out[ROOT_ROWS:] = key_ref[ROOT_ROWS:].astype(BF16)
    values_out[0:ROOT_ROWS] = (value_ref[0:ROOT_ROWS] + total[ROOT_ROWS : 2 * ROOT_ROWS]).astype(BF16)
    values_out[ROOT_ROWS:] = value_ref[ROOT_ROWS:].astype(BF16)
    at = 2 * ROOT_ROWS
    prefix_keys_out[...] = (prompt_ref[0:own] + total[at : at + own]).astype(BF16)
    prefix_values_out[...] = (prompt_ref[own : 2 * own] + total[at + own : at + 2 * own]).astype(BF16)


def finish_call(key_sums, value_sums, prompt_sums, parts):
    own = prompt_sums.shape[0] // 2
    shapes = [jax.ShapeDtypeStruct(key_sums.shape, BF16)] * 2 + [jax.ShapeDtypeStruct((own, HD), BF16)] * 2
    return pl.pallas_call(
        finish_body,
        in_specs=[VMEM] * (3 + len(parts)),
        out_specs=[VMEM] * 4,
        out_shape=shapes,
        name="finish",
    )(key_sums, value_sums, prompt_sums, *parts)


def local(
    grad_out,
    out_weight,
    queries,
    attn_out,
    lse,
    keys,
    values,
    prefix_keys,
    prefix_values,
    fork_owner,
    fork_root,
    fork_offset,
):
    servers_count = lax.axis_size("servers")
    my_index = lax.axis_index("servers")
    prompt_rows = prefix_keys.shape[0]
    part_rows = 2 * ROOT_ROWS + 2 * prompt_rows
    own_part = jnp.concatenate([keys[:ROOT_ROWS], values[:ROOT_ROWS], prefix_keys, prefix_values], axis=0)
    start = my_index * CH_DEV
    my_owners = lax.dynamic_slice_in_dim(fork_owner[:, 0], start, CH_DEV, 0)
    my_roots = lax.dynamic_slice_in_dim(fork_root, start, CH_DEV, 0)
    my_offsets = lax.dynamic_slice_in_dim(fork_offset, start, CH_DEV, 0)
    if servers_count == 4:
        pairs = [[(i, i ^ d) for i in range(4)] for d in range(4)]
        part_two = lax.ppermute(own_part, "servers", pairs[2])
        part_one = lax.ppermute(own_part, "servers", pairs[1])
        prompt_far = lax.ppermute(own_part[2 * ROOT_ROWS :], "servers", pairs[3])
        part_far = lax.ppermute(part_two, "servers", pairs[1])
        out_grad, delta = out_grad_call(grad_out, out_weight, attn_out)
        where = my_owners ^ my_index
        near = where < 3
        slots = jnp.where(near, where * part_rows + my_roots * RLEN, 0)
        near_limits = jnp.where(near, my_offsets, 0)
        far_limits = jnp.where(near, 0, my_offsets)
        gq, child, key_sums, value_sums, prompt_sums, send_one, send_two, prompt_send = attend_call(
            slots,
            near_limits,
            queries,
            out_grad,
            lse,
            delta,
            keys,
            values,
            [own_part, part_one, part_two],
            prompt_far,
            prompt_rows,
        )
        back_one = lax.ppermute(send_one, "servers", pairs[1])
        back_two = lax.ppermute(send_two, "servers", pairs[2])
        send_far, grad_queries = far_call(
            my_roots * RLEN, far_limits, queries, out_grad, lse, delta, part_far, child, prompt_send, gq
        )
        back_far = lax.ppermute(send_far, "servers", pairs[3])
        parts = [back_one, back_two, back_far]
    else:
        all_parts = lax.all_gather(own_part, "servers", axis=0, tiled=True)
        out_grad, delta = out_grad_call(grad_out, out_weight, attn_out)
        slots = my_owners * part_rows + my_roots * RLEN
        gq, child, key_sums, value_sums, prompt_sums, sends = attend_call(
            slots, my_offsets, queries, out_grad, lse, delta, keys, values, [all_parts], None, prompt_rows
        )
        grad_queries = jnp.concatenate([gq[:ROOT_ROWS], child.astype(BF16)], axis=0)
        parts = [lax.psum_scatter(sends, "servers", scatter_dimension=0, tiled=True)]
    grads = finish_call(key_sums, value_sums, prompt_sums, parts)
    return (grad_queries, *grads)


def solution(mesh):
    placed = (
        P(("groups", "servers"), None),
        P(None, "heads"),
        P(("groups", "servers"), "heads"),
        P(("groups", "servers"), "heads"),
        P("heads", ("groups", "servers")),
        P(("groups", "servers"), "heads"),
        P(("groups", "servers"), "heads"),
        P(("groups", "servers"), "heads"),
        P(("groups", "servers"), "heads"),
        P("groups", None),
        P("groups"),
        P("groups"),
    )
    return jax.shard_map(
        local,
        mesh=mesh,
        in_specs=placed,
        out_specs=(P(("groups", "servers"), "heads"),) * 5,
        check_vma=False,
    )
```

```python
import math

import jax
import jax.numpy as jnp
from jax import lax
from jax.experimental import pallas as pl
from jax.experimental.pallas import tpu as pltpu
from jax.sharding import PartitionSpec as P

HD = 128
CH_DEV = 16
ROOTS_DEV = 4
RLEN = 64
CLEN = 16
ROOT_ROWS = ROOTS_DEV * RLEN
BLOCK = 64
PER = BLOCK // CLEN
UNIT_HEADS = 4
UNIT = UNIT_HEADS * BLOCK
SCALE = HD ** (-0.5)
LOG2E = math.log2(math.e)
NT = (((1,), (1,)), ((), ()))
NN = (((1,), (0,)), ((), ()))
TN = (((0,), (0,)), ((), ()))
F32 = jnp.float32
BF16 = jnp.bfloat16
VMEM = pl.BlockSpec(memory_space=pltpu.VMEM)
SMEM = pl.BlockSpec(memory_space=pltpu.SMEM)
ANY = pl.BlockSpec(memory_space=pl.ANY)


def params(mib):
    return pltpu.CompilerParams(vmem_limit_bytes=mib * 1024 * 1024)


def cost(micros):
    return pl.CostEstimate(flops=micros << 30, transcendentals=0, bytes_accessed=1 << 16)


def pinned(array):
    return pltpu.with_memory_space_constraint(array, pltpu.VMEM)


def unmoved(array):
    return pltpu.with_memory_space_constraint(array, pltpu.HBM)


def pinned_scalars(array):
    return pltpu.with_memory_space_constraint(array, pltpu.SMEM)


def kept(shape, dtype):
    return pltpu.VMEM(shape, dtype)


def dot(left, right, numbers):
    return lax.dot_general(left, right, numbers, preferred_element_type=F32)


def pack_body(key_ref, value_ref, prefix_key_ref, prefix_value_ref, part_ref, prompt_ref, sems):
    own = prefix_key_ref.shape[0]
    at = 2 * ROOT_ROWS
    copies = [
        (key_ref.at[0:ROOT_ROWS], part_ref.at[0:ROOT_ROWS]),
        (value_ref.at[0:ROOT_ROWS], part_ref.at[ROOT_ROWS:at]),
        (prefix_key_ref, part_ref.at[at : at + own]),
        (prefix_value_ref, part_ref.at[at + own : at + 2 * own]),
        (prefix_key_ref, prompt_ref.at[0:own]),
        (prefix_value_ref, prompt_ref.at[own : 2 * own]),
    ]
    started = [pltpu.make_async_copy(a, b, sems.at[i]) for i, (a, b) in enumerate(copies)]
    for copy in started:
        copy.start()
    for copy in started:
        copy.wait()


def pack_call(keys, values, prefix_keys, prefix_values):
    own = prefix_keys.shape[0]
    return pl.pallas_call(
        pack_body,
        in_specs=[ANY] * 4,
        out_specs=[VMEM] * 2,
        out_shape=[kept((2 * ROOT_ROWS + 2 * own, HD), BF16), kept((2 * own, HD), BF16)],
        scratch_shapes=[pltpu.SemaphoreType.DMA((6,))],
        compiler_params=params(4),
        cost_estimate=cost(8),
        name="pack",
    )(*(unmoved(x) for x in (keys, values, prefix_keys, prefix_values)))


def out_grad_body(grad_ref, weight_ref, attn_ref, out_ref, delta_ref):
    rows, cols = out_ref.shape
    width = 2 * HD
    lane = lax.broadcasted_iota(jnp.int32, (rows, HD), 1)
    columns = jnp.zeros((rows, HD), F32)
    for step in range(cols // width):
        part = slice(step * width, (step + 1) * width)
        wide = jnp.dot(grad_ref[...], weight_ref[:, part], preferred_element_type=F32).astype(BF16)
        out_ref[:, part] = wide
        products = wide.astype(F32) * attn_ref[:, part].astype(F32)
        for head in range(width // HD):
            total = jnp.sum(products[:, head * HD : (head + 1) * HD], axis=1, keepdims=True)
            columns = jnp.where(lane == step * (width // HD) + head, total, columns)
    delta_ref[...] = jnp.transpose(columns)[: delta_ref.shape[0]]


def out_grad_call(grad_out, out_weight, attn_out):
    rows = grad_out.shape[0]
    cols = out_weight.shape[1]
    return pl.pallas_call(
        out_grad_body,
        in_specs=[VMEM] * 3,
        out_specs=[VMEM] * 2,
        out_shape=[kept((rows, cols), BF16), kept((cols // HD, rows), F32)],
        compiler_params=params(12),
        cost_estimate=cost(6),
        name="out_grad",
    )(pinned(grad_out), pinned(out_weight), pinned(attn_out))


def stacked(ref, start, first):
    return jnp.concatenate(
        [ref[start : start + BLOCK, head * HD : (head + 1) * HD] for head in range(first, first + UNIT_HEADS)],
        axis=0,
    )


def row_of(ref, start, first):
    return jnp.concatenate(
        [ref[head : head + 1, start : start + BLOCK] for head in range(first, first + UNIT_HEADS)], axis=1
    )


def pair_grads(key_part, value_part, query, out, lse, delta, mask):
    weights = mask(jnp.exp2(dot(key_part, query, NT) * (SCALE * LOG2E) - lse * LOG2E))
    weight_grads = dot(value_part, out, NT)
    score_grads = (weights * (weight_grads - delta)).astype(BF16)
    return dot(score_grads, query, NN), dot(weights.astype(BF16), out, NN), score_grads


def places(owner_ref, root_ref, limit_ref, pool_shards, part_rows):
    my_index = lax.axis_index("servers")
    count = lax.axis_size("servers")
    bases, limits = [], []
    for child in range(CH_DEV):
        at = my_index * CH_DEV + child
        slot = owner_ref[at] ^ my_index if count == 4 else owner_ref[at]
        inside = slot < pool_shards
        base = jnp.where(inside, slot * part_rows, 0) + root_ref[at] * RLEN
        bases.append(pl.multiple_of(base, BLOCK))
        limits.append(jnp.where(inside, limit_ref[at], 0))
    return bases, limits


def attend_body(shard_count, part_rows, prompt_rows, has_far, *refs):
    (owner_ref, root_ref, limit_ref, q_ref, out_ref, lse_ref, delta_ref) = refs[:7]
    shards = refs[7 : 7 + shard_count]
    refs = refs[7 + shard_count :]
    if has_far:
        far_ref, refs = refs[0], refs[1:]
    root_ds_ref, child_ds_ref, key_pool_ref, own_ref, *send_refs = refs[:-3]
    pool_ref, sums_ref, values_ref = refs[-3:]
    heads = lse_ref.shape[0]
    tokens = q_ref.shape[0]
    pool_at = 0
    for shard in shards:
        pool_ref[pool_at : pool_at + shard.shape[0]] = shard[...]
        pool_at += shard.shape[0]
    pool_shards = pool_at // part_rows
    bases, limits = places(owner_ref, root_ref, limit_ref, pool_shards, part_rows)
    own = prompt_rows
    prompt_keys, prompt_values = [], []
    for index in range(pool_shards):
        at = index * part_rows + 2 * ROOT_ROWS
        prompt_keys.append(pool_ref[at : at + own])
        prompt_values.append(pool_ref[at + own : at + 2 * own])
    if has_far:
        prompt_keys.append(far_ref[0:own])
        prompt_values.append(far_ref[own : 2 * own])
    prompt_count = own * len(prompt_keys)
    sums_ref[...] = jnp.zeros(sums_ref.shape, F32)
    blocks = key_pool_ref.shape[0]
    for block in range(blocks):
        key_pool_ref[block, 0:prompt_count] = jnp.concatenate(prompt_keys, axis=0)
        for k in range(PER):
            base = bases[block * PER + k]
            at = prompt_count + k * RLEN
            key_pool_ref[block, at : at + RLEN] = pool_ref[pl.ds(base, RLEN)]
            values_ref[block, at : at + RLEN] = pool_ref[pl.ds(base + ROOT_ROWS, RLEN)]
    values_ref[0, 0:prompt_count] = jnp.concatenate(prompt_values, axis=0)
    for block in range(1, blocks):
        values_ref[block, 0:prompt_count] = values_ref[0, 0:prompt_count]
    key_index = lax.broadcasted_iota(jnp.int32, (RLEN, UNIT), 0)
    in_child = (lax.broadcasted_iota(jnp.int32, (RLEN, UNIT), 1) % BLOCK) // CLEN
    prompt_key_sum = jnp.zeros((prompt_count, HD), F32)
    prompt_value_sum = jnp.zeros((prompt_count, HD), F32)
    for block in range(blocks):
        start = ROOT_ROWS + block * BLOCK
        key_sum = jnp.zeros((PER * RLEN, HD), F32)
        value_sum = jnp.zeros((PER * RLEN, HD), F32)

        def mask(weights):
            pieces = [weights[0:prompt_count]]
            for k in range(PER):
                at = prompt_count + k * RLEN
                allowed = (key_index < limits[block * PER + k]) & (in_child == k)
                pieces.append(jnp.where(allowed, weights[at : at + RLEN], 0.0))
            return jnp.concatenate(pieces, axis=0)

        for unit in range(heads // UNIT_HEADS):
            first = unit * UNIT_HEADS
            key_grad, value_grad, score_grads = pair_grads(
                key_pool_ref[block],
                values_ref[block],
                stacked(q_ref, start, first),
                stacked(out_ref, start, first),
                row_of(lse_ref, start, first),
                row_of(delta_ref, start, first),
                mask,
            )
            child_ds_ref[block, unit] = score_grads
            prompt_key_sum = prompt_key_sum + key_grad[0:prompt_count]
            prompt_value_sum = prompt_value_sum + value_grad[0:prompt_count]
            key_sum = key_sum + key_grad[prompt_count:]
            value_sum = value_sum + value_grad[prompt_count:]
        for k in range(PER):
            base = bases[block * PER + k]
            rows = slice(k * RLEN, (k + 1) * RLEN)
            sums_ref[pl.ds(base, RLEN)] = sums_ref[pl.ds(base, RLEN)] + key_sum[rows] * SCALE
            at = base + ROOT_ROWS
            sums_ref[pl.ds(at, RLEN)] = sums_ref[pl.ds(at, RLEN)] + value_sum[rows]
    for block in range(ROOT_ROWS // BLOCK):
        start = block * BLOCK
        for unit in range(heads // UNIT_HEADS):
            first = unit * UNIT_HEADS
            key_grad, value_grad, score_grads = pair_grads(
                key_pool_ref[0, 0:prompt_count],
                values_ref[0, 0:prompt_count],
                stacked(q_ref, start, first),
                stacked(out_ref, start, first),
                row_of(lse_ref, start, first),
                row_of(delta_ref, start, first),
                lambda weights: weights,
            )
            root_ds_ref[block, unit] = score_grads
            prompt_key_sum = prompt_key_sum + key_grad
            prompt_value_sum = prompt_value_sum + value_grad
    prompt_key_sum = prompt_key_sum * SCALE
    for index in range(pool_shards):
        at = index * part_rows + 2 * ROOT_ROWS
        sums_ref[at : at + own] = prompt_key_sum[index * own : (index + 1) * own]
        sums_ref[at + own : at + 2 * own] = prompt_value_sum[index * own : (index + 1) * own]
    if has_far:
        own_ref[...] = sums_ref[0:part_rows]
        for index in range(1, pool_shards):
            send_refs[index - 1][...] = sums_ref[index * part_rows : (index + 1) * part_rows].astype(BF16)
        send_refs[-1][0:own] = prompt_key_sum[pool_shards * own :].astype(BF16)
        send_refs[-1][own : 2 * own] = prompt_value_sum[pool_shards * own :].astype(BF16)
    else:
        own_ref[...] = sums_ref[...]


def attend_call(forks, queries, out_grad, lse, delta, shards, far_prompt, prompt_rows):
    tokens, width = queries.shape
    heads = width // HD
    part_rows = 2 * ROOT_ROWS + 2 * prompt_rows
    pool_rows = sum(shard.shape[0] for shard in shards)
    pool_shards = pool_rows // part_rows
    has_far = far_prompt is not None
    prompt_count = (pool_shards + (1 if has_far else 0)) * prompt_rows
    units = heads // UNIT_HEADS
    blocks = (tokens - ROOT_ROWS) // BLOCK
    child_keys = prompt_count + PER * RLEN
    shapes = [
        kept((ROOT_ROWS // BLOCK, units, prompt_count, UNIT), BF16),
        kept((blocks, units, child_keys, UNIT), BF16),
        kept((blocks, child_keys, HD), BF16),
    ]
    operands = [pinned(x) for x in (queries, out_grad, lse, delta, *shards)]
    if has_far:
        operands.append(pinned(far_prompt))
        shapes.append(kept((part_rows, HD), F32))
        shapes += [kept((part_rows, HD), BF16)] * (pool_shards - 1)
        shapes.append(kept((2 * prompt_rows, HD), BF16))
    else:
        shapes.append(jax.ShapeDtypeStruct((pool_rows, HD), F32))

    def body(*refs):
        attend_body(len(shards), part_rows, prompt_rows, has_far, *refs)

    return pl.pallas_call(
        body,
        in_specs=[SMEM] * 3 + [VMEM] * len(operands),
        out_specs=[VMEM] * len(shapes),
        out_shape=shapes,
        scratch_shapes=[
            pltpu.VMEM((pool_rows, HD), BF16),
            pltpu.VMEM((pool_rows, HD), F32),
            pltpu.VMEM((blocks, child_keys, HD), BF16),
        ],
        compiler_params=params(16 if has_far else 40),
        cost_estimate=cost(5),
        name="attend",
    )(*forks, *operands)


def far_body(owner_ref, root_ref, limit_ref, q_ref, out_ref, lse_ref, delta_ref, shard_ref, prompt_ref, send_ref, ds_ref):
    heads = lse_ref.shape[0]
    my_index = lax.axis_index("servers")
    key_index = lax.broadcasted_iota(jnp.int32, (ROOT_ROWS, UNIT), 0)
    in_child = (lax.broadcasted_iota(jnp.int32, (1, UNIT), 1) % BLOCK) // CLEN
    key_part = shard_ref[0:ROOT_ROWS]
    value_part = shard_ref[ROOT_ROWS : 2 * ROOT_ROWS]
    key_total = jnp.zeros((ROOT_ROWS, HD), F32)
    value_total = jnp.zeros((ROOT_ROWS, HD), F32)
    for block in range(ds_ref.shape[0]):
        start = ROOT_ROWS + block * BLOCK
        low = jnp.zeros((1, UNIT), jnp.int32)
        high = jnp.zeros((1, UNIT), jnp.int32)
        for k in range(PER):
            at = my_index * CH_DEV + block * PER + k
            base = root_ref[at] * RLEN
            limit = jnp.where((owner_ref[at] ^ my_index) == 3, limit_ref[at], 0)
            low = jnp.where(in_child == k, base, low)
            high = jnp.where(in_child == k, base + limit, high)
        allowed = (key_index >= low) & (key_index < high)
        for unit in range(heads // UNIT_HEADS):
            first = unit * UNIT_HEADS
            key_grad, value_grad, score_grads = pair_grads(
                key_part,
                value_part,
                stacked(q_ref, start, first),
                stacked(out_ref, start, first),
                row_of(lse_ref, start, first),
                row_of(delta_ref, start, first),
                lambda weights: jnp.where(allowed, weights, 0.0),
            )
            ds_ref[block, unit] = score_grads
            key_total = key_total + key_grad
            value_total = value_total + value_grad
    send_ref[0:ROOT_ROWS] = (key_total * SCALE).astype(BF16)
    send_ref[ROOT_ROWS : 2 * ROOT_ROWS] = value_total.astype(BF16)
    send_ref[2 * ROOT_ROWS :] = prompt_ref[...]


def far_call(forks, queries, out_grad, lse, delta, shard, prompt):
    tokens, width = queries.shape
    blocks = (tokens - ROOT_ROWS) // BLOCK
    units = width // HD // UNIT_HEADS
    return pl.pallas_call(
        far_body,
        in_specs=[SMEM] * 3 + [VMEM] * 6,
        out_specs=[VMEM] * 2,
        out_shape=[kept(shard.shape, BF16), kept((blocks, units, ROOT_ROWS, UNIT), BF16)],
        compiler_params=params(12),
        cost_estimate=cost(3),
        name="attend_far",
    )(*forks, *(pinned(x) for x in (queries, out_grad, lse, delta, shard, prompt)))


def own_body(has_far, *refs):
    (q_ref, out_ref, lse_ref, delta_ref, key_ref, value_ref, root_ds_ref, child_ds_ref, key_pool_ref) = refs[:9]
    refs = refs[9:]
    if has_far:
        (far_ds_ref, far_ref), refs = refs[:2], refs[2:]
    gq_ref, keys_out, values_out, gq_vmem, sems = refs
    heads = lse_ref.shape[0]
    tokens = q_ref.shape[0]
    prompt_count = root_ds_ref.shape[2]
    key_index = lax.broadcasted_iota(jnp.int32, (BLOCK, UNIT), 0)
    token_index = lax.broadcasted_iota(jnp.int32, (BLOCK, UNIT), 1) % BLOCK
    root_allowed = key_index <= token_index
    child_allowed = root_allowed & (key_index // CLEN == token_index // CLEN)
    copies = []
    for block in range(tokens // BLOCK):
        start = block * BLOCK
        rows = slice(start, start + BLOCK)
        in_root = start < ROOT_ROWS
        allowed = root_allowed if in_root else child_allowed
        child = block - ROOT_ROWS // BLOCK
        key_sum = jnp.zeros((BLOCK, HD), F32)
        value_sum = jnp.zeros((BLOCK, HD), F32)
        key_parts = [key_ref[rows], key_pool_ref[0, 0:prompt_count] if in_root else key_pool_ref[child]]
        if has_far and not in_root:
            key_parts.append(far_ref[0:ROOT_ROWS])
        key_all = jnp.concatenate(key_parts, axis=0)
        for unit in range(heads // UNIT_HEADS):
            first = unit * UNIT_HEADS
            key_grad, value_grad, score_grads = pair_grads(
                key_ref[rows],
                value_ref[rows],
                stacked(q_ref, start, first),
                stacked(out_ref, start, first),
                row_of(lse_ref, start, first),
                row_of(delta_ref, start, first),
                lambda weights: jnp.where(allowed, weights, 0.0),
            )
            key_sum = key_sum + key_grad
            value_sum = value_sum + value_grad
            parts = [score_grads, root_ds_ref[block, unit] if in_root else child_ds_ref[child, unit]]
            if has_far and not in_root:
                parts.append(far_ds_ref[child, unit])
            total = dot(jnp.concatenate(parts, axis=0), key_all, TN) * SCALE
            for index in range(UNIT_HEADS):
                head = first + index
                gq_vmem[rows, head * HD : (head + 1) * HD] = total[index * BLOCK : (index + 1) * BLOCK].astype(BF16)
        keys_out[rows] = key_sum * SCALE
        values_out[rows] = value_sum
        copy = pltpu.make_async_copy(gq_vmem.at[rows], gq_ref.at[rows], sems.at[block])
        copy.start()
        copies.append(copy)
    for copy in copies:
        copy.wait()


def own_call(queries, out_grad, lse, delta, keys, values, root_ds, child_ds, key_pool, far):
    tokens, width = queries.shape
    operands = [pinned(x) for x in (queries, out_grad, lse, delta, keys, values, root_ds, child_ds, key_pool, *far)]

    def body(*refs):
        own_body(bool(far), *refs)

    return pl.pallas_call(
        body,
        in_specs=[VMEM] * len(operands),
        out_specs=[ANY, VMEM, VMEM],
        out_shape=[
            jax.ShapeDtypeStruct((tokens, width), BF16),
            kept((tokens, HD), F32),
            kept((tokens, HD), F32),
        ],
        scratch_shapes=[pltpu.VMEM((tokens, width), BF16), pltpu.SemaphoreType.DMA((tokens // BLOCK,))],
        compiler_params=params(12 if far else 20),
        cost_estimate=cost(5),
        name="attend_own",
    )(*operands)


def finish_body(key_ref, value_ref, *refs):
    parts = refs[:-4]
    keys_out, values_out, prefix_keys_out, prefix_values_out = refs[-4:]
    own = prefix_keys_out.shape[0]
    total = parts[0][...].astype(F32)
    for part in parts[1:]:
        total = total + part[...].astype(F32)
    keys_out[0:ROOT_ROWS] = (key_ref[0:ROOT_ROWS] + total[0:ROOT_ROWS]).astype(BF16)
    keys_out[ROOT_ROWS:] = key_ref[ROOT_ROWS:].astype(BF16)
    values_out[0:ROOT_ROWS] = (value_ref[0:ROOT_ROWS] + total[ROOT_ROWS : 2 * ROOT_ROWS]).astype(BF16)
    values_out[ROOT_ROWS:] = value_ref[ROOT_ROWS:].astype(BF16)
    at = 2 * ROOT_ROWS
    prefix_keys_out[...] = total[at : at + own].astype(BF16)
    prefix_values_out[...] = total[at + own : at + 2 * own].astype(BF16)


def finish_call(key_sums, value_sums, parts):
    own = (parts[0].shape[0] - 2 * ROOT_ROWS) // 2
    shapes = [jax.ShapeDtypeStruct(key_sums.shape, BF16)] * 2 + [jax.ShapeDtypeStruct((own, HD), BF16)] * 2
    return pl.pallas_call(
        finish_body,
        in_specs=[VMEM] * (2 + len(parts)),
        out_specs=[VMEM] * 4,
        out_shape=shapes,
        compiler_params=params(8),
        cost_estimate=cost(1),
        name="finish",
    )(*(pinned(x) for x in (key_sums, value_sums, *parts)))


def local(
    grad_out,
    out_weight,
    queries,
    attn_out,
    lse,
    keys,
    values,
    prefix_keys,
    prefix_values,
    fork_owner,
    fork_root,
    fork_offset,
):
    prompt_rows = prefix_keys.shape[0]
    own_part, own_prompt = pack_call(keys, values, prefix_keys, prefix_values)
    forks = [pinned_scalars(x) for x in (fork_owner.reshape(-1), fork_root, fork_offset)]
    if lax.axis_size("servers") == 4:
        pairs = [[(i, i ^ d) for i in range(4)] for d in range(4)]
        part_two = lax.ppermute(own_part, "servers", pairs[2])
        part_one = lax.ppermute(own_part, "servers", pairs[1])
        prompt_far = lax.ppermute(own_prompt, "servers", pairs[3])
        out_grad, delta = out_grad_call(grad_out, out_weight, attn_out)
        part_two, delta = lax.optimization_barrier((part_two, delta))
        part_far = lax.ppermute(part_two, "servers", pairs[1])
        root_ds, child_ds, key_pool, own_sums, send_one, send_two, prompt_send = attend_call(
            forks, queries, out_grad, lse, delta, [own_part, part_one, part_two], prompt_far, prompt_rows
        )
        back_two = lax.ppermute(send_two, "servers", pairs[2])
        back_one = lax.ppermute(send_one, "servers", pairs[1])
        send_far, far_ds = far_call(forks, queries, out_grad, lse, delta, part_far, prompt_send)
        back_far = lax.ppermute(send_far, "servers", pairs[3])
        grad_queries, key_sums, value_sums = own_call(
            queries, out_grad, lse, delta, keys, values, root_ds, child_ds, key_pool, (far_ds, part_far)
        )
        parts = [own_sums, back_one, back_two, back_far]
    else:
        all_parts = lax.all_gather(own_part, "servers", axis=0, tiled=True)
        out_grad, delta = out_grad_call(grad_out, out_weight, attn_out)
        root_ds, child_ds, key_pool, sends = attend_call(
            forks, queries, out_grad, lse, delta, [all_parts], None, prompt_rows
        )
        grad_queries, key_sums, value_sums = own_call(
            queries, out_grad, lse, delta, keys, values, root_ds, child_ds, key_pool, ()
        )
        parts = [lax.psum_scatter(sends, "servers", scatter_dimension=0, tiled=True)]
    grads = finish_call(key_sums, value_sums, parts)
    return (grad_queries, *grads)


def solution(mesh):
    placed = (
        P(("groups", "servers"), None),
        P(None, "heads"),
        P(("groups", "servers"), "heads"),
        P(("groups", "servers"), "heads"),
        P("heads", ("groups", "servers")),
        P(("groups", "servers"), "heads"),
        P(("groups", "servers"), "heads"),
        P(("groups", "servers"), "heads"),
        P(("groups", "servers"), "heads"),
        P("groups", None),
        P("groups"),
        P("groups"),
    )
    return jax.shard_map(
        local,
        mesh=mesh,
        in_specs=placed,
        out_specs=(P(("groups", "servers"), "heads"),) * 5,
        check_vma=False,
    )
```

```python
import math

import jax
import jax.numpy as jnp
from jax import lax
from jax.experimental import pallas as pl
from jax.experimental.pallas import tpu as pltpu
from jax.sharding import PartitionSpec as P

HD = 128
CH_DEV = 16
ROOTS_DEV = 4
RLEN = 64
CLEN = 16
ROOT_ROWS = ROOTS_DEV * RLEN
BLOCK = 64
UNIT = 256
UNIT_HEADS = UNIT // BLOCK
PAIR = 2
SCALE = HD ** (-0.5)
LOG2E = math.log2(math.e)
NT = (((1,), (1,)), ((), ()))
NN = (((1,), (0,)), ((), ()))
TN = (((0,), (0,)), ((), ()))
F32 = jnp.float32
BF16 = jnp.bfloat16
VMEM = pl.BlockSpec(memory_space=pltpu.VMEM)
SMEM = pl.BlockSpec(memory_space=pltpu.SMEM)
ANY = pl.BlockSpec(memory_space=pl.ANY)


def params(mib):
    return pltpu.CompilerParams(vmem_limit_bytes=mib * 1024 * 1024)


COSTS = {
    "pack": 8,
    "repeat": 8,
    "out_grad": 6,
    "attend_near": 3,
    "attend_parent": 3,
    "attend_prompt": 0.1,
    "attend_far": 0.1,
    "attend_own": 0.1,
    "query_grads": 1,
    "finish": 0.1,
}


def cost(name):
    micros = COSTS[name]
    return pl.CostEstimate(flops=int(micros * (1 << 30)), transcendentals=0, bytes_accessed=1 << 16)


def pinned(array):
    return pltpu.with_memory_space_constraint(array, pltpu.VMEM)


def unmoved(array):
    return pltpu.with_memory_space_constraint(array, pltpu.HBM)


def pinned_scalars(array):
    return pltpu.with_memory_space_constraint(array, pltpu.SMEM)


def kept(shape, dtype):
    return pltpu.VMEM(shape, dtype)


def dot(left, right, numbers):
    return lax.dot_general(left, right, numbers, preferred_element_type=F32)


def pack_body(key_ref, value_ref, prefix_key_ref, prefix_value_ref, part_ref, sems):
    own = prefix_key_ref.shape[0]
    at = 2 * ROOT_ROWS
    copies = [
        (key_ref.at[0:ROOT_ROWS], part_ref.at[0:ROOT_ROWS]),
        (value_ref.at[0:ROOT_ROWS], part_ref.at[ROOT_ROWS:at]),
        (prefix_key_ref, part_ref.at[at : at + own]),
        (prefix_value_ref, part_ref.at[at + own : at + 2 * own]),
    ]
    started = [pltpu.make_async_copy(a, b, sems.at[i]) for i, (a, b) in enumerate(copies)]
    for copy in started:
        copy.start()
    for copy in started:
        copy.wait()


def pack_call(keys, values, prefix_keys, prefix_values):
    own = prefix_keys.shape[0]
    return pl.pallas_call(
        pack_body,
        in_specs=[ANY] * 4,
        out_specs=VMEM,
        out_shape=kept((2 * ROOT_ROWS + 2 * own, HD), BF16),
        scratch_shapes=[pltpu.SemaphoreType.DMA((4,))],
        compiler_params=params(4),
        cost_estimate=cost("pack"),
        name="pack",
    )(*(unmoved(x) for x in (keys, values, prefix_keys, prefix_values)))


def repeat_body(part_ref, part_out, prompt_out):
    part_out[...] = part_ref[...]
    prompt_out[...] = part_ref[2 * ROOT_ROWS :]


def repeat_call(part):
    return pl.pallas_call(
        repeat_body,
        in_specs=[VMEM],
        out_specs=[VMEM] * 2,
        out_shape=[kept(part.shape, BF16), kept((part.shape[0] - 2 * ROOT_ROWS, HD), BF16)],
        compiler_params=params(4),
        cost_estimate=cost("repeat"),
        name="repeat",
    )(pinned(part))


def unit_rows(array):
    heads, tokens = array.shape
    rows = []
    for start in range(0, ROOT_ROWS, BLOCK):
        for first in range(0, heads, UNIT_HEADS):
            picked = range(first, first + UNIT_HEADS)
            rows.append([array[head : head + 1, start : start + BLOCK] for head in picked])
    for start in range(ROOT_ROWS, tokens, PAIR * CLEN):
        starts = range(start, start + PAIR * CLEN, CLEN)
        rows.append([array[head : head + 1, at : at + CLEN] for at in starts for head in range(heads)])
    return [jnp.concatenate(row, axis=1) for row in rows]


def out_grad_body(
    grad_ref, weight_ref, attn_ref, lse_ref, owner_ref, root_ref, offset_ref, out_ref, lse_out, delta_out, forks_out
):
    rows, cols = out_ref.shape
    width = 2 * HD
    lane = lax.broadcasted_iota(jnp.int32, (rows, HD), 1)
    columns = jnp.zeros((rows, HD), F32)
    start = lax.axis_index("servers") * CH_DEV
    for child in range(CH_DEV):
        at = start + child
        forks_out[child] = (owner_ref[at] * ROOTS_DEV + root_ref[at]) * (2 * RLEN) + offset_ref[at]
    for unit, row in enumerate(unit_rows(lse_ref[...] * LOG2E)):
        lse_out[unit : unit + 1] = row
    for step in range(cols // width):
        part = slice(step * width, (step + 1) * width)
        wide = jnp.dot(grad_ref[...], weight_ref[:, part], preferred_element_type=F32).astype(BF16)
        out_ref[:, part] = wide
        products = wide.astype(F32) * attn_ref[:, part].astype(F32)
        for head in range(width // HD):
            total = jnp.sum(products[:, head * HD : (head + 1) * HD], axis=1, keepdims=True)
            columns = jnp.where(lane == step * (width // HD) + head, total, columns)
    for unit, row in enumerate(unit_rows(jnp.transpose(columns)[: cols // HD])):
        delta_out[unit : unit + 1] = row


def out_grad_call(grad_out, out_weight, attn_out, lse, *forks):
    rows = grad_out.shape[0]
    cols = out_weight.shape[1]
    units = rows * (cols // HD) // UNIT
    return pl.pallas_call(
        out_grad_body,
        in_specs=[VMEM] * 4 + [SMEM] * 3,
        out_specs=[VMEM] * 3 + [SMEM],
        out_shape=[
            kept((rows, cols), BF16),
            kept((units, UNIT), F32),
            kept((units, UNIT), F32),
            pltpu.SMEM((CH_DEV,), jnp.int32),
        ],
        compiler_params=params(12),
        cost_estimate=cost("out_grad"),
        name="out_grad",
    )(*(pinned(x) for x in (grad_out, out_weight, attn_out, lse)), *forks)


def unit_counts(tokens, heads):
    roots = ROOT_ROWS * heads // UNIT
    return roots, roots + (tokens - ROOT_ROWS) * heads // UNIT


def unit_tiles(tokens, heads, unit):
    roots, _ = unit_counts(tokens, heads)
    if unit < roots:
        block, part = divmod(unit, heads // UNIT_HEADS)
        picked = range(part * UNIT_HEADS, (part + 1) * UNIT_HEADS)
        return [(block * BLOCK, BLOCK, head) for head in picked]
    return [tile for k in range(PAIR) for tile in child_tiles(heads, (unit - roots) * PAIR + k)]


def child_tiles(heads, child):
    return [(ROOT_ROWS + child * CLEN, CLEN, head) for head in range(heads)]


def tiled(ref, tiles):
    return jnp.concatenate(
        [ref[start : start + rows, head * HD : (head + 1) * HD] for start, rows, head in tiles], axis=0
    )


def swept(jobs, load, parts, mask, keep, ahead=1):
    ready = []
    for job in [*jobs, *[None] * ahead]:
        if job is not None:
            query, out, lse, delta = load(job)
            keys, values = parts(job)
            ready.append((job, query, out, lse, delta, dot(keys, query, NT), dot(values, out, NT)))
        if job is not None and len(ready) <= ahead:
            continue
        done, query, out, lse, delta, scores, weight_grads = ready.pop(0)
        weights = mask(done, jnp.exp2(scores * (SCALE * LOG2E) - lse))
        score_grads = (weights * (weight_grads - delta)).astype(BF16)
        keep(done, dot(score_grads, query, NN), dot(weights.astype(BF16), out, NN), score_grads)


def unit_loader(q_ref, out_ref, lse_ref, delta_ref):
    tokens, heads = q_ref.shape[0], q_ref.shape[1] // HD

    def load(unit):
        tiles = unit_tiles(tokens, heads, unit)
        row = slice(unit, unit + 1)
        return tiled(q_ref, tiles), tiled(out_ref, tiles), lse_ref[row], delta_ref[row]

    return load


def child_loader(q_ref, out_ref, lse_ref, delta_ref):
    tokens, heads = q_ref.shape[0], q_ref.shape[1] // HD
    roots, _ = unit_counts(tokens, heads)

    def load(child):
        tiles = child_tiles(heads, child)
        unit, place = roots + child // PAIR, child % PAIR * heads * CLEN
        row, lanes = slice(unit, unit + 1), slice(place, place + heads * CLEN)
        return tiled(q_ref, tiles), tiled(out_ref, tiles), lse_ref[row, lanes], delta_ref[row, lanes]

    return load


def prompt_body(piece_rows, is_part, q_ref, out_ref, lse_ref, delta_ref, *refs):
    value_ref = refs[-1]
    if is_part:
        *pieces, ds_ref, key_ref, sums_ref, two_ref = refs[:-1]
    else:
        *pieces, ds_ref, key_ref, sums_ref = refs[:-1]
    own = piece_rows // 2
    count = 0
    for piece in pieces:
        first = 2 * ROOT_ROWS if is_part and piece.shape[0] > piece_rows else 0
        for at in range(first, piece.shape[0], piece_rows):
            key_ref[count : count + own] = piece[at : at + own]
            value_ref[count : count + own] = piece[at + own : at + piece_rows]
            count += own
    sums = [jnp.zeros((count, HD), F32), jnp.zeros((count, HD), F32)]

    def keep(unit, key_grad, value_grad, score_grads):
        ds_ref[unit] = score_grads
        sums[0] = sums[0] + key_grad
        sums[1] = sums[1] + value_grad

    swept(
        range(ds_ref.shape[0]),
        unit_loader(q_ref, out_ref, lse_ref, delta_ref),
        lambda unit: (key_ref[...], value_ref[...]),
        lambda unit, weights: weights,
        keep,
    )

    def store(ref, at, index):
        rows = slice(index * own, (index + 1) * own)
        ref[at : at + own] = (sums[0][rows] * SCALE).astype(ref.dtype)
        ref[at + own : at + piece_rows] = sums[1][rows].astype(ref.dtype)

    for index in range(count // own):
        store(sums_ref, index * piece_rows, index)
    if is_part:
        store(two_ref, 0, 2)


def prompt_call(shared, pieces, piece_rows, is_part):
    count = lax.axis_size("servers") * piece_rows // 2
    units = shared[2].shape[0]
    operands = [*shared, *pieces]
    shapes = [
        kept((units, count, UNIT), BF16),
        kept((count, HD), BF16),
        kept((2 * count, HD), F32),
    ]
    if is_part:
        shapes.append(kept((piece_rows, HD), BF16))

    def body(*refs):
        prompt_body(piece_rows, is_part, *refs)

    return pl.pallas_call(
        body,
        in_specs=[VMEM] * len(operands),
        out_specs=[VMEM] * len(shapes),
        out_shape=shapes,
        scratch_shapes=[pltpu.VMEM((count, HD), BF16)],
        compiler_params=params(12 if is_part else 20),
        cost_estimate=cost("attend_prompt"),
        name="attend_prompt",
    )(*(pinned(x) for x in operands))


def parent_body(held, has_prompt, fork_ref, q_ref, out_ref, lse_ref, delta_ref, *refs):
    is_part = held is not None
    count = len(held) if is_part else 1
    shards, refs = refs[:count], refs[count:]
    if has_prompt:
        prompt_ref, refs = refs[0], refs[1:]
    ds_ref, key_ref, *sum_refs = refs[:-2]
    grads_ref, sums_ref = refs[-2:]
    heads = q_ref.shape[1] // HD
    part = 2 * ROOT_ROWS
    my_index = lax.axis_index("servers")
    bases, limits = {}, {}

    def parts(child):
        fork = fork_ref[child]
        limit = fork & (2 * RLEN - 1)
        row = pl.multiple_of(((fork >> 7) & (ROOTS_DEV - 1)) * RLEN, RLEN)
        owner = fork >> 9
        if is_part:
            slot = owner ^ my_index
            is_last = slot == held[1]
            bases[child] = pl.multiple_of(jnp.where(is_last, part, 0) + row, RLEN)
            limits[child] = jnp.where(is_last | (slot == held[0]), limit, 0)
            at = row + ROOT_ROWS
            keys = jnp.where(is_last, shards[1][pl.ds(row, RLEN)], shards[0][pl.ds(row, RLEN)])
            values = jnp.where(is_last, shards[1][pl.ds(at, RLEN)], shards[0][pl.ds(at, RLEN)])
        else:
            bases[child] = pl.multiple_of(owner * part + row, RLEN)
            limits[child] = limit
            keys = shards[0][pl.ds(bases[child], RLEN)]
            values = shards[0][pl.ds(bases[child] + ROOT_ROWS, RLEN)]
        key_ref[child] = keys
        return keys, values

    key_index = lax.broadcasted_iota(jnp.int32, (RLEN, heads * CLEN), 0)

    def keep(child, key_grad, value_grad, score_grads):
        ds_ref[child] = score_grads
        grads_ref[child, 0:RLEN] = key_grad * SCALE
        grads_ref[child, RLEN:] = value_grad

    swept(
        range(CH_DEV),
        child_loader(q_ref, out_ref, lse_ref, delta_ref),
        parts,
        lambda child, weights: jnp.where(key_index < limits[child], weights, 0.0),
        keep,
        2,
    )
    sums_ref[...] = jnp.zeros(sums_ref.shape, F32)
    for child in range(CH_DEV):
        base = bases[child]
        sums_ref[pl.ds(base, RLEN)] = sums_ref[pl.ds(base, RLEN)] + grads_ref[child, 0:RLEN]
        base = base + ROOT_ROWS
        sums_ref[pl.ds(base, RLEN)] = sums_ref[pl.ds(base, RLEN)] + grads_ref[child, RLEN:]
    for index, ref in enumerate(sum_refs):
        first = index * part
        size = part if is_part else ref.shape[0]
        ref[0:size] = sums_ref[first : first + size].astype(ref.dtype)
        if is_part and ref.shape[0] > part:
            rows = ref.shape[0] - part
            first = held[index] * rows
            ref[part:] = prompt_ref[first : first + rows].astype(ref.dtype)


def parent_call(forks, shared, shards, held=None, sums=(), prompt_sums=None, name="attend_parent"):
    is_part = held is not None
    rows = 2 * ROOT_ROWS * len(shards) if is_part else shards[0].shape[0]
    columns = shared[0].shape[1] // HD * CLEN
    shapes = [kept((CH_DEV, RLEN, columns), BF16), kept((CH_DEV, RLEN, HD), BF16)]
    operands = [*shared, *shards]
    if is_part:
        shapes += sums
        if prompt_sums is not None:
            operands.append(prompt_sums)
    else:
        shapes.append(jax.ShapeDtypeStruct((rows, HD), F32))

    def body(*refs):
        parent_body(held, prompt_sums is not None, *refs)

    return pl.pallas_call(
        body,
        in_specs=[SMEM] + [VMEM] * len(operands),
        out_specs=[VMEM] * len(shapes),
        out_shape=shapes,
        scratch_shapes=[
            pltpu.VMEM((CH_DEV, 2 * RLEN, HD), F32),
            pltpu.VMEM((rows, HD), F32),
        ],
        compiler_params=params(8 if is_part else 40),
        cost_estimate=cost(name),
        name=name,
    )(pinned_scalars(forks), *(pinned(x) for x in operands))


def own_rows(tokens, heads, unit):
    roots, _ = unit_counts(tokens, heads)
    if unit < roots:
        start = unit // (heads // UNIT_HEADS) * BLOCK
        return slice(start, start + BLOCK)
    start = ROOT_ROWS + (unit - roots) * PAIR * CLEN
    return slice(start, start + PAIR * CLEN)


def own_body(q_ref, out_ref, lse_ref, delta_ref, key_ref, value_ref, root_ds_ref, child_ds_ref, keys_out, values_out):
    tokens, heads = q_ref.shape[0], q_ref.shape[1] // HD
    roots, units = unit_counts(tokens, heads)
    per_block = heads // UNIT_HEADS
    key_index = lax.broadcasted_iota(jnp.int32, (BLOCK, UNIT), 0)
    column = lax.broadcasted_iota(jnp.int32, (BLOCK, UNIT), 1)
    root_allowed = key_index <= column % BLOCK
    key_index, column = key_index[: PAIR * CLEN], column[: PAIR * CLEN]
    child_allowed = (key_index // CLEN == column // (heads * CLEN)) & (key_index % CLEN <= column % CLEN)
    totals = [None, None]

    def parts(unit):
        rows = own_rows(tokens, heads, unit)
        return key_ref[rows], value_ref[rows]

    def keep(unit, key_grad, value_grad, score_grads):
        rows = own_rows(tokens, heads, unit)
        if unit >= roots:
            child_ds_ref[unit - roots] = score_grads
            keys_out[rows] = key_grad * SCALE
            values_out[rows] = value_grad
            return
        root_ds_ref[unit] = score_grads
        totals[0] = key_grad if unit % per_block == 0 else totals[0] + key_grad
        totals[1] = value_grad if unit % per_block == 0 else totals[1] + value_grad
        if unit % per_block == per_block - 1:
            keys_out[rows] = totals[0] * SCALE
            values_out[rows] = totals[1]

    swept(
        range(units),
        unit_loader(q_ref, out_ref, lse_ref, delta_ref),
        parts,
        lambda unit, weights: jnp.where(root_allowed if unit < roots else child_allowed, weights, 0.0),
        keep,
    )


def own_call(shared, keys, values):
    tokens, width = shared[0].shape
    roots, units = unit_counts(tokens, width // HD)
    return pl.pallas_call(
        own_body,
        in_specs=[VMEM] * 6,
        out_specs=[VMEM] * 4,
        out_shape=[
            kept((roots, BLOCK, UNIT), BF16),
            kept((units - roots, PAIR * CLEN, UNIT), BF16),
            kept((tokens, HD), F32),
            kept((tokens, HD), F32),
        ],
        compiler_params=params(8),
        cost_estimate=cost("attend_own"),
        name="attend_own",
    )(*(pinned(x) for x in (*shared, keys, values)))


def query_body(has_back, key_ref, root_ds_ref, child_ds_ref, prompt_ref, prompt_ds_ref, *refs):
    if has_back:
        *parent_refs, sums_ref, back_ref, gq_ref, total_ref, gq_vmem, sems = refs
        total_ref[...] = sums_ref[...] + back_ref[...].astype(F32)
    else:
        *parent_refs, gq_ref, gq_vmem, sems = refs
    tokens, heads = gq_vmem.shape[0], gq_vmem.shape[1] // HD
    roots, units = unit_counts(tokens, heads)
    copies = []

    def store(tiles, total):
        at = 0
        for start, rows, head in tiles:
            piece = total[at : at + rows] * SCALE
            gq_vmem[start : start + rows, head * HD : (head + 1) * HD] = piece.astype(BF16)
            at += rows

    for unit in range(units):
        tiles = unit_tiles(tokens, heads, unit)
        own_ds = root_ds_ref[unit] if unit < roots else child_ds_ref[unit - roots]
        grads = jnp.concatenate([own_ds, prompt_ds_ref[unit]], axis=0)
        total = dot(grads, jnp.concatenate([key_ref[own_rows(tokens, heads, unit)], prompt_ref[...]], axis=0), TN)
        if unit < roots:
            store(tiles, total)
        else:
            columns = heads * CLEN
            for k in range(PAIR):
                child = (unit - roots) * PAIR + k
                grads = jnp.concatenate([ref[child] for ref in parent_refs[1::2]], axis=0)
                keys = jnp.concatenate([ref[child] for ref in parent_refs[0::2]], axis=0)
                store(child_tiles(heads, child), total[k * columns : (k + 1) * columns] + dot(grads, keys, TN))
        done = tiles[-1][0] + tiles[-1][1]
        first = len(copies) * BLOCK
        if done >= first + BLOCK and (unit + 1 >= roots or (unit + 1) % (heads // UNIT_HEADS) == 0):
            rows = slice(first, first + BLOCK)
            copy = pltpu.make_async_copy(gq_vmem.at[rows], gq_ref.at[rows], sems.at[len(copies)])
            copy.start()
            copies.append(copy)
    for copy in copies:
        copy.wait()


def query_call(tokens, width, operands, back=()):
    shapes = [jax.ShapeDtypeStruct((tokens, width), BF16), *(kept(x.shape, F32) for x in back[:1])]
    operands = [*operands, *back]

    def body(*refs):
        query_body(bool(back), *refs)

    return pl.pallas_call(
        body,
        in_specs=[VMEM] * len(operands),
        out_specs=[ANY, *[VMEM] * (len(shapes) - 1)],
        out_shape=shapes,
        scratch_shapes=[pltpu.VMEM((tokens, width), BF16), pltpu.SemaphoreType.DMA((tokens // BLOCK,))],
        compiler_params=params(12),
        cost_estimate=cost("query_grads"),
        name="query_grads",
    )(*(pinned(x) for x in operands))


def finish_body(key_ref, value_ref, *refs):
    parts = refs[:-4]
    keys_out, values_out, prefix_keys_out, prefix_values_out = refs[-4:]
    own = prefix_keys_out.shape[0]
    part = 2 * ROOT_ROWS
    total, prompt = [], []
    for ref in parts:
        rows = ref.shape[0]
        if rows >= part:
            total.append(ref[0:part].astype(F32))
        if rows != part:
            first = rows - 2 * own if rows > part else 0
            prompt.append(ref[first : first + 2 * own].astype(F32))
    total, prompt = sum(total[1:], total[0]), sum(prompt[1:], prompt[0])
    keys_out[0:ROOT_ROWS] = (key_ref[0:ROOT_ROWS] + total[0:ROOT_ROWS]).astype(BF16)
    keys_out[ROOT_ROWS:] = key_ref[ROOT_ROWS:].astype(BF16)
    values_out[0:ROOT_ROWS] = (value_ref[0:ROOT_ROWS] + total[ROOT_ROWS:]).astype(BF16)
    values_out[ROOT_ROWS:] = value_ref[ROOT_ROWS:].astype(BF16)
    prefix_keys_out[...] = prompt[0:own].astype(BF16)
    prefix_values_out[...] = prompt[own:].astype(BF16)


def finish_call(key_sums, value_sums, parts, own):
    shapes = [jax.ShapeDtypeStruct(key_sums.shape, BF16)] * 2 + [jax.ShapeDtypeStruct((own, HD), BF16)] * 2
    return pl.pallas_call(
        finish_body,
        in_specs=[VMEM] * (2 + len(parts)),
        out_specs=[VMEM] * 4,
        out_shape=shapes,
        compiler_params=params(8),
        cost_estimate=cost("finish"),
        name="finish",
    )(*(pinned(x) for x in (key_sums, value_sums, *parts)))


def local(
    grad_out,
    out_weight,
    queries,
    attn_out,
    lse,
    keys,
    values,
    prefix_keys,
    prefix_values,
    fork_owner,
    fork_root,
    fork_offset,
):
    own_part = pack_call(keys, values, prefix_keys, prefix_values)
    forks = [fork_owner.reshape(-1), fork_root, fork_offset]
    own = prefix_keys.shape[0]
    if lax.axis_size("servers") == 4:
        pairs = [[(i, i ^ d) for i in range(4)] for d in range(4)]
        part_two = lax.ppermute(own_part, "servers", pairs[2])
        later_part, later_prompt = repeat_call(own_part)
        prompt_far = lax.ppermute(later_prompt, "servers", pairs[3])
        part_one = lax.ppermute(later_part, "servers", pairs[1])
        out_grad, lse_rows, delta, forks = out_grad_call(grad_out, out_weight, attn_out, lse, *forks)
        part_two, delta = lax.optimization_barrier((part_two, delta))
        part_far = lax.ppermute(part_two, "servers", pairs[1])
        delta, prompt_far = lax.optimization_barrier((delta, prompt_far))
        part, whole = (2 * ROOT_ROWS, HD), (2 * ROOT_ROWS + 2 * own, HD)
        near_ds, near_keys, own_sums, send_two = parent_call(
            forks,
            (queries, out_grad, lse_rows, delta),
            [own_part, part_two],
            (0, 2),
            [kept(part, F32), kept(part, BF16)],
            None,
            "attend_near",
        )
        back_two = lax.ppermute(send_two, "servers", pairs[2])
        delta, own_sums = lax.optimization_barrier((delta, own_sums))
        prompt_ds, prompt_keys, prompt_sums, send_two_prompt = prompt_call(
            (queries, out_grad, lse_rows, delta), [own_part, part_one, part_two, prompt_far], 2 * own, True
        )
        far_ds, far_keys, send_far, send_one = parent_call(
            forks,
            (queries, out_grad, lse_rows, delta),
            [part_far, part_one],
            (3, 1),
            [kept(whole, BF16), kept(whole, BF16)],
            prompt_sums,
            "attend_far",
        )
        back_far = lax.ppermute(send_far, "servers", pairs[3])
        back_one = lax.ppermute(send_one, "servers", pairs[1])
        back_two_prompt = lax.ppermute(send_two_prompt, "servers", pairs[2])
        delta, far_ds = lax.optimization_barrier((delta, far_ds))
        shared = (queries, out_grad, lse_rows, delta)
        parents = (near_keys, near_ds, far_keys, far_ds)
        back = (own_sums, back_two)
        parts = [prompt_sums, back_far, back_one, back_two_prompt]
    else:
        count = lax.axis_size("servers")
        all_parts = lax.all_gather(own_part, "servers", axis=0, tiled=False)
        part = 2 * ROOT_ROWS
        all_roots = all_parts[:, :part].reshape(-1, HD)
        all_prompts = all_parts[:, part:].reshape(-1, HD)
        out_grad, lse_rows, delta, forks = out_grad_call(grad_out, out_weight, attn_out, lse, *forks)
        shared = (queries, out_grad, lse_rows, delta)
        prompt_ds, prompt_keys, prompt_sums = prompt_call(shared, [all_prompts], 2 * own, False)
        parent_ds, parent_keys, root_sums = parent_call(forks, shared, [all_roots])
        parents = (parent_keys, parent_ds)
        sends = jnp.concatenate(
            [root_sums.reshape(count, part, HD), prompt_sums.reshape(count, 2 * own, HD)], axis=1
        ).reshape(-1, HD)
        back = ()
        parts = [lax.psum_scatter(sends, "servers", scatter_dimension=0, tiled=True)]
    root_ds, child_ds, key_sums, value_sums = own_call(shared, keys, values)
    operands = (keys, root_ds, child_ds, prompt_keys, prompt_ds, *parents)
    grad_queries, *totals = query_call(*queries.shape, operands, back)
    parts = totals + parts
    grads = finish_call(key_sums, value_sums, parts, own)
    return (grad_queries, *grads)


def solution(mesh):
    placed = (
        P(("groups", "servers"), None),
        P(None, "heads"),
        P(("groups", "servers"), "heads"),
        P(("groups", "servers"), "heads"),
        P("heads", ("groups", "servers")),
        P(("groups", "servers"), "heads"),
        P(("groups", "servers"), "heads"),
        P(("groups", "servers"), "heads"),
        P(("groups", "servers"), "heads"),
        P("groups", None),
        P("groups"),
        P("groups"),
    )
    return jax.shard_map(
        local,
        mesh=mesh,
        in_specs=placed,
        out_specs=(P(("groups", "servers"), "heads"),) * 5,
        check_vma=False,
    )
```

```python
import math

import jax
import jax.numpy as jnp
from jax import lax
from jax.experimental import pallas as pl
from jax.experimental.pallas import tpu as pltpu
from jax.sharding import PartitionSpec as P

HD = 128
CH_DEV = 16
ROOTS_DEV = 4
RLEN = 64
CLEN = 16
ROOT_ROWS = ROOTS_DEV * RLEN
BLOCK = 64
UNIT = 256
UNIT_HEADS = UNIT // BLOCK
PAIR = 2
SCALE = HD ** (-0.5)
LOG2E = math.log2(math.e)
NT = (((1,), (1,)), ((), ()))
NN = (((1,), (0,)), ((), ()))
TN = (((0,), (0,)), ((), ()))
F32 = jnp.float32
BF16 = jnp.bfloat16
VMEM = pl.BlockSpec(memory_space=pltpu.VMEM)
SMEM = pl.BlockSpec(memory_space=pltpu.SMEM)
ANY = pl.BlockSpec(memory_space=pl.ANY)


def params(mib):
    return pltpu.CompilerParams(vmem_limit_bytes=mib * 1024 * 1024)


COSTS = {
    "pack": 8,
    "repeat": 8,
    "out_grad": 6,
    "attend_near": 3,
    "attend_parent": 3,
    "attend_prompt": 0.1,
    "attend_far": 0.1,
    "attend_own": 0.1,
    "query_grads": 0.3,
    "finish": 0.01,
}


def cost(name):
    micros = COSTS[name]
    return pl.CostEstimate(flops=int(micros * (1 << 30)), transcendentals=0, bytes_accessed=1 << 16)


def pinned(array):
    return pltpu.with_memory_space_constraint(array, pltpu.VMEM)


def unmoved(array):
    return pltpu.with_memory_space_constraint(array, pltpu.HBM)


def pinned_scalars(array):
    return pltpu.with_memory_space_constraint(array, pltpu.SMEM)


def kept(shape, dtype):
    return pltpu.VMEM(shape, dtype)


def dot(left, right, numbers):
    return lax.dot_general(left, right, numbers, preferred_element_type=F32)


def pack_body(key_ref, value_ref, prefix_key_ref, prefix_value_ref, part_ref, sems):
    own = prefix_key_ref.shape[0]
    at = 2 * ROOT_ROWS
    copies = [
        (key_ref.at[0:ROOT_ROWS], part_ref.at[0:ROOT_ROWS]),
        (value_ref.at[0:ROOT_ROWS], part_ref.at[ROOT_ROWS:at]),
        (prefix_key_ref, part_ref.at[at : at + own]),
        (prefix_value_ref, part_ref.at[at + own : at + 2 * own]),
    ]
    started = [pltpu.make_async_copy(a, b, sems.at[i]) for i, (a, b) in enumerate(copies)]
    for copy in started:
        copy.start()
    for copy in started:
        copy.wait()


def pack_call(keys, values, prefix_keys, prefix_values):
    own = prefix_keys.shape[0]
    return pl.pallas_call(
        pack_body,
        in_specs=[ANY] * 4,
        out_specs=VMEM,
        out_shape=kept((2 * ROOT_ROWS + 2 * own, HD), BF16),
        scratch_shapes=[pltpu.SemaphoreType.DMA((4,))],
        compiler_params=params(4),
        cost_estimate=cost("pack"),
        name="pack",
    )(*(unmoved(x) for x in (keys, values, prefix_keys, prefix_values)))


def repeat_body(part_ref, part_out, prompt_out):
    part_out[...] = part_ref[...]
    prompt_out[...] = part_ref[2 * ROOT_ROWS :]


def repeat_call(part):
    return pl.pallas_call(
        repeat_body,
        in_specs=[VMEM],
        out_specs=[VMEM] * 2,
        out_shape=[kept(part.shape, BF16), kept((part.shape[0] - 2 * ROOT_ROWS, HD), BF16)],
        compiler_params=params(4),
        cost_estimate=cost("repeat"),
        name="repeat",
    )(pinned(part))


def unit_rows(array):
    heads, tokens = array.shape
    rows = []
    for start in range(0, ROOT_ROWS, BLOCK):
        for first in range(0, heads, UNIT_HEADS):
            picked = range(first, first + UNIT_HEADS)
            rows.append([array[head : head + 1, start : start + BLOCK] for head in picked])
    for start in range(ROOT_ROWS, tokens, PAIR * CLEN):
        starts = range(start, start + PAIR * CLEN, CLEN)
        rows.append([array[head : head + 1, at : at + CLEN] for at in starts for head in range(heads)])
    return [jnp.concatenate(row, axis=1) for row in rows]


def out_grad_body(
    grad_ref, weight_ref, attn_ref, lse_ref, owner_ref, root_ref, offset_ref, out_ref, lse_out, delta_out, forks_out
):
    rows, cols = out_ref.shape
    width = 2 * HD
    lane = lax.broadcasted_iota(jnp.int32, (rows, HD), 1)
    columns = jnp.zeros((rows, HD), F32)
    start = lax.axis_index("servers") * CH_DEV
    for child in range(CH_DEV):
        at = start + child
        forks_out[child] = (owner_ref[at] * ROOTS_DEV + root_ref[at]) * (2 * RLEN) + offset_ref[at]
    for unit, row in enumerate(unit_rows(lse_ref[...] * LOG2E)):
        lse_out[unit : unit + 1] = row
    for step in range(cols // width):
        part = slice(step * width, (step + 1) * width)
        wide = jnp.dot(grad_ref[...], weight_ref[:, part], preferred_element_type=F32).astype(BF16)
        out_ref[:, part] = wide
        products = wide.astype(F32) * attn_ref[:, part].astype(F32)
        for head in range(width // HD):
            total = jnp.sum(products[:, head * HD : (head + 1) * HD], axis=1, keepdims=True)
            columns = jnp.where(lane == step * (width // HD) + head, total, columns)
    for unit, row in enumerate(unit_rows(jnp.transpose(columns)[: cols // HD])):
        delta_out[unit : unit + 1] = row


def out_grad_call(grad_out, out_weight, attn_out, lse, *forks):
    rows = grad_out.shape[0]
    cols = out_weight.shape[1]
    units = rows * (cols // HD) // UNIT
    return pl.pallas_call(
        out_grad_body,
        in_specs=[VMEM] * 4 + [SMEM] * 3,
        out_specs=[VMEM] * 3 + [SMEM],
        out_shape=[
            kept((rows, cols), BF16),
            kept((units, UNIT), F32),
            kept((units, UNIT), F32),
            pltpu.SMEM((CH_DEV,), jnp.int32),
        ],
        compiler_params=params(12),
        cost_estimate=cost("out_grad"),
        name="out_grad",
    )(*(pinned(x) for x in (grad_out, out_weight, attn_out, lse)), *forks)


def unit_counts(tokens, heads):
    roots = ROOT_ROWS * heads // UNIT
    return roots, roots + (tokens - ROOT_ROWS) * heads // UNIT


def unit_tiles(tokens, heads, unit):
    roots, _ = unit_counts(tokens, heads)
    if unit < roots:
        block, part = divmod(unit, heads // UNIT_HEADS)
        picked = range(part * UNIT_HEADS, (part + 1) * UNIT_HEADS)
        return [(block * BLOCK, BLOCK, head) for head in picked]
    return [tile for k in range(PAIR) for tile in child_tiles(heads, (unit - roots) * PAIR + k)]


def child_tiles(heads, child):
    return [(ROOT_ROWS + child * CLEN, CLEN, head) for head in range(heads)]


def tiled(ref, tiles):
    return jnp.concatenate(
        [ref[start : start + rows, head * HD : (head + 1) * HD] for start, rows, head in tiles], axis=0
    )


def swept(jobs, load, parts, mask, keep, ahead=1):
    ready = []
    for job in [*jobs, *[None] * ahead]:
        if job is not None:
            query, out, lse, delta = load(job)
            keys, values = parts(job)
            ready.append((job, query, out, lse, delta, dot(keys, query, NT), dot(values, out, NT)))
        if job is not None and len(ready) <= ahead:
            continue
        done, query, out, lse, delta, scores, weight_grads = ready.pop(0)
        weights = mask(done, jnp.exp2(scores * (SCALE * LOG2E) - lse))
        score_grads = (weights * (weight_grads - delta)).astype(BF16)
        keep(done, dot(score_grads, query, NN), dot(weights.astype(BF16), out, NN), score_grads)


def unit_loader(q_ref, out_ref, lse_ref, delta_ref):
    tokens, heads = q_ref.shape[0], q_ref.shape[1] // HD

    def load(unit):
        tiles = unit_tiles(tokens, heads, unit)
        row = slice(unit, unit + 1)
        return tiled(q_ref, tiles), tiled(out_ref, tiles), lse_ref[row], delta_ref[row]

    return load


def child_loader(q_ref, out_ref, lse_ref, delta_ref):
    tokens, heads = q_ref.shape[0], q_ref.shape[1] // HD
    roots, _ = unit_counts(tokens, heads)

    def load(child):
        tiles = child_tiles(heads, child)
        unit, place = roots + child // PAIR, child % PAIR * heads * CLEN
        row, lanes = slice(unit, unit + 1), slice(place, place + heads * CLEN)
        return tiled(q_ref, tiles), tiled(out_ref, tiles), lse_ref[row, lanes], delta_ref[row, lanes]

    return load


def prompt_body(piece_rows, is_part, q_ref, out_ref, lse_ref, delta_ref, *refs):
    value_ref = refs[-1]
    if is_part:
        *pieces, ds_ref, key_ref, sums_ref, two_ref = refs[:-1]
    else:
        *pieces, ds_ref, key_ref, sums_ref = refs[:-1]
    own = piece_rows // 2
    count = 0
    for piece in pieces:
        first = 2 * ROOT_ROWS if is_part and piece.shape[0] > piece_rows else 0
        for at in range(first, piece.shape[0], piece_rows):
            key_ref[count : count + own] = piece[at : at + own]
            value_ref[count : count + own] = piece[at + own : at + piece_rows]
            count += own
    sums = [jnp.zeros((count, HD), F32), jnp.zeros((count, HD), F32)]

    def keep(unit, key_grad, value_grad, score_grads):
        ds_ref[unit] = score_grads
        sums[0] = sums[0] + key_grad
        sums[1] = sums[1] + value_grad

    swept(
        range(ds_ref.shape[0]),
        unit_loader(q_ref, out_ref, lse_ref, delta_ref),
        lambda unit: (key_ref[...], value_ref[...]),
        lambda unit, weights: weights,
        keep,
    )

    def store(ref, at, index):
        rows = slice(index * own, (index + 1) * own)
        ref[at : at + own] = (sums[0][rows] * SCALE).astype(ref.dtype)
        ref[at + own : at + piece_rows] = sums[1][rows].astype(ref.dtype)

    for index in range(count // own):
        store(sums_ref, index * piece_rows, index)
    if is_part:
        store(two_ref, 0, 3)


def prompt_call(shared, pieces, piece_rows, is_part):
    count = lax.axis_size("servers") * piece_rows // 2
    units = shared[2].shape[0]
    operands = [*shared, *pieces]
    shapes = [
        kept((units, count, UNIT), BF16),
        kept((count, HD), BF16),
        kept((2 * count, HD), F32),
    ]
    if is_part:
        shapes.append(kept((piece_rows, HD), BF16))

    def body(*refs):
        prompt_body(piece_rows, is_part, *refs)

    return pl.pallas_call(
        body,
        in_specs=[VMEM] * len(operands),
        out_specs=[VMEM] * len(shapes),
        out_shape=shapes,
        scratch_shapes=[pltpu.VMEM((count, HD), BF16)],
        compiler_params=params(12 if is_part else 20),
        cost_estimate=cost("attend_prompt"),
        name="attend_prompt",
    )(*(pinned(x) for x in operands))


def parent_body(held, has_prompt, fork_ref, q_ref, out_ref, lse_ref, delta_ref, *refs):
    is_part = held is not None
    count = len(held) if is_part else 1
    shards, refs = refs[:count], refs[count:]
    if has_prompt:
        prompt_ref, refs = refs[0], refs[1:]
    ds_ref, key_ref, *sum_refs = refs[:-2]
    grads_ref, sums_ref = refs[-2:]
    heads = q_ref.shape[1] // HD
    part = 2 * ROOT_ROWS
    my_index = lax.axis_index("servers")
    bases, limits = {}, {}

    def parts(child):
        fork = fork_ref[child]
        limit = fork & (2 * RLEN - 1)
        row = pl.multiple_of(((fork >> 7) & (ROOTS_DEV - 1)) * RLEN, RLEN)
        owner = fork >> 9
        if is_part:
            slot = owner ^ my_index
            is_last = slot == held[1]
            bases[child] = pl.multiple_of(jnp.where(is_last, part, 0) + row, RLEN)
            limits[child] = jnp.where(is_last | (slot == held[0]), limit, 0)
            at = row + ROOT_ROWS
            keys = jnp.where(is_last, shards[1][pl.ds(row, RLEN)], shards[0][pl.ds(row, RLEN)])
            values = jnp.where(is_last, shards[1][pl.ds(at, RLEN)], shards[0][pl.ds(at, RLEN)])
        else:
            bases[child] = pl.multiple_of(owner * part + row, RLEN)
            limits[child] = limit
            keys = shards[0][pl.ds(bases[child], RLEN)]
            values = shards[0][pl.ds(bases[child] + ROOT_ROWS, RLEN)]
        key_ref[child] = keys
        return keys, values

    key_index = lax.broadcasted_iota(jnp.int32, (RLEN, heads * CLEN), 0)

    def keep(child, key_grad, value_grad, score_grads):
        ds_ref[child] = score_grads
        grads_ref[child, 0:RLEN] = key_grad * SCALE
        grads_ref[child, RLEN:] = value_grad

    swept(
        range(CH_DEV),
        child_loader(q_ref, out_ref, lse_ref, delta_ref),
        parts,
        lambda child, weights: jnp.where(key_index < limits[child], weights, 0.0),
        keep,
        2,
    )
    sums_ref[...] = jnp.zeros(sums_ref.shape, F32)
    for child in range(CH_DEV):
        base = bases[child]
        sums_ref[pl.ds(base, RLEN)] = sums_ref[pl.ds(base, RLEN)] + grads_ref[child, 0:RLEN]
        base = base + ROOT_ROWS
        sums_ref[pl.ds(base, RLEN)] = sums_ref[pl.ds(base, RLEN)] + grads_ref[child, RLEN:]
    for index, ref in enumerate(sum_refs):
        first = index * part
        size = part if is_part else ref.shape[0]
        ref[0:size] = sums_ref[first : first + size].astype(ref.dtype)
        if is_part and ref.shape[0] > part:
            rows = ref.shape[0] - part
            first = held[index] * rows
            ref[part:] = prompt_ref[first : first + rows].astype(ref.dtype)


def parent_call(forks, shared, shards, held=None, sums=(), prompt_sums=None, name="attend_parent"):
    is_part = held is not None
    rows = 2 * ROOT_ROWS * len(shards) if is_part else shards[0].shape[0]
    columns = shared[0].shape[1] // HD * CLEN
    shapes = [kept((CH_DEV, RLEN, columns), BF16), kept((CH_DEV, RLEN, HD), BF16)]
    operands = [*shared, *shards]
    if is_part:
        shapes += sums
        if prompt_sums is not None:
            operands.append(prompt_sums)
    else:
        shapes.append(jax.ShapeDtypeStruct((rows, HD), F32))

    def body(*refs):
        parent_body(held, prompt_sums is not None, *refs)

    return pl.pallas_call(
        body,
        in_specs=[SMEM] + [VMEM] * len(operands),
        out_specs=[VMEM] * len(shapes),
        out_shape=shapes,
        scratch_shapes=[
            pltpu.VMEM((CH_DEV, 2 * RLEN, HD), F32),
            pltpu.VMEM((rows, HD), F32),
        ],
        compiler_params=params(8 if is_part else 40),
        cost_estimate=cost(name),
        name=name,
    )(pinned_scalars(forks), *(pinned(x) for x in operands))


def own_rows(tokens, heads, unit):
    roots, _ = unit_counts(tokens, heads)
    if unit < roots:
        start = unit // (heads // UNIT_HEADS) * BLOCK
        return slice(start, start + BLOCK)
    start = ROOT_ROWS + (unit - roots) * PAIR * CLEN
    return slice(start, start + PAIR * CLEN)


def own_body(q_ref, out_ref, lse_ref, delta_ref, key_ref, value_ref, root_ds_ref, child_ds_ref, keys_out, values_out):
    tokens, heads = q_ref.shape[0], q_ref.shape[1] // HD
    roots, units = unit_counts(tokens, heads)
    per_block = heads // UNIT_HEADS
    key_index = lax.broadcasted_iota(jnp.int32, (BLOCK, UNIT), 0)
    column = lax.broadcasted_iota(jnp.int32, (BLOCK, UNIT), 1)
    root_allowed = key_index <= column % BLOCK
    key_index, column = key_index[: PAIR * CLEN], column[: PAIR * CLEN]
    child_allowed = (key_index // CLEN == column // (heads * CLEN)) & (key_index % CLEN <= column % CLEN)
    totals = [None, None]

    def parts(unit):
        rows = own_rows(tokens, heads, unit)
        return key_ref[rows], value_ref[rows]

    def keep(unit, key_grad, value_grad, score_grads):
        rows = own_rows(tokens, heads, unit)
        if unit >= roots:
            child_ds_ref[unit - roots] = score_grads
            keys_out[rows] = key_grad * SCALE
            values_out[rows] = value_grad
            return
        root_ds_ref[unit] = score_grads
        totals[0] = key_grad if unit % per_block == 0 else totals[0] + key_grad
        totals[1] = value_grad if unit % per_block == 0 else totals[1] + value_grad
        if unit % per_block == per_block - 1:
            keys_out[rows] = totals[0] * SCALE
            values_out[rows] = totals[1]

    swept(
        range(units),
        unit_loader(q_ref, out_ref, lse_ref, delta_ref),
        parts,
        lambda unit, weights: jnp.where(root_allowed if unit < roots else child_allowed, weights, 0.0),
        keep,
    )


def own_call(shared, keys, values):
    tokens, width = shared[0].shape
    roots, units = unit_counts(tokens, width // HD)
    return pl.pallas_call(
        own_body,
        in_specs=[VMEM] * 6,
        out_specs=[VMEM] * 4,
        out_shape=[
            kept((roots, BLOCK, UNIT), BF16),
            kept((units - roots, PAIR * CLEN, UNIT), BF16),
            kept((tokens, HD), F32),
            kept((tokens, HD), F32),
        ],
        compiler_params=params(8),
        cost_estimate=cost("attend_own"),
        name="attend_own",
    )(*(pinned(x) for x in (*shared, keys, values)))


def query_body(has_back, key_ref, root_ds_ref, child_ds_ref, prompt_ref, prompt_ds_ref, *refs):
    if has_back:
        *parent_refs, sums_ref, back_ref, gq_ref, total_ref, gq_vmem, sems = refs
        total_ref[...] = sums_ref[...] + back_ref[...].astype(F32)
    else:
        *parent_refs, gq_ref, gq_vmem, sems = refs
    tokens, heads = gq_vmem.shape[0], gq_vmem.shape[1] // HD
    roots, units = unit_counts(tokens, heads)
    copies = []

    def store(tiles, total):
        at = 0
        for start, rows, head in tiles:
            piece = total[at : at + rows] * SCALE
            gq_vmem[start : start + rows, head * HD : (head + 1) * HD] = piece.astype(BF16)
            at += rows

    for unit in range(units):
        tiles = unit_tiles(tokens, heads, unit)
        own_ds = root_ds_ref[unit] if unit < roots else child_ds_ref[unit - roots]
        grads = jnp.concatenate([own_ds, prompt_ds_ref[unit]], axis=0)
        total = dot(grads, jnp.concatenate([key_ref[own_rows(tokens, heads, unit)], prompt_ref[...]], axis=0), TN)
        if unit < roots:
            store(tiles, total)
        else:
            columns = heads * CLEN
            for k in range(PAIR):
                child = (unit - roots) * PAIR + k
                grads = jnp.concatenate([ref[child] for ref in parent_refs[1::2]], axis=0)
                keys = jnp.concatenate([ref[child] for ref in parent_refs[0::2]], axis=0)
                store(child_tiles(heads, child), total[k * columns : (k + 1) * columns] + dot(grads, keys, TN))
        done = tiles[-1][0] + tiles[-1][1]
        first = len(copies) * BLOCK
        if done >= first + BLOCK and (unit + 1 >= roots or (unit + 1) % (heads // UNIT_HEADS) == 0):
            rows = slice(first, first + BLOCK)
            copy = pltpu.make_async_copy(gq_vmem.at[rows], gq_ref.at[rows], sems.at[len(copies)])
            copy.start()
            copies.append(copy)
    for copy in copies:
        copy.wait()


def query_call(tokens, width, operands, back=()):
    shapes = [jax.ShapeDtypeStruct((tokens, width), BF16), *(kept(x.shape, F32) for x in back[:1])]
    operands = [*operands, *back]

    def body(*refs):
        query_body(bool(back), *refs)

    return pl.pallas_call(
        body,
        in_specs=[VMEM] * len(operands),
        out_specs=[ANY, *[VMEM] * (len(shapes) - 1)],
        out_shape=shapes,
        scratch_shapes=[pltpu.VMEM((tokens, width), BF16), pltpu.SemaphoreType.DMA((tokens // BLOCK,))],
        compiler_params=params(12),
        cost_estimate=cost("query_grads"),
        name="query_grads",
    )(*(pinned(x) for x in operands))


def finish_body(key_ref, value_ref, *refs):
    parts = refs[:-4]
    keys_out, values_out, prefix_keys_out, prefix_values_out = refs[-4:]
    own = prefix_keys_out.shape[0]
    part = 2 * ROOT_ROWS
    total, prompt = [], []
    for ref in parts:
        rows = ref.shape[0]
        if rows >= part:
            total.append(ref[0:part].astype(F32))
        if rows != part:
            first = rows - 2 * own if rows > part else 0
            prompt.append(ref[first : first + 2 * own].astype(F32))
    total, prompt = sum(total[1:], total[0]), sum(prompt[1:], prompt[0])
    keys_out[0:ROOT_ROWS] = (key_ref[0:ROOT_ROWS] + total[0:ROOT_ROWS]).astype(BF16)
    keys_out[ROOT_ROWS:] = key_ref[ROOT_ROWS:].astype(BF16)
    values_out[0:ROOT_ROWS] = (value_ref[0:ROOT_ROWS] + total[ROOT_ROWS:]).astype(BF16)
    values_out[ROOT_ROWS:] = value_ref[ROOT_ROWS:].astype(BF16)
    prefix_keys_out[...] = prompt[0:own].astype(BF16)
    prefix_values_out[...] = prompt[own:].astype(BF16)


def finish_call(key_sums, value_sums, parts, own):
    shapes = [jax.ShapeDtypeStruct(key_sums.shape, BF16)] * 2 + [jax.ShapeDtypeStruct((own, HD), BF16)] * 2
    return pl.pallas_call(
        finish_body,
        in_specs=[VMEM] * (2 + len(parts)),
        out_specs=[VMEM] * 4,
        out_shape=shapes,
        compiler_params=params(8),
        cost_estimate=cost("finish"),
        name="finish",
    )(*(pinned(x) for x in (key_sums, value_sums, *parts)))


def local(
    grad_out,
    out_weight,
    queries,
    attn_out,
    lse,
    keys,
    values,
    prefix_keys,
    prefix_values,
    fork_owner,
    fork_root,
    fork_offset,
):
    own_part = pack_call(keys, values, prefix_keys, prefix_values)
    forks = [fork_owner.reshape(-1), fork_root, fork_offset]
    own = prefix_keys.shape[0]
    if lax.axis_size("servers") == 4:
        pairs = [[(i, i ^ d) for i in range(4)] for d in range(4)]
        part_two = lax.ppermute(own_part, "servers", pairs[3])
        later_part, later_prompt = repeat_call(own_part)
        prompt_far = lax.ppermute(later_prompt, "servers", pairs[2])
        part_one = lax.ppermute(later_part, "servers", pairs[1])
        out_grad, lse_rows, delta, forks = out_grad_call(grad_out, out_weight, attn_out, lse, *forks)
        part_two, delta = lax.optimization_barrier((part_two, delta))
        part_far = lax.ppermute(part_two, "servers", pairs[1])
        part, whole = (2 * ROOT_ROWS, HD), (2 * ROOT_ROWS + 2 * own, HD)
        near_ds, near_keys, own_sums, send_two = parent_call(
            forks,
            (queries, out_grad, lse_rows, delta),
            [own_part, part_two],
            (0, 3),
            [kept(part, F32), kept(part, BF16)],
            None,
            "attend_near",
        )
        back_two = lax.ppermute(send_two, "servers", pairs[3])
        delta, own_sums = lax.optimization_barrier((delta, own_sums))
        prompt_ds, prompt_keys, prompt_sums, send_two_prompt = prompt_call(
            (queries, out_grad, lse_rows, delta), [own_part, part_one, prompt_far, part_two], 2 * own, True
        )
        far_ds, far_keys, send_far, send_one = parent_call(
            forks,
            (queries, out_grad, lse_rows, delta),
            [part_far, part_one],
            (2, 1),
            [kept(whole, BF16), kept(whole, BF16)],
            prompt_sums,
            "attend_far",
        )
        back_far = lax.ppermute(send_far, "servers", pairs[2])
        back_one = lax.ppermute(send_one, "servers", pairs[1])
        back_two_prompt = lax.ppermute(send_two_prompt, "servers", pairs[3])
        delta, far_ds = lax.optimization_barrier((delta, far_ds))
        shared = (queries, out_grad, lse_rows, delta)
        parents = (near_keys, near_ds, far_keys, far_ds)
        back = (own_sums, back_two)
        parts = [prompt_sums, back_far, back_one, back_two_prompt]
    else:
        count = lax.axis_size("servers")
        all_parts = lax.all_gather(own_part, "servers", axis=0, tiled=False)
        part = 2 * ROOT_ROWS
        all_roots = all_parts[:, :part].reshape(-1, HD)
        all_prompts = all_parts[:, part:].reshape(-1, HD)
        out_grad, lse_rows, delta, forks = out_grad_call(grad_out, out_weight, attn_out, lse, *forks)
        shared = (queries, out_grad, lse_rows, delta)
        prompt_ds, prompt_keys, prompt_sums = prompt_call(shared, [all_prompts], 2 * own, False)
        parent_ds, parent_keys, root_sums = parent_call(forks, shared, [all_roots])
        parents = (parent_keys, parent_ds)
        sends = jnp.concatenate(
            [root_sums.reshape(count, part, HD), prompt_sums.reshape(count, 2 * own, HD)], axis=1
        ).reshape(-1, HD)
        back = ()
        parts = [lax.psum_scatter(sends, "servers", scatter_dimension=0, tiled=True)]
    root_ds, child_ds, key_sums, value_sums = own_call(shared, keys, values)
    operands = (keys, root_ds, child_ds, prompt_keys, prompt_ds, *parents)
    grad_queries, *totals = query_call(*queries.shape, operands, back)
    parts = totals + parts
    grads = finish_call(key_sums, value_sums, parts, own)
    return (grad_queries, *grads)


def solution(mesh):
    placed = (
        P(("groups", "servers"), None),
        P(None, "heads"),
        P(("groups", "servers"), "heads"),
        P(("groups", "servers"), "heads"),
        P("heads", ("groups", "servers")),
        P(("groups", "servers"), "heads"),
        P(("groups", "servers"), "heads"),
        P(("groups", "servers"), "heads"),
        P(("groups", "servers"), "heads"),
        P("groups", None),
        P("groups"),
        P("groups"),
    )
    return jax.shard_map(
        local,
        mesh=mesh,
        in_specs=placed,
        out_specs=(P(("groups", "servers"), "heads"),) * 5,
        check_vma=False,
    )
```

```python
import math

import jax
import jax.numpy as jnp
from jax import lax
from jax.experimental import pallas as pl
from jax.experimental.pallas import tpu as pltpu
from jax.sharding import PartitionSpec as P

HD = 128
CH_DEV = 16
ROOTS_DEV = 4
RLEN = 64
CLEN = 16
MOST = 8
ROOT_ROWS = ROOTS_DEV * RLEN
BLOCK = 64
UNIT = 256
UNIT_HEADS = UNIT // BLOCK
PAIR = 2
SCALE = HD ** (-0.5)
LOG2E = math.log2(math.e)
NT = (((1,), (1,)), ((), ()))
NN = (((1,), (0,)), ((), ()))
TN = (((0,), (0,)), ((), ()))
F32 = jnp.float32
BF16 = jnp.bfloat16
VMEM = pl.BlockSpec(memory_space=pltpu.VMEM)
SMEM = pl.BlockSpec(memory_space=pltpu.SMEM)
ANY = pl.BlockSpec(memory_space=pl.ANY)


def params(mib):
    return pltpu.CompilerParams(vmem_limit_bytes=mib * 1024 * 1024)


COSTS = {
    "pack": 8,
    "repeat": 8,
    "out_grad": 6,
    "attend_near": 3,
    "attend_parent": 3,
    "attend_prompt": 0.1,
    "attend_far": 0.1,
    "attend_own": 0.1,
    "query_grads": 0.3,
    "finish": 0.01,
}


def cost(name):
    micros = COSTS[name]
    return pl.CostEstimate(flops=int(micros * (1 << 30)), transcendentals=0, bytes_accessed=1 << 16)


def pinned(array):
    return pltpu.with_memory_space_constraint(array, pltpu.VMEM)


def unmoved(array):
    return pltpu.with_memory_space_constraint(array, pltpu.HBM)


def pinned_scalars(array):
    return pltpu.with_memory_space_constraint(array, pltpu.SMEM)


def kept(shape, dtype):
    return pltpu.VMEM(shape, dtype)


def dot(left, right, numbers):
    return lax.dot_general(left, right, numbers, preferred_element_type=F32)


def pack_body(key_ref, value_ref, prefix_key_ref, prefix_value_ref, part_ref, sems):
    own = prefix_key_ref.shape[0]
    at = 2 * ROOT_ROWS
    copies = [
        (key_ref.at[0:ROOT_ROWS], part_ref.at[0:ROOT_ROWS]),
        (value_ref.at[0:ROOT_ROWS], part_ref.at[ROOT_ROWS:at]),
        (prefix_key_ref, part_ref.at[at : at + own]),
        (prefix_value_ref, part_ref.at[at + own : at + 2 * own]),
    ]
    started = [pltpu.make_async_copy(a, b, sems.at[i]) for i, (a, b) in enumerate(copies)]
    for copy in started:
        copy.start()
    for copy in started:
        copy.wait()


def pack_call(keys, values, prefix_keys, prefix_values):
    own = prefix_keys.shape[0]
    return pl.pallas_call(
        pack_body,
        in_specs=[ANY] * 4,
        out_specs=VMEM,
        out_shape=kept((2 * ROOT_ROWS + 2 * own, HD), BF16),
        scratch_shapes=[pltpu.SemaphoreType.DMA((4,))],
        compiler_params=params(4),
        cost_estimate=cost("pack"),
        name="pack",
    )(*(unmoved(x) for x in (keys, values, prefix_keys, prefix_values)))


def repeat_body(part_ref, part_out, prompt_out):
    part_out[...] = part_ref[...]
    prompt_out[...] = part_ref[2 * ROOT_ROWS :]


def repeat_call(part):
    return pl.pallas_call(
        repeat_body,
        in_specs=[VMEM],
        out_specs=[VMEM] * 2,
        out_shape=[kept(part.shape, BF16), kept((part.shape[0] - 2 * ROOT_ROWS, HD), BF16)],
        compiler_params=params(4),
        cost_estimate=cost("repeat"),
        name="repeat",
    )(pinned(part))


def unit_rows(array):
    heads, tokens = array.shape
    rows = []
    for start in range(0, ROOT_ROWS, BLOCK):
        for first in range(0, heads, UNIT_HEADS):
            picked = range(first, first + UNIT_HEADS)
            rows.append([array[head : head + 1, start : start + BLOCK] for head in picked])
    for start in range(ROOT_ROWS, tokens, PAIR * CLEN):
        starts = range(start, start + PAIR * CLEN, CLEN)
        rows.append([array[head : head + 1, at : at + CLEN] for at in starts for head in range(heads)])
    return [jnp.concatenate(row, axis=1) for row in rows]


def out_grad_body(
    grad_ref, weight_ref, attn_ref, lse_ref, owner_ref, root_ref, offset_ref, out_ref, lse_out, delta_out, forks_out
):
    rows, cols = out_ref.shape
    width = 2 * HD
    lane = lax.broadcasted_iota(jnp.int32, (rows, HD), 1)
    columns = jnp.zeros((rows, HD), F32)
    my_index = lax.axis_index("servers")
    for child in range(CH_DEV + 1):
        forks_out[CH_DEV + child] = CH_DEV
    found = jnp.int32(0)
    for child in range(CH_DEV):
        at = my_index * CH_DEV + child
        owner = owner_ref[at]
        forks_out[child] = (owner * ROOTS_DEV + root_ref[at]) * (2 * RLEN) + offset_ref[at]
        forks_out[CH_DEV + found] = child
        found = found + jnp.where((owner ^ my_index) == 3, 1, 0)
    forks_out[CH_DEV + found] = CH_DEV
    for unit, row in enumerate(unit_rows(lse_ref[...] * LOG2E)):
        lse_out[unit : unit + 1] = row
    for step in range(cols // width):
        part = slice(step * width, (step + 1) * width)
        wide = jnp.dot(grad_ref[...], weight_ref[:, part], preferred_element_type=F32).astype(BF16)
        out_ref[:, part] = wide
        products = wide.astype(F32) * attn_ref[:, part].astype(F32)
        for head in range(width // HD):
            total = jnp.sum(products[:, head * HD : (head + 1) * HD], axis=1, keepdims=True)
            columns = jnp.where(lane == step * (width // HD) + head, total, columns)
    for unit, row in enumerate(unit_rows(jnp.transpose(columns)[: cols // HD])):
        delta_out[unit : unit + 1] = row


def out_grad_call(grad_out, out_weight, attn_out, lse, *forks):
    rows = grad_out.shape[0]
    cols = out_weight.shape[1]
    units = rows * (cols // HD) // UNIT
    return pl.pallas_call(
        out_grad_body,
        in_specs=[VMEM] * 4 + [SMEM] * 3,
        out_specs=[VMEM] * 3 + [SMEM],
        out_shape=[
            kept((rows, cols), BF16),
            kept((units, UNIT), F32),
            kept((units, UNIT), F32),
            pltpu.SMEM((2 * CH_DEV + 1,), jnp.int32),
        ],
        compiler_params=params(12),
        cost_estimate=cost("out_grad"),
        name="out_grad",
    )(*(pinned(x) for x in (grad_out, out_weight, attn_out, lse)), *forks)


def unit_counts(tokens, heads):
    roots = ROOT_ROWS * heads // UNIT
    return roots, roots + (tokens - ROOT_ROWS) * heads // UNIT


def unit_tiles(tokens, heads, unit):
    roots, _ = unit_counts(tokens, heads)
    if unit < roots:
        block, part = divmod(unit, heads // UNIT_HEADS)
        picked = range(part * UNIT_HEADS, (part + 1) * UNIT_HEADS)
        return [(block * BLOCK, BLOCK, head) for head in picked]
    return [tile for k in range(PAIR) for tile in child_tiles(heads, (unit - roots) * PAIR + k)]


def child_tiles(heads, child):
    return [(ROOT_ROWS + child * CLEN, CLEN, head) for head in range(heads)]


def tiled(ref, tiles):
    return jnp.concatenate(
        [ref[start : start + rows, head * HD : (head + 1) * HD] for start, rows, head in tiles], axis=0
    )


def swept(jobs, load, parts, mask, keep, ahead=1):
    ready = []
    for job in [*jobs, *[None] * ahead]:
        if job is not None:
            query, out, lse, delta = load(job)
            keys, values = parts(job)
            ready.append((job, query, out, lse, delta, dot(keys, query, NT), dot(values, out, NT)))
        if job is not None and len(ready) <= ahead:
            continue
        done, query, out, lse, delta, scores, weight_grads = ready.pop(0)
        weights = mask(done, jnp.exp2(scores * (SCALE * LOG2E) - lse))
        score_grads = (weights * (weight_grads - delta)).astype(BF16)
        keep(done, dot(score_grads, query, NN), dot(weights.astype(BF16), out, NN), score_grads)


def unit_loader(q_ref, out_ref, lse_ref, delta_ref):
    tokens, heads = q_ref.shape[0], q_ref.shape[1] // HD

    def load(unit):
        tiles = unit_tiles(tokens, heads, unit)
        row = slice(unit, unit + 1)
        return tiled(q_ref, tiles), tiled(out_ref, tiles), lse_ref[row], delta_ref[row]

    return load


def child_loader(q_ref, out_ref, lse_ref, delta_ref):
    tokens, heads = q_ref.shape[0], q_ref.shape[1] // HD
    roots, _ = unit_counts(tokens, heads)

    def load(child):
        tiles = child_tiles(heads, child)
        unit, place = roots + child // PAIR, child % PAIR * heads * CLEN
        row, lanes = slice(unit, unit + 1), slice(place, place + heads * CLEN)
        return tiled(q_ref, tiles), tiled(out_ref, tiles), lse_ref[row, lanes], delta_ref[row, lanes]

    return load


def prompt_body(piece_rows, is_part, q_ref, out_ref, lse_ref, delta_ref, *refs):
    value_ref = refs[-1]
    if is_part:
        *pieces, ds_ref, key_ref, sums_ref, two_ref = refs[:-1]
    else:
        *pieces, ds_ref, key_ref, sums_ref = refs[:-1]
    own = piece_rows // 2
    count = 0
    for piece in pieces:
        first = 2 * ROOT_ROWS if is_part and piece.shape[0] > piece_rows else 0
        for at in range(first, piece.shape[0], piece_rows):
            key_ref[count : count + own] = piece[at : at + own]
            value_ref[count : count + own] = piece[at + own : at + piece_rows]
            count += own
    sums = [jnp.zeros((count, HD), F32), jnp.zeros((count, HD), F32)]

    def keep(unit, key_grad, value_grad, score_grads):
        ds_ref[unit] = score_grads
        sums[0] = sums[0] + key_grad
        sums[1] = sums[1] + value_grad

    swept(
        range(ds_ref.shape[0]),
        unit_loader(q_ref, out_ref, lse_ref, delta_ref),
        lambda unit: (key_ref[...], value_ref[...]),
        lambda unit, weights: weights,
        keep,
    )

    def store(ref, at, index):
        rows = slice(index * own, (index + 1) * own)
        ref[at : at + own] = (sums[0][rows] * SCALE).astype(ref.dtype)
        ref[at + own : at + piece_rows] = sums[1][rows].astype(ref.dtype)

    for index in range(count // own):
        store(sums_ref, index * piece_rows, index)
    if is_part:
        store(two_ref, 0, 3)


def prompt_call(shared, pieces, piece_rows, is_part):
    count = lax.axis_size("servers") * piece_rows // 2
    units = shared[2].shape[0]
    operands = [*shared, *pieces]
    shapes = [
        kept((units, count, UNIT), BF16),
        kept((count, HD), BF16),
        kept((2 * count, HD), F32),
    ]
    if is_part:
        shapes.append(kept((piece_rows, HD), BF16))

    def body(*refs):
        prompt_body(piece_rows, is_part, *refs)

    return pl.pallas_call(
        body,
        in_specs=[VMEM] * len(operands),
        out_specs=[VMEM] * len(shapes),
        out_shape=shapes,
        scratch_shapes=[pltpu.VMEM((count, HD), BF16)],
        compiler_params=params(12 if is_part else 20),
        cost_estimate=cost("attend_prompt"),
        name="attend_prompt",
    )(*(pinned(x) for x in operands))


def parent_body(held, has_prompt, fork_ref, q_ref, out_ref, lse_ref, delta_ref, *refs):
    is_part = held is not None
    count = len(held) if is_part else 1
    shards, refs = refs[:count], refs[count:]
    if has_prompt:
        prompt_ref, refs = refs[0], refs[1:]
    ds_ref, key_ref, *sum_refs = refs[:-2]
    grads_ref, sums_ref = refs[-2:]
    heads = q_ref.shape[1] // HD
    part = 2 * ROOT_ROWS
    my_index = lax.axis_index("servers")
    bases, limits = {}, {}

    def parts(child):
        fork = fork_ref[child]
        limit = fork & (2 * RLEN - 1)
        row = pl.multiple_of(((fork >> 7) & (ROOTS_DEV - 1)) * RLEN, RLEN)
        owner = fork >> 9
        if is_part:
            slot = owner ^ my_index
            at = row + ROOT_ROWS
            keys, values = shards[0][pl.ds(row, RLEN)], shards[0][pl.ds(at, RLEN)]
            place, inside = 0, slot == held[0]
            for index in range(1, count):
                here = slot == held[index]
                place, inside = jnp.where(here, index, place), inside | here
                keys = jnp.where(here, shards[index][pl.ds(row, RLEN)], keys)
                values = jnp.where(here, shards[index][pl.ds(at, RLEN)], values)
            bases[child] = pl.multiple_of(place * part + row, RLEN)
            limits[child] = jnp.where(inside, limit, 0)
        else:
            bases[child] = pl.multiple_of(owner * part + row, RLEN)
            limits[child] = limit
            keys = shards[0][pl.ds(bases[child], RLEN)]
            values = shards[0][pl.ds(bases[child] + ROOT_ROWS, RLEN)]
        key_ref[child] = keys
        return keys, values

    key_index = lax.broadcasted_iota(jnp.int32, (RLEN, heads * CLEN), 0)

    columns = heads * CLEN
    load = unit_loader(q_ref, out_ref, lse_ref, delta_ref)
    roots, _ = unit_counts(q_ref.shape[0], heads)
    empty = jnp.zeros((RLEN, columns), BF16)

    def diagonal(pieces):
        rows = [[piece if k == place else empty for place in range(PAIR)] for k, piece in enumerate(pieces)]
        return jnp.concatenate([jnp.concatenate(row, axis=1) for row in rows], axis=0)

    ready = []
    for pair in range(CH_DEV // PAIR + 3):
        if pair < CH_DEV // PAIR:
            query, out, lse, delta = load(roots + pair)
            held_parts = [parts(pair * PAIR + k) for k in range(PAIR)]
            scores = dot(jnp.concatenate([keys for keys, _ in held_parts], axis=0), query, NT)
            weight_grads = dot(jnp.concatenate([values for _, values in held_parts], axis=0), out, NT)
            ready.append((pair, query, out, lse, delta, scores, weight_grads))
            if len(ready) <= 3:
                continue
        done, query, out, lse, delta, scores, weight_grads = ready.pop(0)
        low, score_grads = [], []
        for k in range(PAIR):
            child = done * PAIR + k
            rows, lanes = slice(k * RLEN, (k + 1) * RLEN), slice(k * columns, (k + 1) * columns)
            weights = jnp.exp2(scores[rows, lanes] * (SCALE * LOG2E) - lse[:, lanes])
            weights = jnp.where(key_index < limits[child], weights, 0.0)
            grads = (weights * (weight_grads[rows, lanes] - delta[:, lanes])).astype(BF16)
            ds_ref[child] = grads
            low.append(weights.astype(BF16))
            score_grads.append(grads)
        key_grads = dot(diagonal(score_grads), query, NN) * SCALE
        value_grads = dot(diagonal(low), out, NN)
        for k in range(PAIR):
            child, rows = done * PAIR + k, slice(k * RLEN, (k + 1) * RLEN)
            grads_ref[child, 0:RLEN] = key_grads[rows]
            grads_ref[child, RLEN:] = value_grads[rows]
    sums_ref[...] = jnp.zeros(sums_ref.shape, F32)
    for child in range(CH_DEV):
        base = bases[child]
        sums_ref[pl.ds(base, RLEN)] = sums_ref[pl.ds(base, RLEN)] + grads_ref[child, 0:RLEN]
        base = base + ROOT_ROWS
        sums_ref[pl.ds(base, RLEN)] = sums_ref[pl.ds(base, RLEN)] + grads_ref[child, RLEN:]
    for index, ref in enumerate(sum_refs):
        first = index * part
        size = part if is_part else ref.shape[0]
        ref[0:size] = sums_ref[first : first + size].astype(ref.dtype)
        if is_part and ref.shape[0] > part:
            rows = ref.shape[0] - part
            first = held[index] * rows
            ref[part:] = prompt_ref[first : first + rows].astype(ref.dtype)


def parent_call(forks, shared, shards, held=None, sums=(), prompt_sums=None, name="attend_parent"):
    is_part = held is not None
    rows = 2 * ROOT_ROWS * len(shards) if is_part else shards[0].shape[0]
    columns = shared[0].shape[1] // HD * CLEN
    shapes = [kept((CH_DEV, RLEN, columns), BF16), kept((CH_DEV, RLEN, HD), BF16)]
    operands = [*shared, *shards]
    if is_part:
        shapes += sums
        if prompt_sums is not None:
            operands.append(prompt_sums)
    else:
        shapes.append(jax.ShapeDtypeStruct((rows, HD), F32))

    def body(*refs):
        parent_body(held, prompt_sums is not None, *refs)

    return pl.pallas_call(
        body,
        in_specs=[SMEM] + [VMEM] * len(operands),
        out_specs=[VMEM] * len(shapes),
        out_shape=shapes,
        scratch_shapes=[
            pltpu.VMEM((CH_DEV, 2 * RLEN, HD), F32),
            pltpu.VMEM((rows, HD), F32),
        ],
        compiler_params=params(8 if is_part else 40),
        cost_estimate=cost(name),
        name=name,
    )(pinned_scalars(forks), *(pinned(x) for x in operands))


def near_body(fork_ref, q_ref, out_ref, lse_ref, delta_ref, shard_ref, ds_ref, key_ref, send_ref, grads_ref, sums_ref):
    tokens, heads = q_ref.shape[0], q_ref.shape[1] // HD
    columns = heads * CLEN
    roots, _ = unit_counts(tokens, heads)
    ds_ref[...] = jnp.zeros(ds_ref.shape, BF16)
    key_ref[...] = jnp.zeros(key_ref.shape, BF16)
    key_index = lax.broadcasted_iota(jnp.int32, (RLEN, columns), 0)
    empty = jnp.zeros((RLEN, columns), BF16)

    def diagonal(pieces):
        rows = [[piece if k == place else empty for place in range(PAIR)] for k, piece in enumerate(pieces)]
        return jnp.concatenate([jnp.concatenate(row, axis=1) for row in rows], axis=0)

    def tiles(ref, starts):
        return jnp.concatenate(
            [ref[pl.ds(start, CLEN), head * HD : (head + 1) * HD] for start in starts for head in range(heads)], axis=0
        )

    def half(ref, child):
        row = ref[pl.ds(roots + child // PAIR, 1)]
        return jnp.where(child % PAIR == 0, row[:, :columns], row[:, columns:])

    places, ready = [], []
    for pair in range(MOST // PAIR + 2):
        if pair < MOST // PAIR:
            picked, starts, keys, values, lse, delta = [], [], [], [], [], []
            for k in range(PAIR):
                target = fork_ref[CH_DEV + pair * PAIR + k]
                child = jnp.minimum(target, CH_DEV - 1)
                fork = fork_ref[child]
                limit = jnp.where(target < CH_DEV, fork & (2 * RLEN - 1), 0)
                row = pl.multiple_of(((fork >> 7) & (ROOTS_DEV - 1)) * RLEN, RLEN)
                starts.append(pl.multiple_of(ROOT_ROWS + child * CLEN, CLEN))
                keys.append(shard_ref[pl.ds(row, RLEN)])
                values.append(shard_ref[pl.ds(row + ROOT_ROWS, RLEN)])
                lse.append(half(lse_ref, child))
                delta.append(half(delta_ref, child))
                key_ref[target] = keys[k]
                picked.append((target, limit, row))
            places += [row for _, _, row in picked]
            query, out = tiles(q_ref, starts), tiles(out_ref, starts)
            scores = dot(jnp.concatenate(keys, axis=0), query, NT)
            weight_grads = dot(jnp.concatenate(values, axis=0), out, NT)
            ready.append((pair, picked, query, out, lse, delta, scores, weight_grads))
            if len(ready) <= 2:
                continue
        done, picked, query, out, lse, delta, scores, weight_grads = ready.pop(0)
        low, score_grads = [], []
        for k, (target, limit, _) in enumerate(picked):
            rows, lanes = slice(k * RLEN, (k + 1) * RLEN), slice(k * columns, (k + 1) * columns)
            weights = jnp.exp2(scores[rows, lanes] * (SCALE * LOG2E) - lse[k])
            weights = jnp.where(key_index < limit, weights, 0.0)
            grads = (weights * (weight_grads[rows, lanes] - delta[k])).astype(BF16)
            ds_ref[target] = grads
            low.append(weights.astype(BF16))
            score_grads.append(grads)
        key_grads = dot(diagonal(score_grads), query, NN) * SCALE
        value_grads = dot(diagonal(low), out, NN)
        for k in range(PAIR):
            rows = slice(k * RLEN, (k + 1) * RLEN)
            grads_ref[done * PAIR + k, 0:RLEN] = key_grads[rows]
            grads_ref[done * PAIR + k, RLEN:] = value_grads[rows]
    sums_ref[...] = jnp.zeros(sums_ref.shape, F32)
    for index, row in enumerate(places):
        sums_ref[pl.ds(row, RLEN)] = sums_ref[pl.ds(row, RLEN)] + grads_ref[index, 0:RLEN]
        at = row + ROOT_ROWS
        sums_ref[pl.ds(at, RLEN)] = sums_ref[pl.ds(at, RLEN)] + grads_ref[index, RLEN:]
    send_ref[...] = sums_ref[...].astype(BF16)


def near_call(forks, shared, shard):
    columns = shared[0].shape[1] // HD * CLEN
    part = 2 * ROOT_ROWS
    return pl.pallas_call(
        near_body,
        in_specs=[SMEM] + [VMEM] * 5,
        out_specs=[VMEM] * 3,
        out_shape=[
            kept((CH_DEV + 1, RLEN, columns), BF16),
            kept((CH_DEV + 1, RLEN, HD), BF16),
            kept((part, HD), BF16),
        ],
        scratch_shapes=[pltpu.VMEM((MOST, 2 * RLEN, HD), F32), pltpu.VMEM((part, HD), F32)],
        compiler_params=params(8),
        cost_estimate=cost("attend_near"),
        name="attend_near",
    )(pinned_scalars(forks), *(pinned(x) for x in (*shared, shard)))


def own_rows(tokens, heads, unit):
    roots, _ = unit_counts(tokens, heads)
    if unit < roots:
        start = unit // (heads // UNIT_HEADS) * BLOCK
        return slice(start, start + BLOCK)
    start = ROOT_ROWS + (unit - roots) * PAIR * CLEN
    return slice(start, start + PAIR * CLEN)


def own_body(q_ref, out_ref, lse_ref, delta_ref, key_ref, value_ref, root_ds_ref, child_ds_ref, keys_out, values_out):
    tokens, heads = q_ref.shape[0], q_ref.shape[1] // HD
    roots, units = unit_counts(tokens, heads)
    per_block = heads // UNIT_HEADS
    key_index = lax.broadcasted_iota(jnp.int32, (BLOCK, UNIT), 0)
    column = lax.broadcasted_iota(jnp.int32, (BLOCK, UNIT), 1)
    root_allowed = key_index <= column % BLOCK
    key_index, column = key_index[: PAIR * CLEN], column[: PAIR * CLEN]
    child_allowed = (key_index // CLEN == column // (heads * CLEN)) & (key_index % CLEN <= column % CLEN)
    totals = [None, None]

    def parts(unit):
        rows = own_rows(tokens, heads, unit)
        return key_ref[rows], value_ref[rows]

    def keep(unit, key_grad, value_grad, score_grads):
        rows = own_rows(tokens, heads, unit)
        if unit >= roots:
            child_ds_ref[unit - roots] = score_grads
            keys_out[rows] = key_grad * SCALE
            values_out[rows] = value_grad
            return
        root_ds_ref[unit] = score_grads
        totals[0] = key_grad if unit % per_block == 0 else totals[0] + key_grad
        totals[1] = value_grad if unit % per_block == 0 else totals[1] + value_grad
        if unit % per_block == per_block - 1:
            keys_out[rows] = totals[0] * SCALE
            values_out[rows] = totals[1]

    swept(
        range(units),
        unit_loader(q_ref, out_ref, lse_ref, delta_ref),
        parts,
        lambda unit, weights: jnp.where(root_allowed if unit < roots else child_allowed, weights, 0.0),
        keep,
    )


def own_call(shared, keys, values):
    tokens, width = shared[0].shape
    roots, units = unit_counts(tokens, width // HD)
    return pl.pallas_call(
        own_body,
        in_specs=[VMEM] * 6,
        out_specs=[VMEM] * 4,
        out_shape=[
            kept((roots, BLOCK, UNIT), BF16),
            kept((units - roots, PAIR * CLEN, UNIT), BF16),
            kept((tokens, HD), F32),
            kept((tokens, HD), F32),
        ],
        compiler_params=params(8),
        cost_estimate=cost("attend_own"),
        name="attend_own",
    )(*(pinned(x) for x in (*shared, keys, values)))


def query_body(has_back, key_ref, root_ds_ref, child_ds_ref, prompt_ref, prompt_ds_ref, *refs):
    if has_back:
        *parent_refs, sums_ref, back_ref, gq_ref, total_ref, gq_vmem, sems = refs
        total_ref[...] = sums_ref[...] + back_ref[...].astype(F32)
    else:
        *parent_refs, gq_ref, gq_vmem, sems = refs
    tokens, heads = gq_vmem.shape[0], gq_vmem.shape[1] // HD
    roots, units = unit_counts(tokens, heads)
    copies = []

    def store(tiles, total):
        at = 0
        for start, rows, head in tiles:
            piece = total[at : at + rows] * SCALE
            gq_vmem[start : start + rows, head * HD : (head + 1) * HD] = piece.astype(BF16)
            at += rows

    for unit in range(units):
        tiles = unit_tiles(tokens, heads, unit)
        own_ds = root_ds_ref[unit] if unit < roots else child_ds_ref[unit - roots]
        grads = jnp.concatenate([own_ds, prompt_ds_ref[unit]], axis=0)
        total = dot(grads, jnp.concatenate([key_ref[own_rows(tokens, heads, unit)], prompt_ref[...]], axis=0), TN)
        if unit < roots:
            store(tiles, total)
        else:
            columns = heads * CLEN
            for k in range(PAIR):
                child = (unit - roots) * PAIR + k
                grads = jnp.concatenate([ref[child] for ref in parent_refs[1::2]], axis=0)
                keys = jnp.concatenate([ref[child] for ref in parent_refs[0::2]], axis=0)
                store(child_tiles(heads, child), total[k * columns : (k + 1) * columns] + dot(grads, keys, TN))
        done = tiles[-1][0] + tiles[-1][1]
        first = len(copies) * BLOCK
        if done >= first + BLOCK and (unit + 1 >= roots or (unit + 1) % (heads // UNIT_HEADS) == 0):
            rows = slice(first, first + BLOCK)
            copy = pltpu.make_async_copy(gq_vmem.at[rows], gq_ref.at[rows], sems.at[len(copies)])
            copy.start()
            copies.append(copy)
    for copy in copies:
        copy.wait()


def query_call(tokens, width, operands, back=()):
    shapes = [jax.ShapeDtypeStruct((tokens, width), BF16), *(kept(x.shape, F32) for x in back[:1])]
    operands = [*operands, *back]

    def body(*refs):
        query_body(bool(back), *refs)

    return pl.pallas_call(
        body,
        in_specs=[VMEM] * len(operands),
        out_specs=[ANY, *[VMEM] * (len(shapes) - 1)],
        out_shape=shapes,
        scratch_shapes=[pltpu.VMEM((tokens, width), BF16), pltpu.SemaphoreType.DMA((tokens // BLOCK,))],
        compiler_params=params(12),
        cost_estimate=cost("query_grads"),
        name="query_grads",
    )(*(pinned(x) for x in operands))


def finish_body(key_ref, value_ref, *refs):
    parts = refs[:-4]
    keys_out, values_out, prefix_keys_out, prefix_values_out = refs[-4:]
    own = prefix_keys_out.shape[0]
    part = 2 * ROOT_ROWS
    total, prompt = [], []
    for ref in parts:
        rows = ref.shape[0]
        if rows >= part:
            total.append(ref[0:part].astype(F32))
        if rows != part:
            first = rows - 2 * own if rows > part else 0
            prompt.append(ref[first : first + 2 * own].astype(F32))
    total, prompt = sum(total[1:], total[0]), sum(prompt[1:], prompt[0])
    keys_out[0:ROOT_ROWS] = (key_ref[0:ROOT_ROWS] + total[0:ROOT_ROWS]).astype(BF16)
    keys_out[ROOT_ROWS:] = key_ref[ROOT_ROWS:].astype(BF16)
    values_out[0:ROOT_ROWS] = (value_ref[0:ROOT_ROWS] + total[ROOT_ROWS:]).astype(BF16)
    values_out[ROOT_ROWS:] = value_ref[ROOT_ROWS:].astype(BF16)
    prefix_keys_out[...] = prompt[0:own].astype(BF16)
    prefix_values_out[...] = prompt[own:].astype(BF16)


def finish_call(key_sums, value_sums, parts, own):
    shapes = [jax.ShapeDtypeStruct(key_sums.shape, BF16)] * 2 + [jax.ShapeDtypeStruct((own, HD), BF16)] * 2
    return pl.pallas_call(
        finish_body,
        in_specs=[VMEM] * (2 + len(parts)),
        out_specs=[VMEM] * 4,
        out_shape=shapes,
        compiler_params=params(8),
        cost_estimate=cost("finish"),
        name="finish",
    )(*(pinned(x) for x in (key_sums, value_sums, *parts)))


def local(
    grad_out,
    out_weight,
    queries,
    attn_out,
    lse,
    keys,
    values,
    prefix_keys,
    prefix_values,
    fork_owner,
    fork_root,
    fork_offset,
):
    own_part = pack_call(keys, values, prefix_keys, prefix_values)
    forks = [fork_owner.reshape(-1), fork_root, fork_offset]
    own = prefix_keys.shape[0]
    if lax.axis_size("servers") == 4:
        pairs = [[(i, i ^ d) for i in range(4)] for d in range(4)]
        part_two = lax.ppermute(own_part, "servers", pairs[3])
        later_part, later_prompt = repeat_call(own_part)
        prompt_far = lax.ppermute(later_prompt, "servers", pairs[2])
        part_one = lax.ppermute(later_part, "servers", pairs[1])
        out_grad, lse_rows, delta, forks = out_grad_call(grad_out, out_weight, attn_out, lse, *forks)
        part_two, delta = lax.optimization_barrier((part_two, delta))
        part_far = lax.ppermute(part_two[: 2 * ROOT_ROWS], "servers", pairs[1])
        part, whole = (2 * ROOT_ROWS, HD), (2 * ROOT_ROWS + 2 * own, HD)
        near_ds, near_keys, send_two = near_call(forks, (queries, out_grad, lse_rows, delta), part_two)
        back_two = lax.ppermute(send_two, "servers", pairs[3])
        delta, near_ds = lax.optimization_barrier((delta, near_ds))
        prompt_ds, prompt_keys, prompt_sums, send_two_prompt = prompt_call(
            (queries, out_grad, lse_rows, delta), [own_part, part_one, prompt_far, part_two], 2 * own, True
        )
        far_ds, far_keys, own_sums, send_far, send_one = parent_call(
            forks,
            (queries, out_grad, lse_rows, delta),
            [own_part, part_far, part_one],
            (0, 2, 1),
            [kept(part, F32), kept(whole, BF16), kept(whole, BF16)],
            prompt_sums,
            "attend_far",
        )
        back_far = lax.ppermute(send_far, "servers", pairs[2])
        back_one = lax.ppermute(send_one, "servers", pairs[1])
        back_two_prompt = lax.ppermute(send_two_prompt, "servers", pairs[3])
        delta, far_ds = lax.optimization_barrier((delta, far_ds))
        shared = (queries, out_grad, lse_rows, delta)
        parents = (near_keys, near_ds, far_keys, far_ds)
        back = (own_sums, back_two)
        parts = [prompt_sums, back_far, back_one, back_two_prompt]
    else:
        count = lax.axis_size("servers")
        all_parts = lax.all_gather(own_part, "servers", axis=0, tiled=False)
        part = 2 * ROOT_ROWS
        all_roots = all_parts[:, :part].reshape(-1, HD)
        all_prompts = all_parts[:, part:].reshape(-1, HD)
        out_grad, lse_rows, delta, forks = out_grad_call(grad_out, out_weight, attn_out, lse, *forks)
        shared = (queries, out_grad, lse_rows, delta)
        prompt_ds, prompt_keys, prompt_sums = prompt_call(shared, [all_prompts], 2 * own, False)
        parent_ds, parent_keys, root_sums = parent_call(forks, shared, [all_roots])
        parents = (parent_keys, parent_ds)
        sends = jnp.concatenate(
            [root_sums.reshape(count, part, HD), prompt_sums.reshape(count, 2 * own, HD)], axis=1
        ).reshape(-1, HD)
        back = ()
        parts = [lax.psum_scatter(sends, "servers", scatter_dimension=0, tiled=True)]
    root_ds, child_ds, key_sums, value_sums = own_call(shared, keys, values)
    operands = (keys, root_ds, child_ds, prompt_keys, prompt_ds, *parents)
    grad_queries, *totals = query_call(*queries.shape, operands, back)
    parts = totals + parts
    grads = finish_call(key_sums, value_sums, parts, own)
    return (grad_queries, *grads)


def solution(mesh):
    placed = (
        P(("groups", "servers"), None),
        P(None, "heads"),
        P(("groups", "servers"), "heads"),
        P(("groups", "servers"), "heads"),
        P("heads", ("groups", "servers")),
        P(("groups", "servers"), "heads"),
        P(("groups", "servers"), "heads"),
        P(("groups", "servers"), "heads"),
        P(("groups", "servers"), "heads"),
        P("groups", None),
        P("groups"),
        P("groups"),
    )
    return jax.shard_map(
        local,
        mesh=mesh,
        in_specs=placed,
        out_specs=(P(("groups", "servers"), "heads"),) * 5,
        check_vma=False,
    )
```

```python
import math

import jax
import jax.numpy as jnp
from jax import lax
from jax.experimental import pallas as pl
from jax.experimental.pallas import tpu as pltpu
from jax.sharding import PartitionSpec as P

HD = 128
CH_DEV = 16
ROOTS_DEV = 4
RLEN = 64
CLEN = 16
MOST = 8
ROOT_ROWS = ROOTS_DEV * RLEN
BLOCK = 64
UNIT = 256
UNIT_HEADS = UNIT // BLOCK
PAIR = 2
SCALE = HD ** (-0.5)
LOG2E = math.log2(math.e)
NT = (((1,), (1,)), ((), ()))
NN = (((1,), (0,)), ((), ()))
TN = (((0,), (0,)), ((), ()))
F32 = jnp.float32
BF16 = jnp.bfloat16
VMEM = pl.BlockSpec(memory_space=pltpu.VMEM)
SMEM = pl.BlockSpec(memory_space=pltpu.SMEM)
ANY = pl.BlockSpec(memory_space=pl.ANY)


def params(mib):
    return pltpu.CompilerParams(vmem_limit_bytes=mib * 1024 * 1024)


COSTS = {
    "pack": 8,
    "repeat": 8,
    "out_grad": 6,
    "attend_near": 3,
    "attend_parent": 3,
    "attend_prompt": 0.1,
    "attend_far": 0.1,
    "attend_own": 0.1,
    "query_grads": 0.3,
    "finish": 0.01,
}


def cost(name):
    micros = COSTS[name]
    return pl.CostEstimate(flops=int(micros * (1 << 30)), transcendentals=0, bytes_accessed=1 << 16)


def pinned(array):
    return pltpu.with_memory_space_constraint(array, pltpu.VMEM)


def unmoved(array):
    return pltpu.with_memory_space_constraint(array, pltpu.HBM)


def pinned_scalars(array):
    return pltpu.with_memory_space_constraint(array, pltpu.SMEM)


def kept(shape, dtype):
    return pltpu.VMEM(shape, dtype)


def dot(left, right, numbers):
    return lax.dot_general(left, right, numbers, preferred_element_type=F32)


def pack_body(key_ref, value_ref, prefix_key_ref, prefix_value_ref, part_ref, sems):
    own = prefix_key_ref.shape[0]
    at = 2 * ROOT_ROWS
    copies = [
        (key_ref.at[0:ROOT_ROWS], part_ref.at[0:ROOT_ROWS]),
        (value_ref.at[0:ROOT_ROWS], part_ref.at[ROOT_ROWS:at]),
        (prefix_key_ref, part_ref.at[at : at + own]),
        (prefix_value_ref, part_ref.at[at + own : at + 2 * own]),
    ]
    started = [pltpu.make_async_copy(a, b, sems.at[i]) for i, (a, b) in enumerate(copies)]
    for copy in started:
        copy.start()
    for copy in started:
        copy.wait()


def pack_call(keys, values, prefix_keys, prefix_values):
    own = prefix_keys.shape[0]
    return pl.pallas_call(
        pack_body,
        in_specs=[ANY] * 4,
        out_specs=VMEM,
        out_shape=kept((2 * ROOT_ROWS + 2 * own, HD), BF16),
        scratch_shapes=[pltpu.SemaphoreType.DMA((4,))],
        compiler_params=params(4),
        cost_estimate=cost("pack"),
        name="pack",
    )(*(unmoved(x) for x in (keys, values, prefix_keys, prefix_values)))


def repeat_body(part_ref, part_out, prompt_out):
    part_out[...] = part_ref[...]
    prompt_out[...] = part_ref[2 * ROOT_ROWS :]


def repeat_call(part):
    return pl.pallas_call(
        repeat_body,
        in_specs=[VMEM],
        out_specs=[VMEM] * 2,
        out_shape=[kept(part.shape, BF16), kept((part.shape[0] - 2 * ROOT_ROWS, HD), BF16)],
        compiler_params=params(4),
        cost_estimate=cost("repeat"),
        name="repeat",
    )(pinned(part))


def unit_rows(array):
    heads, tokens = array.shape
    rows = []
    for start in range(0, ROOT_ROWS, BLOCK):
        for first in range(0, heads, UNIT_HEADS):
            picked = range(first, first + UNIT_HEADS)
            rows.append([array[head : head + 1, start : start + BLOCK] for head in picked])
    for start in range(ROOT_ROWS, tokens, PAIR * CLEN):
        starts = range(start, start + PAIR * CLEN, CLEN)
        rows.append([array[head : head + 1, at : at + CLEN] for at in starts for head in range(heads)])
    return [jnp.concatenate(row, axis=1) for row in rows]


def out_grad_body(
    grad_ref, weight_ref, attn_ref, lse_ref, owner_ref, root_ref, offset_ref, out_ref, lse_out, delta_out, forks_out
):
    rows, cols = out_ref.shape
    width = 2 * HD
    lane = lax.broadcasted_iota(jnp.int32, (rows, HD), 1)
    columns = jnp.zeros((rows, HD), F32)
    my_index = lax.axis_index("servers")
    for child in range(CH_DEV + 1):
        forks_out[CH_DEV + child] = CH_DEV
    found = jnp.int32(0)
    for child in range(CH_DEV):
        at = my_index * CH_DEV + child
        owner = owner_ref[at]
        forks_out[child] = (owner * ROOTS_DEV + root_ref[at]) * (2 * RLEN) + offset_ref[at]
        forks_out[CH_DEV + found] = child
        found = found + jnp.where((owner ^ my_index) == 3, 1, 0)
    forks_out[CH_DEV + found] = CH_DEV
    for unit, row in enumerate(unit_rows(lse_ref[...] * LOG2E)):
        lse_out[unit : unit + 1] = row
    for step in range(cols // width):
        part = slice(step * width, (step + 1) * width)
        wide = jnp.dot(grad_ref[...], weight_ref[:, part], preferred_element_type=F32).astype(BF16)
        out_ref[:, part] = wide
        products = wide.astype(F32) * attn_ref[:, part].astype(F32)
        for head in range(width // HD):
            total = jnp.sum(products[:, head * HD : (head + 1) * HD], axis=1, keepdims=True)
            columns = jnp.where(lane == step * (width // HD) + head, total, columns)
    for unit, row in enumerate(unit_rows(jnp.transpose(columns)[: cols // HD])):
        delta_out[unit : unit + 1] = row


def out_grad_call(grad_out, out_weight, attn_out, lse, *forks):
    rows = grad_out.shape[0]
    cols = out_weight.shape[1]
    units = rows * (cols // HD) // UNIT
    return pl.pallas_call(
        out_grad_body,
        in_specs=[VMEM] * 4 + [SMEM] * 3,
        out_specs=[VMEM] * 3 + [SMEM],
        out_shape=[
            kept((rows, cols), BF16),
            kept((units, UNIT), F32),
            kept((units, UNIT), F32),
            pltpu.SMEM((2 * CH_DEV + 1,), jnp.int32),
        ],
        compiler_params=params(12),
        cost_estimate=cost("out_grad"),
        name="out_grad",
    )(*(pinned(x) for x in (grad_out, out_weight, attn_out, lse)), *forks)


def unit_counts(tokens, heads):
    roots = ROOT_ROWS * heads // UNIT
    return roots, roots + (tokens - ROOT_ROWS) * heads // UNIT


def unit_tiles(tokens, heads, unit):
    roots, _ = unit_counts(tokens, heads)
    if unit < roots:
        block, part = divmod(unit, heads // UNIT_HEADS)
        picked = range(part * UNIT_HEADS, (part + 1) * UNIT_HEADS)
        return [(block * BLOCK, BLOCK, head) for head in picked]
    return [tile for k in range(PAIR) for tile in child_tiles(heads, (unit - roots) * PAIR + k)]


def child_tiles(heads, child):
    return [(ROOT_ROWS + child * CLEN, CLEN, head) for head in range(heads)]


def tiled(ref, tiles):
    return jnp.concatenate(
        [ref[start : start + rows, head * HD : (head + 1) * HD] for start, rows, head in tiles], axis=0
    )


def swept(jobs, load, parts, mask, keep, ahead=1):
    ready = []
    for job in [*jobs, *[None] * ahead]:
        if job is not None:
            query, out, lse, delta = load(job)
            keys, values = parts(job)
            ready.append((job, query, out, lse, delta, dot(keys, query, NT), dot(values, out, NT)))
        if job is not None and len(ready) <= ahead:
            continue
        done, query, out, lse, delta, scores, weight_grads = ready.pop(0)
        weights = mask(done, jnp.exp2(scores * (SCALE * LOG2E) - lse))
        score_grads = (weights * (weight_grads - delta)).astype(BF16)
        keep(done, dot(score_grads, query, NN), dot(weights.astype(BF16), out, NN), score_grads)


def unit_loader(q_ref, out_ref, lse_ref, delta_ref):
    tokens, heads = q_ref.shape[0], q_ref.shape[1] // HD

    def load(unit):
        tiles = unit_tiles(tokens, heads, unit)
        row = slice(unit, unit + 1)
        return tiled(q_ref, tiles), tiled(out_ref, tiles), lse_ref[row], delta_ref[row]

    return load


def child_loader(q_ref, out_ref, lse_ref, delta_ref):
    tokens, heads = q_ref.shape[0], q_ref.shape[1] // HD
    roots, _ = unit_counts(tokens, heads)

    def load(child):
        tiles = child_tiles(heads, child)
        unit, place = roots + child // PAIR, child % PAIR * heads * CLEN
        row, lanes = slice(unit, unit + 1), slice(place, place + heads * CLEN)
        return tiled(q_ref, tiles), tiled(out_ref, tiles), lse_ref[row, lanes], delta_ref[row, lanes]

    return load


def prompt_body(piece_rows, is_part, q_ref, out_ref, lse_ref, delta_ref, *refs):
    value_ref = refs[-1]
    if is_part:
        *pieces, ds_ref, key_ref, sums_ref, two_ref = refs[:-1]
    else:
        *pieces, ds_ref, key_ref, sums_ref = refs[:-1]
    own = piece_rows // 2
    count = 0
    for piece in pieces:
        first = 2 * ROOT_ROWS if is_part and piece.shape[0] > piece_rows else 0
        for at in range(first, piece.shape[0], piece_rows):
            key_ref[count : count + own] = piece[at : at + own]
            value_ref[count : count + own] = piece[at + own : at + piece_rows]
            count += own
    sums = [jnp.zeros((count, HD), F32), jnp.zeros((count, HD), F32)]

    def keep(unit, key_grad, value_grad, score_grads):
        ds_ref[unit] = score_grads
        sums[0] = sums[0] + key_grad
        sums[1] = sums[1] + value_grad

    swept(
        range(ds_ref.shape[0]),
        unit_loader(q_ref, out_ref, lse_ref, delta_ref),
        lambda unit: (key_ref[...], value_ref[...]),
        lambda unit, weights: weights,
        keep,
        2,
    )

    def store(ref, at, index):
        rows = slice(index * own, (index + 1) * own)
        ref[at : at + own] = (sums[0][rows] * SCALE).astype(ref.dtype)
        ref[at + own : at + piece_rows] = sums[1][rows].astype(ref.dtype)

    for index in range(count // own):
        store(sums_ref, index * piece_rows, index)
    if is_part:
        store(two_ref, 0, 3)


def prompt_call(shared, pieces, piece_rows, is_part):
    count = lax.axis_size("servers") * piece_rows // 2
    units = shared[2].shape[0]
    operands = [*shared, *pieces]
    shapes = [
        kept((units, count, UNIT), BF16),
        kept((count, HD), BF16),
        kept((2 * count, HD), F32),
    ]
    if is_part:
        shapes.append(kept((piece_rows, HD), BF16))

    def body(*refs):
        prompt_body(piece_rows, is_part, *refs)

    return pl.pallas_call(
        body,
        in_specs=[VMEM] * len(operands),
        out_specs=[VMEM] * len(shapes),
        out_shape=shapes,
        scratch_shapes=[pltpu.VMEM((count, HD), BF16)],
        compiler_params=params(12 if is_part else 20),
        cost_estimate=cost("attend_prompt"),
        name="attend_prompt",
    )(*(pinned(x) for x in operands))


def parent_body(held, has_prompt, fork_ref, q_ref, out_ref, lse_ref, delta_ref, *refs):
    is_part = held is not None
    count = len(held) if is_part else 1
    shards, refs = refs[:count], refs[count:]
    if has_prompt:
        prompt_ref, refs = refs[0], refs[1:]
    ds_ref, key_ref, *sum_refs = refs[:-2]
    grads_ref, sums_ref = refs[-2:]
    heads = q_ref.shape[1] // HD
    part = 2 * ROOT_ROWS
    my_index = lax.axis_index("servers")
    bases, limits = {}, {}

    def parts(child):
        fork = fork_ref[child]
        limit = fork & (2 * RLEN - 1)
        row = pl.multiple_of(((fork >> 7) & (ROOTS_DEV - 1)) * RLEN, RLEN)
        owner = fork >> 9
        if is_part:
            slot = owner ^ my_index
            at = row + ROOT_ROWS
            keys, values = shards[0][pl.ds(row, RLEN)], shards[0][pl.ds(at, RLEN)]
            place, inside = 0, slot == held[0]
            for index in range(1, count):
                here = slot == held[index]
                place, inside = jnp.where(here, index, place), inside | here
                keys = jnp.where(here, shards[index][pl.ds(row, RLEN)], keys)
                values = jnp.where(here, shards[index][pl.ds(at, RLEN)], values)
            bases[child] = pl.multiple_of(place * part + row, RLEN)
            limits[child] = jnp.where(inside, limit, 0)
        else:
            bases[child] = pl.multiple_of(owner * part + row, RLEN)
            limits[child] = limit
            keys = shards[0][pl.ds(bases[child], RLEN)]
            values = shards[0][pl.ds(bases[child] + ROOT_ROWS, RLEN)]
        key_ref[child] = keys
        return keys, values

    key_index = lax.broadcasted_iota(jnp.int32, (RLEN, heads * CLEN), 0)

    columns = heads * CLEN
    load = unit_loader(q_ref, out_ref, lse_ref, delta_ref)
    roots, _ = unit_counts(q_ref.shape[0], heads)
    empty = jnp.zeros((RLEN, columns), BF16)

    def diagonal(pieces):
        rows = [[piece if k == place else empty for place in range(PAIR)] for k, piece in enumerate(pieces)]
        return jnp.concatenate([jnp.concatenate(row, axis=1) for row in rows], axis=0)

    ready = []
    for pair in range(CH_DEV // PAIR + 3):
        if pair < CH_DEV // PAIR:
            query, out, lse, delta = load(roots + pair)
            held_parts = [parts(pair * PAIR + k) for k in range(PAIR)]
            scores = dot(jnp.concatenate([keys for keys, _ in held_parts], axis=0), query, NT)
            weight_grads = dot(jnp.concatenate([values for _, values in held_parts], axis=0), out, NT)
            ready.append((pair, query, out, lse, delta, scores, weight_grads))
            if len(ready) <= 3:
                continue
        done, query, out, lse, delta, scores, weight_grads = ready.pop(0)
        low, score_grads = [], []
        for k in range(PAIR):
            child = done * PAIR + k
            rows, lanes = slice(k * RLEN, (k + 1) * RLEN), slice(k * columns, (k + 1) * columns)
            weights = jnp.exp2(scores[rows, lanes] * (SCALE * LOG2E) - lse[:, lanes])
            weights = jnp.where(key_index < limits[child], weights, 0.0)
            grads = (weights * (weight_grads[rows, lanes] - delta[:, lanes])).astype(BF16)
            ds_ref[child] = grads
            low.append(weights.astype(BF16))
            score_grads.append(grads)
        key_grads = dot(diagonal(score_grads), query, NN) * SCALE
        value_grads = dot(diagonal(low), out, NN)
        for k in range(PAIR):
            child, rows = done * PAIR + k, slice(k * RLEN, (k + 1) * RLEN)
            grads_ref[child, 0:RLEN] = key_grads[rows]
            grads_ref[child, RLEN:] = value_grads[rows]
    sums_ref[...] = jnp.zeros(sums_ref.shape, F32)
    for child in range(CH_DEV):
        base = bases[child]
        sums_ref[pl.ds(base, RLEN)] = sums_ref[pl.ds(base, RLEN)] + grads_ref[child, 0:RLEN]
        base = base + ROOT_ROWS
        sums_ref[pl.ds(base, RLEN)] = sums_ref[pl.ds(base, RLEN)] + grads_ref[child, RLEN:]
    for index, ref in enumerate(sum_refs):
        first = index * part
        size = part if is_part else ref.shape[0]
        ref[0:size] = sums_ref[first : first + size].astype(ref.dtype)
        if is_part and ref.shape[0] > part:
            rows = ref.shape[0] - part
            first = held[index] * rows
            ref[part:] = prompt_ref[first : first + rows].astype(ref.dtype)


def parent_call(forks, shared, shards, held=None, sums=(), prompt_sums=None, name="attend_parent"):
    is_part = held is not None
    rows = 2 * ROOT_ROWS * len(shards) if is_part else shards[0].shape[0]
    columns = shared[0].shape[1] // HD * CLEN
    shapes = [kept((CH_DEV, RLEN, columns), BF16), kept((CH_DEV, RLEN, HD), BF16)]
    operands = [*shared, *shards]
    if is_part:
        shapes += sums
        if prompt_sums is not None:
            operands.append(prompt_sums)
    else:
        shapes.append(jax.ShapeDtypeStruct((rows, HD), F32))

    def body(*refs):
        parent_body(held, prompt_sums is not None, *refs)

    return pl.pallas_call(
        body,
        in_specs=[SMEM] + [VMEM] * len(operands),
        out_specs=[VMEM] * len(shapes),
        out_shape=shapes,
        scratch_shapes=[
            pltpu.VMEM((CH_DEV, 2 * RLEN, HD), F32),
            pltpu.VMEM((rows, HD), F32),
        ],
        compiler_params=params(8 if is_part else 40),
        cost_estimate=cost(name),
        name=name,
    )(pinned_scalars(forks), *(pinned(x) for x in operands))


def near_body(fork_ref, q_ref, out_ref, lse_ref, delta_ref, shard_ref, ds_ref, key_ref, send_ref, grads_ref, sums_ref):
    tokens, heads = q_ref.shape[0], q_ref.shape[1] // HD
    columns = heads * CLEN
    roots, _ = unit_counts(tokens, heads)
    ds_ref[...] = jnp.zeros(ds_ref.shape, BF16)
    key_ref[...] = jnp.zeros(key_ref.shape, BF16)
    key_index = lax.broadcasted_iota(jnp.int32, (RLEN, columns), 0)
    empty = jnp.zeros((RLEN, columns), BF16)

    def diagonal(pieces):
        rows = [[piece if k == place else empty for place in range(PAIR)] for k, piece in enumerate(pieces)]
        return jnp.concatenate([jnp.concatenate(row, axis=1) for row in rows], axis=0)

    def tiles(ref, starts):
        return jnp.concatenate(
            [ref[pl.ds(start, CLEN), head * HD : (head + 1) * HD] for start in starts for head in range(heads)], axis=0
        )

    def half(ref, child):
        row = ref[pl.ds(roots + child // PAIR, 1)]
        return jnp.where(child % PAIR == 0, row[:, :columns], row[:, columns:])

    places, ready = [], []
    for pair in range(MOST // PAIR + 2):
        if pair < MOST // PAIR:
            picked, starts, keys, values, lse, delta = [], [], [], [], [], []
            for k in range(PAIR):
                target = fork_ref[CH_DEV + pair * PAIR + k]
                child = jnp.minimum(target, CH_DEV - 1)
                fork = fork_ref[child]
                limit = jnp.where(target < CH_DEV, fork & (2 * RLEN - 1), 0)
                row = pl.multiple_of(((fork >> 7) & (ROOTS_DEV - 1)) * RLEN, RLEN)
                starts.append(pl.multiple_of(ROOT_ROWS + child * CLEN, CLEN))
                keys.append(shard_ref[pl.ds(row, RLEN)])
                values.append(shard_ref[pl.ds(row + ROOT_ROWS, RLEN)])
                lse.append(half(lse_ref, child))
                delta.append(half(delta_ref, child))
                key_ref[target] = keys[k]
                picked.append((target, limit, row))
            places += [row for _, _, row in picked]
            query, out = tiles(q_ref, starts), tiles(out_ref, starts)
            scores = dot(jnp.concatenate(keys, axis=0), query, NT)
            weight_grads = dot(jnp.concatenate(values, axis=0), out, NT)
            ready.append((pair, picked, query, out, lse, delta, scores, weight_grads))
            if len(ready) <= 2:
                continue
        done, picked, query, out, lse, delta, scores, weight_grads = ready.pop(0)
        low, score_grads = [], []
        for k, (target, limit, _) in enumerate(picked):
            rows, lanes = slice(k * RLEN, (k + 1) * RLEN), slice(k * columns, (k + 1) * columns)
            weights = jnp.exp2(scores[rows, lanes] * (SCALE * LOG2E) - lse[k])
            weights = jnp.where(key_index < limit, weights, 0.0)
            grads = (weights * (weight_grads[rows, lanes] - delta[k])).astype(BF16)
            ds_ref[target] = grads
            low.append(weights.astype(BF16))
            score_grads.append(grads)
        key_grads = dot(diagonal(score_grads), query, NN) * SCALE
        value_grads = dot(diagonal(low), out, NN)
        for k in range(PAIR):
            rows = slice(k * RLEN, (k + 1) * RLEN)
            grads_ref[done * PAIR + k, 0:RLEN] = key_grads[rows]
            grads_ref[done * PAIR + k, RLEN:] = value_grads[rows]
    sums_ref[...] = jnp.zeros(sums_ref.shape, F32)
    for index, row in enumerate(places):
        sums_ref[pl.ds(row, RLEN)] = sums_ref[pl.ds(row, RLEN)] + grads_ref[index, 0:RLEN]
        at = row + ROOT_ROWS
        sums_ref[pl.ds(at, RLEN)] = sums_ref[pl.ds(at, RLEN)] + grads_ref[index, RLEN:]
    send_ref[...] = sums_ref[...].astype(BF16)


def near_call(forks, shared, shard):
    columns = shared[0].shape[1] // HD * CLEN
    part = 2 * ROOT_ROWS
    return pl.pallas_call(
        near_body,
        in_specs=[SMEM] + [VMEM] * 5,
        out_specs=[VMEM] * 3,
        out_shape=[
            kept((CH_DEV + 1, RLEN, columns), BF16),
            kept((CH_DEV + 1, RLEN, HD), BF16),
            kept((part, HD), BF16),
        ],
        scratch_shapes=[pltpu.VMEM((MOST, 2 * RLEN, HD), F32), pltpu.VMEM((part, HD), F32)],
        compiler_params=params(8),
        cost_estimate=cost("attend_near"),
        name="attend_near",
    )(pinned_scalars(forks), *(pinned(x) for x in (*shared, shard)))


def own_rows(tokens, heads, unit):
    roots, _ = unit_counts(tokens, heads)
    if unit < roots:
        start = unit // (heads // UNIT_HEADS) * BLOCK
        return slice(start, start + BLOCK)
    start = ROOT_ROWS + (unit - roots) * PAIR * CLEN
    return slice(start, start + PAIR * CLEN)


def own_body(q_ref, out_ref, lse_ref, delta_ref, key_ref, value_ref, root_ds_ref, child_ds_ref, keys_out, values_out):
    tokens, heads = q_ref.shape[0], q_ref.shape[1] // HD
    roots, units = unit_counts(tokens, heads)
    per_block = heads // UNIT_HEADS
    key_index = lax.broadcasted_iota(jnp.int32, (BLOCK, UNIT), 0)
    column = lax.broadcasted_iota(jnp.int32, (BLOCK, UNIT), 1)
    root_allowed = key_index <= column % BLOCK
    key_index, column = key_index[: PAIR * CLEN], column[: PAIR * CLEN]
    child_allowed = (key_index // CLEN == column // (heads * CLEN)) & (key_index % CLEN <= column % CLEN)
    totals = [None, None]

    def parts(unit):
        rows = own_rows(tokens, heads, unit)
        return key_ref[rows], value_ref[rows]

    def keep(unit, key_grad, value_grad, score_grads):
        rows = own_rows(tokens, heads, unit)
        if unit >= roots:
            child_ds_ref[unit - roots] = score_grads
            keys_out[rows] = key_grad * SCALE
            values_out[rows] = value_grad
            return
        root_ds_ref[unit] = score_grads
        totals[0] = key_grad if unit % per_block == 0 else totals[0] + key_grad
        totals[1] = value_grad if unit % per_block == 0 else totals[1] + value_grad
        if unit % per_block == per_block - 1:
            keys_out[rows] = totals[0] * SCALE
            values_out[rows] = totals[1]

    swept(
        range(units),
        unit_loader(q_ref, out_ref, lse_ref, delta_ref),
        parts,
        lambda unit, weights: jnp.where(root_allowed if unit < roots else child_allowed, weights, 0.0),
        keep,
        2,
    )


def own_call(shared, keys, values):
    tokens, width = shared[0].shape
    roots, units = unit_counts(tokens, width // HD)
    return pl.pallas_call(
        own_body,
        in_specs=[VMEM] * 6,
        out_specs=[VMEM] * 4,
        out_shape=[
            kept((roots, BLOCK, UNIT), BF16),
            kept((units - roots, PAIR * CLEN, UNIT), BF16),
            kept((tokens, HD), F32),
            kept((tokens, HD), F32),
        ],
        compiler_params=params(8),
        cost_estimate=cost("attend_own"),
        name="attend_own",
    )(*(pinned(x) for x in (*shared, keys, values)))


def query_body(has_back, key_ref, root_ds_ref, child_ds_ref, prompt_ref, prompt_ds_ref, *refs):
    if has_back:
        *parent_refs, sums_ref, back_ref, gq_ref, total_ref, gq_vmem, sems = refs
        total_ref[...] = sums_ref[...] + back_ref[...].astype(F32)
    else:
        *parent_refs, gq_ref, gq_vmem, sems = refs
    tokens, heads = gq_vmem.shape[0], gq_vmem.shape[1] // HD
    roots, units = unit_counts(tokens, heads)
    copies = []

    def store(tiles, total):
        at = 0
        for start, rows, head in tiles:
            piece = total[at : at + rows] * SCALE
            gq_vmem[start : start + rows, head * HD : (head + 1) * HD] = piece.astype(BF16)
            at += rows

    for unit in range(units):
        tiles = unit_tiles(tokens, heads, unit)
        own_ds = root_ds_ref[unit] if unit < roots else child_ds_ref[unit - roots]
        grads = jnp.concatenate([own_ds, prompt_ds_ref[unit]], axis=0)
        total = dot(grads, jnp.concatenate([key_ref[own_rows(tokens, heads, unit)], prompt_ref[...]], axis=0), TN)
        if unit < roots:
            store(tiles, total)
        else:
            columns = heads * CLEN
            for k in range(PAIR):
                child = (unit - roots) * PAIR + k
                grads = jnp.concatenate([ref[child] for ref in parent_refs[1::2]], axis=0)
                keys = jnp.concatenate([ref[child] for ref in parent_refs[0::2]], axis=0)
                store(child_tiles(heads, child), total[k * columns : (k + 1) * columns] + dot(grads, keys, TN))
        done = tiles[-1][0] + tiles[-1][1]
        first = len(copies) * BLOCK
        if done >= first + BLOCK and (unit + 1 >= roots or (unit + 1) % (heads // UNIT_HEADS) == 0):
            rows = slice(first, first + BLOCK)
            copy = pltpu.make_async_copy(gq_vmem.at[rows], gq_ref.at[rows], sems.at[len(copies)])
            copy.start()
            copies.append(copy)
    for copy in copies:
        copy.wait()


def query_call(tokens, width, operands, back=()):
    shapes = [jax.ShapeDtypeStruct((tokens, width), BF16), *(kept(x.shape, F32) for x in back[:1])]
    operands = [*operands, *back]

    def body(*refs):
        query_body(bool(back), *refs)

    return pl.pallas_call(
        body,
        in_specs=[VMEM] * len(operands),
        out_specs=[ANY, *[VMEM] * (len(shapes) - 1)],
        out_shape=shapes,
        scratch_shapes=[pltpu.VMEM((tokens, width), BF16), pltpu.SemaphoreType.DMA((tokens // BLOCK,))],
        compiler_params=params(12),
        cost_estimate=cost("query_grads"),
        name="query_grads",
    )(*(pinned(x) for x in operands))


def finish_body(key_ref, value_ref, *refs):
    parts = refs[:-4]
    keys_out, values_out, prefix_keys_out, prefix_values_out = refs[-4:]
    own = prefix_keys_out.shape[0]
    part = 2 * ROOT_ROWS
    total, prompt = [], []
    for ref in parts:
        rows = ref.shape[0]
        if rows >= part:
            total.append(ref[0:part].astype(F32))
        if rows != part:
            first = rows - 2 * own if rows > part else 0
            prompt.append(ref[first : first + 2 * own].astype(F32))
    total, prompt = sum(total[1:], total[0]), sum(prompt[1:], prompt[0])
    keys_out[0:ROOT_ROWS] = (key_ref[0:ROOT_ROWS] + total[0:ROOT_ROWS]).astype(BF16)
    keys_out[ROOT_ROWS:] = key_ref[ROOT_ROWS:].astype(BF16)
    values_out[0:ROOT_ROWS] = (value_ref[0:ROOT_ROWS] + total[ROOT_ROWS:]).astype(BF16)
    values_out[ROOT_ROWS:] = value_ref[ROOT_ROWS:].astype(BF16)
    prefix_keys_out[...] = prompt[0:own].astype(BF16)
    prefix_values_out[...] = prompt[own:].astype(BF16)


def finish_call(key_sums, value_sums, parts, own):
    shapes = [jax.ShapeDtypeStruct(key_sums.shape, BF16)] * 2 + [jax.ShapeDtypeStruct((own, HD), BF16)] * 2
    return pl.pallas_call(
        finish_body,
        in_specs=[VMEM] * (2 + len(parts)),
        out_specs=[VMEM] * 4,
        out_shape=shapes,
        compiler_params=params(8),
        cost_estimate=cost("finish"),
        name="finish",
    )(*(pinned(x) for x in (key_sums, value_sums, *parts)))


def local(
    grad_out,
    out_weight,
    queries,
    attn_out,
    lse,
    keys,
    values,
    prefix_keys,
    prefix_values,
    fork_owner,
    fork_root,
    fork_offset,
):
    own_part = pack_call(keys, values, prefix_keys, prefix_values)
    forks = [fork_owner.reshape(-1), fork_root, fork_offset]
    own = prefix_keys.shape[0]
    if lax.axis_size("servers") == 4:
        pairs = [[(i, i ^ d) for i in range(4)] for d in range(4)]
        part_two = lax.ppermute(own_part, "servers", pairs[3])
        later_part, later_prompt = repeat_call(own_part)
        part_one = lax.ppermute(later_part, "servers", pairs[1])
        prompt_far = lax.ppermute(later_prompt, "servers", pairs[2])
        out_grad, lse_rows, delta, forks = out_grad_call(grad_out, out_weight, attn_out, lse, *forks)
        part_two, delta = lax.optimization_barrier((part_two, delta))
        part_far = lax.ppermute(part_two[: 2 * ROOT_ROWS], "servers", pairs[1])
        part, whole = (2 * ROOT_ROWS, HD), (2 * ROOT_ROWS + 2 * own, HD)
        near_ds, near_keys, send_two = near_call(forks, (queries, out_grad, lse_rows, delta), part_two)
        back_two = lax.ppermute(send_two, "servers", pairs[3])
        delta, near_ds = lax.optimization_barrier((delta, near_ds))
        prompt_ds, prompt_keys, prompt_sums, send_two_prompt = prompt_call(
            (queries, out_grad, lse_rows, delta), [own_part, part_one, prompt_far, part_two], 2 * own, True
        )
        far_ds, far_keys, own_sums, send_far, send_one = parent_call(
            forks,
            (queries, out_grad, lse_rows, delta),
            [own_part, part_far, part_one],
            (0, 2, 1),
            [kept(part, F32), kept(whole, BF16), kept(whole, BF16)],
            prompt_sums,
            "attend_far",
        )
        back_far = lax.ppermute(send_far, "servers", pairs[2])
        back_one = lax.ppermute(send_one, "servers", pairs[1])
        back_two_prompt = lax.ppermute(send_two_prompt, "servers", pairs[3])
        delta, far_ds = lax.optimization_barrier((delta, far_ds))
        shared = (queries, out_grad, lse_rows, delta)
        parents = (near_keys, near_ds, far_keys, far_ds)
        back = (own_sums, back_two)
        parts = [prompt_sums, back_far, back_one, back_two_prompt]
    else:
        count = lax.axis_size("servers")
        all_parts = lax.all_gather(own_part, "servers", axis=0, tiled=False)
        part = 2 * ROOT_ROWS
        all_roots = all_parts[:, :part].reshape(-1, HD)
        all_prompts = all_parts[:, part:].reshape(-1, HD)
        out_grad, lse_rows, delta, forks = out_grad_call(grad_out, out_weight, attn_out, lse, *forks)
        shared = (queries, out_grad, lse_rows, delta)
        prompt_ds, prompt_keys, prompt_sums = prompt_call(shared, [all_prompts], 2 * own, False)
        parent_ds, parent_keys, root_sums = parent_call(forks, shared, [all_roots])
        parents = (parent_keys, parent_ds)
        sends = jnp.concatenate(
            [root_sums.reshape(count, part, HD), prompt_sums.reshape(count, 2 * own, HD)], axis=1
        ).reshape(-1, HD)
        back = ()
        parts = [lax.psum_scatter(sends, "servers", scatter_dimension=0, tiled=True)]
    root_ds, child_ds, key_sums, value_sums = own_call(shared, keys, values)
    operands = (keys, root_ds, child_ds, prompt_keys, prompt_ds, *parents)
    grad_queries, *totals = query_call(*queries.shape, operands, back)
    parts = totals + parts
    grads = finish_call(key_sums, value_sums, parts, own)
    return (grad_queries, *grads)


def solution(mesh):
    placed = (
        P(("groups", "servers"), None),
        P(None, "heads"),
        P(("groups", "servers"), "heads"),
        P(("groups", "servers"), "heads"),
        P("heads", ("groups", "servers")),
        P(("groups", "servers"), "heads"),
        P(("groups", "servers"), "heads"),
        P(("groups", "servers"), "heads"),
        P(("groups", "servers"), "heads"),
        P("groups", None),
        P("groups"),
        P("groups"),
    )
    return jax.shard_map(
        local,
        mesh=mesh,
        in_specs=placed,
        out_specs=(P(("groups", "servers"), "heads"),) * 5,
        check_vma=False,
    )
```

```python
import math

import jax
import jax.numpy as jnp
from jax import lax
from jax.experimental import pallas as pl
from jax.experimental.pallas import tpu as pltpu
from jax.sharding import PartitionSpec as P

HD = 128
CH_DEV = 16
ROOTS_DEV = 4
RLEN = 64
CLEN = 16
MOST = 8
ROOT_ROWS = ROOTS_DEV * RLEN
BLOCK = 64
UNIT = 256
UNIT_HEADS = UNIT // BLOCK
PAIR = 2
SCALE = HD ** (-0.5)
LOG2E = math.log2(math.e)
NT = (((1,), (1,)), ((), ()))
NN = (((1,), (0,)), ((), ()))
TN = (((0,), (0,)), ((), ()))
F32 = jnp.float32
BF16 = jnp.bfloat16
VMEM = pl.BlockSpec(memory_space=pltpu.VMEM)
SMEM = pl.BlockSpec(memory_space=pltpu.SMEM)
ANY = pl.BlockSpec(memory_space=pl.ANY)


def params(mib):
    return pltpu.CompilerParams(vmem_limit_bytes=mib * 1024 * 1024)


COSTS = {
    "pack": 8,
    "repeat": 8,
    "out_grad": 6,
    "attend_near": 3,
    "attend_parent": 3,
    "attend_prompt": 0.1,
    "attend_far": 0.1,
    "attend_own": 0.1,
    "query_grads": 0.3,
    "finish": 0.01,
}


def cost(name):
    micros = COSTS[name]
    return pl.CostEstimate(flops=int(micros * (1 << 30)), transcendentals=0, bytes_accessed=1 << 16)


def pinned(array):
    return pltpu.with_memory_space_constraint(array, pltpu.VMEM)


def unmoved(array):
    return pltpu.with_memory_space_constraint(array, pltpu.HBM)


def pinned_scalars(array):
    return pltpu.with_memory_space_constraint(array, pltpu.SMEM)


def kept(shape, dtype):
    return pltpu.VMEM(shape, dtype)


def dot(left, right, numbers):
    return lax.dot_general(left, right, numbers, preferred_element_type=F32)


def pack_body(key_ref, value_ref, prefix_key_ref, prefix_value_ref, part_ref, sems):
    own = prefix_key_ref.shape[0]
    at = 2 * ROOT_ROWS
    copies = [
        (key_ref.at[0:ROOT_ROWS], part_ref.at[0:ROOT_ROWS]),
        (value_ref.at[0:ROOT_ROWS], part_ref.at[ROOT_ROWS:at]),
        (prefix_key_ref, part_ref.at[at : at + own]),
        (prefix_value_ref, part_ref.at[at + own : at + 2 * own]),
    ]
    started = [pltpu.make_async_copy(a, b, sems.at[i]) for i, (a, b) in enumerate(copies)]
    for copy in started:
        copy.start()
    for copy in started:
        copy.wait()


def pack_call(keys, values, prefix_keys, prefix_values):
    own = prefix_keys.shape[0]
    return pl.pallas_call(
        pack_body,
        in_specs=[ANY] * 4,
        out_specs=VMEM,
        out_shape=kept((2 * ROOT_ROWS + 2 * own, HD), BF16),
        scratch_shapes=[pltpu.SemaphoreType.DMA((4,))],
        compiler_params=params(4),
        cost_estimate=cost("pack"),
        name="pack",
    )(*(unmoved(x) for x in (keys, values, prefix_keys, prefix_values)))


def repeat_body(part_ref, part_out, prompt_out):
    part_out[...] = part_ref[...]
    prompt_out[...] = part_ref[2 * ROOT_ROWS :]


def repeat_call(part):
    return pl.pallas_call(
        repeat_body,
        in_specs=[VMEM],
        out_specs=[VMEM] * 2,
        out_shape=[kept(part.shape, BF16), kept((part.shape[0] - 2 * ROOT_ROWS, HD), BF16)],
        compiler_params=params(4),
        cost_estimate=cost("repeat"),
        name="repeat",
    )(pinned(part))


def unit_rows(array):
    heads, tokens = array.shape
    rows = []
    for start in range(0, ROOT_ROWS, BLOCK):
        for first in range(0, heads, UNIT_HEADS):
            picked = range(first, first + UNIT_HEADS)
            rows.append([array[head : head + 1, start : start + BLOCK] for head in picked])
    for start in range(ROOT_ROWS, tokens, PAIR * CLEN):
        starts = range(start, start + PAIR * CLEN, CLEN)
        rows.append([array[head : head + 1, at : at + CLEN] for at in starts for head in range(heads)])
    return [jnp.concatenate(row, axis=1) for row in rows]


def out_grad_body(
    grad_ref, weight_ref, attn_ref, lse_ref, owner_ref, root_ref, offset_ref, out_ref, lse_out, delta_out, forks_out
):
    rows, cols = out_ref.shape
    width = 2 * HD
    lane = lax.broadcasted_iota(jnp.int32, (rows, HD), 1)
    columns = jnp.zeros((rows, HD), F32)
    my_index = lax.axis_index("servers")
    for child in range(CH_DEV + 1):
        forks_out[CH_DEV + child] = CH_DEV
    found = jnp.int32(0)
    for child in range(CH_DEV):
        at = my_index * CH_DEV + child
        owner = owner_ref[at]
        forks_out[child] = (owner * ROOTS_DEV + root_ref[at]) * (2 * RLEN) + offset_ref[at]
        forks_out[CH_DEV + found] = child
        found = found + jnp.where((owner ^ my_index) == 3, 1, 0)
    forks_out[CH_DEV + found] = CH_DEV
    for unit, row in enumerate(unit_rows(lse_ref[...] * LOG2E)):
        lse_out[unit : unit + 1] = row
    for step in range(cols // width):
        part = slice(step * width, (step + 1) * width)
        wide = jnp.dot(grad_ref[...], weight_ref[:, part], preferred_element_type=F32).astype(BF16)
        out_ref[:, part] = wide
        products = wide.astype(F32) * attn_ref[:, part].astype(F32)
        for head in range(width // HD):
            total = jnp.sum(products[:, head * HD : (head + 1) * HD], axis=1, keepdims=True)
            columns = jnp.where(lane == step * (width // HD) + head, total, columns)
    for unit, row in enumerate(unit_rows(jnp.transpose(columns)[: cols // HD])):
        delta_out[unit : unit + 1] = row


def out_grad_call(grad_out, out_weight, attn_out, lse, *forks):
    rows = grad_out.shape[0]
    cols = out_weight.shape[1]
    units = rows * (cols // HD) // UNIT
    return pl.pallas_call(
        out_grad_body,
        in_specs=[VMEM] * 4 + [SMEM] * 3,
        out_specs=[VMEM] * 3 + [SMEM],
        out_shape=[
            kept((rows, cols), BF16),
            kept((units, UNIT), F32),
            kept((units, UNIT), F32),
            pltpu.SMEM((2 * CH_DEV + 1,), jnp.int32),
        ],
        compiler_params=params(12),
        cost_estimate=cost("out_grad"),
        name="out_grad",
    )(*(pinned(x) for x in (grad_out, out_weight, attn_out, lse)), *forks)


def unit_counts(tokens, heads):
    roots = ROOT_ROWS * heads // UNIT
    return roots, roots + (tokens - ROOT_ROWS) * heads // UNIT


def unit_tiles(tokens, heads, unit):
    roots, _ = unit_counts(tokens, heads)
    if unit < roots:
        block, part = divmod(unit, heads // UNIT_HEADS)
        picked = range(part * UNIT_HEADS, (part + 1) * UNIT_HEADS)
        return [(block * BLOCK, BLOCK, head) for head in picked]
    return [tile for k in range(PAIR) for tile in child_tiles(heads, (unit - roots) * PAIR + k)]


def child_tiles(heads, child):
    return [(ROOT_ROWS + child * CLEN, CLEN, head) for head in range(heads)]


def tiled(ref, tiles):
    return jnp.concatenate(
        [ref[start : start + rows, head * HD : (head + 1) * HD] for start, rows, head in tiles], axis=0
    )


def swept(jobs, load, parts, mask, keep, ahead=1):
    ready = []
    for job in [*jobs, *[None] * ahead]:
        if job is not None:
            query, out, lse, delta = load(job)
            keys, values = parts(job)
            ready.append((job, query, out, lse, delta, dot(keys, query, NT), dot(values, out, NT)))
        if job is not None and len(ready) <= ahead:
            continue
        done, query, out, lse, delta, scores, weight_grads = ready.pop(0)
        weights = mask(done, jnp.exp2(scores * (SCALE * LOG2E) - lse))
        score_grads = (weights * (weight_grads - delta)).astype(BF16)
        keep(done, dot(score_grads, query, NN), dot(weights.astype(BF16), out, NN), score_grads)


def unit_loader(q_ref, out_ref, lse_ref, delta_ref):
    tokens, heads = q_ref.shape[0], q_ref.shape[1] // HD

    def load(unit):
        tiles = unit_tiles(tokens, heads, unit)
        row = slice(unit, unit + 1)
        return tiled(q_ref, tiles), tiled(out_ref, tiles), lse_ref[row], delta_ref[row]

    return load


def child_loader(q_ref, out_ref, lse_ref, delta_ref):
    tokens, heads = q_ref.shape[0], q_ref.shape[1] // HD
    roots, _ = unit_counts(tokens, heads)

    def load(child):
        tiles = child_tiles(heads, child)
        unit, place = roots + child // PAIR, child % PAIR * heads * CLEN
        row, lanes = slice(unit, unit + 1), slice(place, place + heads * CLEN)
        return tiled(q_ref, tiles), tiled(out_ref, tiles), lse_ref[row, lanes], delta_ref[row, lanes]

    return load


def prompt_body(piece_rows, is_part, q_ref, out_ref, lse_ref, delta_ref, *refs):
    value_ref = refs[-1]
    if is_part:
        *pieces, ds_ref, key_ref, sums_ref, two_ref = refs[:-1]
    else:
        *pieces, ds_ref, key_ref, sums_ref = refs[:-1]
    own = piece_rows // 2
    count = 0
    for piece in pieces:
        first = 2 * ROOT_ROWS if is_part and piece.shape[0] > piece_rows else 0
        for at in range(first, piece.shape[0], piece_rows):
            key_ref[count : count + own] = piece[at : at + own]
            value_ref[count : count + own] = piece[at + own : at + piece_rows]
            count += own
    sums = [jnp.zeros((count, HD), F32), jnp.zeros((count, HD), F32)]

    def keep(unit, key_grad, value_grad, score_grads):
        ds_ref[unit] = score_grads
        sums[0] = sums[0] + key_grad
        sums[1] = sums[1] + value_grad

    swept(
        range(ds_ref.shape[0]),
        unit_loader(q_ref, out_ref, lse_ref, delta_ref),
        lambda unit: (key_ref[...], value_ref[...]),
        lambda unit, weights: weights,
        keep,
        2,
    )

    def store(ref, at, index):
        rows = slice(index * own, (index + 1) * own)
        ref[at : at + own] = (sums[0][rows] * SCALE).astype(ref.dtype)
        ref[at + own : at + piece_rows] = sums[1][rows].astype(ref.dtype)

    for index in range(count // own):
        store(sums_ref, index * piece_rows, index)
    if is_part:
        store(two_ref, 0, 3)


def prompt_call(shared, pieces, piece_rows, is_part):
    count = lax.axis_size("servers") * piece_rows // 2
    units = shared[2].shape[0]
    operands = [*shared, *pieces]
    shapes = [
        kept((units, count, UNIT), BF16),
        kept((count, HD), BF16),
        kept((2 * count, HD), F32),
    ]
    if is_part:
        shapes.append(kept((piece_rows, HD), BF16))

    def body(*refs):
        prompt_body(piece_rows, is_part, *refs)

    return pl.pallas_call(
        body,
        in_specs=[VMEM] * len(operands),
        out_specs=[VMEM] * len(shapes),
        out_shape=shapes,
        scratch_shapes=[pltpu.VMEM((count, HD), BF16)],
        compiler_params=params(12 if is_part else 20),
        cost_estimate=cost("attend_prompt"),
        name="attend_prompt",
    )(*(pinned(x) for x in operands))


def parent_body(held, has_prompt, fork_ref, q_ref, out_ref, lse_ref, delta_ref, *refs):
    is_part = held is not None
    count = len(held) if is_part else 1
    shards, refs = refs[:count], refs[count:]
    if has_prompt:
        prompt_ref, refs = refs[0], refs[1:]
    ds_ref, key_ref, *sum_refs = refs[:-2]
    grads_ref, sums_ref = refs[-2:]
    heads = q_ref.shape[1] // HD
    part = 2 * ROOT_ROWS
    my_index = lax.axis_index("servers")
    bases, limits = {}, {}

    def parts(child):
        fork = fork_ref[child]
        limit = fork & (2 * RLEN - 1)
        row = pl.multiple_of(((fork >> 7) & (ROOTS_DEV - 1)) * RLEN, RLEN)
        owner = fork >> 9
        if is_part:
            slot = owner ^ my_index
            at = row + ROOT_ROWS
            keys, values = shards[0][pl.ds(row, RLEN)], shards[0][pl.ds(at, RLEN)]
            place, inside = 0, slot == held[0]
            for index in range(1, count):
                here = slot == held[index]
                place, inside = jnp.where(here, index, place), inside | here
                keys = jnp.where(here, shards[index][pl.ds(row, RLEN)], keys)
                values = jnp.where(here, shards[index][pl.ds(at, RLEN)], values)
            bases[child] = pl.multiple_of(place * part + row, RLEN)
            limits[child] = jnp.where(inside, limit, 0)
        else:
            bases[child] = pl.multiple_of(owner * part + row, RLEN)
            limits[child] = limit
            keys = shards[0][pl.ds(bases[child], RLEN)]
            values = shards[0][pl.ds(bases[child] + ROOT_ROWS, RLEN)]
        key_ref[child] = keys
        return keys, values

    key_index = lax.broadcasted_iota(jnp.int32, (RLEN, heads * CLEN), 0)

    columns = heads * CLEN
    load = unit_loader(q_ref, out_ref, lse_ref, delta_ref)
    roots, _ = unit_counts(q_ref.shape[0], heads)
    empty = jnp.zeros((RLEN, columns), BF16)

    def diagonal(pieces):
        rows = [[piece if k == place else empty for place in range(PAIR)] for k, piece in enumerate(pieces)]
        return jnp.concatenate([jnp.concatenate(row, axis=1) for row in rows], axis=0)

    ready = []
    for pair in range(CH_DEV // PAIR + 3):
        if pair < CH_DEV // PAIR:
            query, out, lse, delta = load(roots + pair)
            held_parts = [parts(pair * PAIR + k) for k in range(PAIR)]
            scores = dot(jnp.concatenate([keys for keys, _ in held_parts], axis=0), query, NT)
            weight_grads = dot(jnp.concatenate([values for _, values in held_parts], axis=0), out, NT)
            ready.append((pair, query, out, lse, delta, scores, weight_grads))
            if len(ready) <= 3:
                continue
        done, query, out, lse, delta, scores, weight_grads = ready.pop(0)
        low, score_grads = [], []
        for k in range(PAIR):
            child = done * PAIR + k
            rows, lanes = slice(k * RLEN, (k + 1) * RLEN), slice(k * columns, (k + 1) * columns)
            weights = jnp.exp2(scores[rows, lanes] * (SCALE * LOG2E) - lse[:, lanes])
            weights = jnp.where(key_index < limits[child], weights, 0.0)
            grads = (weights * (weight_grads[rows, lanes] - delta[:, lanes])).astype(BF16)
            ds_ref[child] = grads
            low.append(weights.astype(BF16))
            score_grads.append(grads)
        key_grads = dot(diagonal(score_grads), query, NN) * SCALE
        value_grads = dot(diagonal(low), out, NN)
        for k in range(PAIR):
            child, rows = done * PAIR + k, slice(k * RLEN, (k + 1) * RLEN)
            grads_ref[child, 0:RLEN] = key_grads[rows]
            grads_ref[child, RLEN:] = value_grads[rows]
    sums_ref[...] = jnp.zeros(sums_ref.shape, F32)
    for child in range(CH_DEV):
        base = bases[child]
        sums_ref[pl.ds(base, RLEN)] = sums_ref[pl.ds(base, RLEN)] + grads_ref[child, 0:RLEN]
        base = base + ROOT_ROWS
        sums_ref[pl.ds(base, RLEN)] = sums_ref[pl.ds(base, RLEN)] + grads_ref[child, RLEN:]
    for index, ref in enumerate(sum_refs):
        first = index * part
        size = part if is_part else ref.shape[0]
        ref[0:size] = sums_ref[first : first + size].astype(ref.dtype)
        if is_part and ref.shape[0] > part:
            rows = ref.shape[0] - part
            first = held[index] * rows
            ref[part:] = prompt_ref[first : first + rows].astype(ref.dtype)


def parent_call(forks, shared, shards, held=None, sums=(), prompt_sums=None, name="attend_parent"):
    is_part = held is not None
    rows = 2 * ROOT_ROWS * len(shards) if is_part else shards[0].shape[0]
    columns = shared[0].shape[1] // HD * CLEN
    shapes = [kept((CH_DEV, RLEN, columns), BF16), kept((CH_DEV, RLEN, HD), BF16)]
    operands = [*shared, *shards]
    if is_part:
        shapes += sums
        if prompt_sums is not None:
            operands.append(prompt_sums)
    else:
        shapes.append(jax.ShapeDtypeStruct((rows, HD), F32))

    def body(*refs):
        parent_body(held, prompt_sums is not None, *refs)

    return pl.pallas_call(
        body,
        in_specs=[SMEM] + [VMEM] * len(operands),
        out_specs=[VMEM] * len(shapes),
        out_shape=shapes,
        scratch_shapes=[
            pltpu.VMEM((CH_DEV, 2 * RLEN, HD), F32),
            pltpu.VMEM((rows, HD), F32),
        ],
        compiler_params=params(8 if is_part else 40),
        cost_estimate=cost(name),
        name=name,
    )(pinned_scalars(forks), *(pinned(x) for x in operands))


def near_body(fork_ref, q_ref, out_ref, lse_ref, delta_ref, shard_ref, ds_ref, key_ref, send_ref, grads_ref, sums_ref):
    tokens, heads = q_ref.shape[0], q_ref.shape[1] // HD
    columns = heads * CLEN
    roots, _ = unit_counts(tokens, heads)
    ds_ref[...] = jnp.zeros(ds_ref.shape, BF16)
    key_ref[...] = jnp.zeros(key_ref.shape, BF16)
    key_index = lax.broadcasted_iota(jnp.int32, (RLEN, columns), 0)
    empty = jnp.zeros((RLEN, columns), BF16)

    def diagonal(pieces):
        rows = [[piece if k == place else empty for place in range(PAIR)] for k, piece in enumerate(pieces)]
        return jnp.concatenate([jnp.concatenate(row, axis=1) for row in rows], axis=0)

    def tiles(ref, starts):
        return jnp.concatenate(
            [ref[pl.ds(start, CLEN), head * HD : (head + 1) * HD] for start in starts for head in range(heads)], axis=0
        )

    def half(ref, child):
        row = ref[pl.ds(roots + child // PAIR, 1)]
        return jnp.where(child % PAIR == 0, row[:, :columns], row[:, columns:])

    places, ready = [], []
    for pair in range(MOST // PAIR + 2):
        if pair < MOST // PAIR:
            picked, starts, keys, values, lse, delta = [], [], [], [], [], []
            for k in range(PAIR):
                target = fork_ref[CH_DEV + pair * PAIR + k]
                child = jnp.minimum(target, CH_DEV - 1)
                fork = fork_ref[child]
                limit = jnp.where(target < CH_DEV, fork & (2 * RLEN - 1), 0)
                row = pl.multiple_of(((fork >> 7) & (ROOTS_DEV - 1)) * RLEN, RLEN)
                starts.append(pl.multiple_of(ROOT_ROWS + child * CLEN, CLEN))
                keys.append(shard_ref[pl.ds(row, RLEN)])
                values.append(shard_ref[pl.ds(row + ROOT_ROWS, RLEN)])
                lse.append(half(lse_ref, child))
                delta.append(half(delta_ref, child))
                key_ref[target] = keys[k]
                picked.append((target, limit, row))
            places += [row for _, _, row in picked]
            query, out = tiles(q_ref, starts), tiles(out_ref, starts)
            scores = dot(jnp.concatenate(keys, axis=0), query, NT)
            weight_grads = dot(jnp.concatenate(values, axis=0), out, NT)
            ready.append((pair, picked, query, out, lse, delta, scores, weight_grads))
            if len(ready) <= 2:
                continue
        done, picked, query, out, lse, delta, scores, weight_grads = ready.pop(0)
        low, score_grads = [], []
        for k, (target, limit, _) in enumerate(picked):
            rows, lanes = slice(k * RLEN, (k + 1) * RLEN), slice(k * columns, (k + 1) * columns)
            weights = jnp.exp2(scores[rows, lanes] * (SCALE * LOG2E) - lse[k])
            weights = jnp.where(key_index < limit, weights, 0.0)
            grads = (weights * (weight_grads[rows, lanes] - delta[k])).astype(BF16)
            ds_ref[target] = grads
            low.append(weights.astype(BF16))
            score_grads.append(grads)
        key_grads = dot(diagonal(score_grads), query, NN) * SCALE
        value_grads = dot(diagonal(low), out, NN)
        for k in range(PAIR):
            rows = slice(k * RLEN, (k + 1) * RLEN)
            grads_ref[done * PAIR + k, 0:RLEN] = key_grads[rows]
            grads_ref[done * PAIR + k, RLEN:] = value_grads[rows]
    sums_ref[...] = jnp.zeros(sums_ref.shape, F32)
    for index, row in enumerate(places):
        sums_ref[pl.ds(row, RLEN)] = sums_ref[pl.ds(row, RLEN)] + grads_ref[index, 0:RLEN]
        at = row + ROOT_ROWS
        sums_ref[pl.ds(at, RLEN)] = sums_ref[pl.ds(at, RLEN)] + grads_ref[index, RLEN:]
    send_ref[...] = sums_ref[...].astype(BF16)


def near_call(forks, shared, shard):
    columns = shared[0].shape[1] // HD * CLEN
    part = 2 * ROOT_ROWS
    return pl.pallas_call(
        near_body,
        in_specs=[SMEM] + [VMEM] * 5,
        out_specs=[VMEM] * 3,
        out_shape=[
            kept((CH_DEV + 1, RLEN, columns), BF16),
            kept((CH_DEV + 1, RLEN, HD), BF16),
            kept((part, HD), BF16),
        ],
        scratch_shapes=[pltpu.VMEM((MOST, 2 * RLEN, HD), F32), pltpu.VMEM((part, HD), F32)],
        compiler_params=params(8),
        cost_estimate=cost("attend_near"),
        name="attend_near",
    )(pinned_scalars(forks), *(pinned(x) for x in (*shared, shard)))


def own_rows(tokens, heads, unit):
    roots, _ = unit_counts(tokens, heads)
    if unit < roots:
        start = unit // (heads // UNIT_HEADS) * BLOCK
        return slice(start, start + BLOCK)
    start = ROOT_ROWS + (unit - roots) * PAIR * CLEN
    return slice(start, start + PAIR * CLEN)


def own_body(q_ref, out_ref, lse_ref, delta_ref, key_ref, value_ref, root_ds_ref, child_ds_ref, keys_out, values_out):
    tokens, heads = q_ref.shape[0], q_ref.shape[1] // HD
    roots, units = unit_counts(tokens, heads)
    per_block = heads // UNIT_HEADS
    key_index = lax.broadcasted_iota(jnp.int32, (BLOCK, UNIT), 0)
    column = lax.broadcasted_iota(jnp.int32, (BLOCK, UNIT), 1)
    root_allowed = key_index <= column % BLOCK
    key_index, column = key_index[: PAIR * CLEN], column[: PAIR * CLEN]
    child_allowed = (key_index // CLEN == column // (heads * CLEN)) & (key_index % CLEN <= column % CLEN)
    totals = [None, None]

    def parts(unit):
        rows = own_rows(tokens, heads, unit)
        return key_ref[rows], value_ref[rows]

    def keep(unit, key_grad, value_grad, score_grads):
        rows = own_rows(tokens, heads, unit)
        if unit >= roots:
            child_ds_ref[unit - roots] = score_grads
            keys_out[rows] = key_grad * SCALE
            values_out[rows] = value_grad
            return
        root_ds_ref[unit] = score_grads
        totals[0] = key_grad if unit % per_block == 0 else totals[0] + key_grad
        totals[1] = value_grad if unit % per_block == 0 else totals[1] + value_grad
        if unit % per_block == per_block - 1:
            keys_out[rows] = totals[0] * SCALE
            values_out[rows] = totals[1]

    swept(
        range(units),
        unit_loader(q_ref, out_ref, lse_ref, delta_ref),
        parts,
        lambda unit, weights: jnp.where(root_allowed if unit < roots else child_allowed, weights, 0.0),
        keep,
    )


def own_call(shared, keys, values):
    tokens, width = shared[0].shape
    roots, units = unit_counts(tokens, width // HD)
    return pl.pallas_call(
        own_body,
        in_specs=[VMEM] * 6,
        out_specs=[VMEM] * 4,
        out_shape=[
            kept((roots, BLOCK, UNIT), BF16),
            kept((units - roots, PAIR * CLEN, UNIT), BF16),
            kept((tokens, HD), F32),
            kept((tokens, HD), F32),
        ],
        compiler_params=params(8),
        cost_estimate=cost("attend_own"),
        name="attend_own",
    )(*(pinned(x) for x in (*shared, keys, values)))


def query_body(has_back, key_ref, root_ds_ref, child_ds_ref, prompt_ref, prompt_ds_ref, *refs):
    if has_back:
        *parent_refs, sums_ref, back_ref, gq_ref, total_ref, gq_vmem, sems = refs
        total_ref[...] = sums_ref[...] + back_ref[...].astype(F32)
    else:
        *parent_refs, gq_ref, gq_vmem, sems = refs
    tokens, heads = gq_vmem.shape[0], gq_vmem.shape[1] // HD
    roots, units = unit_counts(tokens, heads)
    copies = []

    def store(tiles, total):
        at = 0
        for start, rows, head in tiles:
            piece = total[at : at + rows] * SCALE
            gq_vmem[start : start + rows, head * HD : (head + 1) * HD] = piece.astype(BF16)
            at += rows

    for unit in range(units):
        tiles = unit_tiles(tokens, heads, unit)
        own_ds = root_ds_ref[unit] if unit < roots else child_ds_ref[unit - roots]
        grads = jnp.concatenate([own_ds, prompt_ds_ref[unit]], axis=0)
        total = dot(grads, jnp.concatenate([key_ref[own_rows(tokens, heads, unit)], prompt_ref[...]], axis=0), TN)
        if unit < roots:
            store(tiles, total)
        else:
            columns = heads * CLEN
            for k in range(PAIR):
                child = (unit - roots) * PAIR + k
                grads = jnp.concatenate([ref[child] for ref in parent_refs[1::2]], axis=0)
                keys = jnp.concatenate([ref[child] for ref in parent_refs[0::2]], axis=0)
                store(child_tiles(heads, child), total[k * columns : (k + 1) * columns] + dot(grads, keys, TN))
        done = tiles[-1][0] + tiles[-1][1]
        first = len(copies) * BLOCK
        if done >= first + BLOCK and (unit + 1 >= roots or (unit + 1) % (heads // UNIT_HEADS) == 0):
            rows = slice(first, first + BLOCK)
            copy = pltpu.make_async_copy(gq_vmem.at[rows], gq_ref.at[rows], sems.at[len(copies)])
            copy.start()
            copies.append(copy)
    for copy in copies:
        copy.wait()


def query_call(tokens, width, operands, back=()):
    shapes = [jax.ShapeDtypeStruct((tokens, width), BF16), *(kept(x.shape, F32) for x in back[:1])]
    operands = [*operands, *back]

    def body(*refs):
        query_body(bool(back), *refs)

    return pl.pallas_call(
        body,
        in_specs=[VMEM] * len(operands),
        out_specs=[ANY, *[VMEM] * (len(shapes) - 1)],
        out_shape=shapes,
        scratch_shapes=[pltpu.VMEM((tokens, width), BF16), pltpu.SemaphoreType.DMA((tokens // BLOCK,))],
        compiler_params=params(12),
        cost_estimate=cost("query_grads"),
        name="query_grads",
    )(*(pinned(x) for x in operands))


def finish_body(key_ref, value_ref, *refs):
    parts = refs[:-4]
    keys_out, values_out, prefix_keys_out, prefix_values_out = refs[-4:]
    own = prefix_keys_out.shape[0]
    part = 2 * ROOT_ROWS
    total, prompt = [], []
    for ref in parts:
        rows = ref.shape[0]
        if rows >= part:
            total.append(ref[0:part].astype(F32))
        if rows != part:
            first = rows - 2 * own if rows > part else 0
            prompt.append(ref[first : first + 2 * own].astype(F32))
    total, prompt = sum(total[1:], total[0]), sum(prompt[1:], prompt[0])
    keys_out[0:ROOT_ROWS] = (key_ref[0:ROOT_ROWS] + total[0:ROOT_ROWS]).astype(BF16)
    keys_out[ROOT_ROWS:] = key_ref[ROOT_ROWS:].astype(BF16)
    values_out[0:ROOT_ROWS] = (value_ref[0:ROOT_ROWS] + total[ROOT_ROWS:]).astype(BF16)
    values_out[ROOT_ROWS:] = value_ref[ROOT_ROWS:].astype(BF16)
    prefix_keys_out[...] = prompt[0:own].astype(BF16)
    prefix_values_out[...] = prompt[own:].astype(BF16)


def finish_call(key_sums, value_sums, parts, own):
    shapes = [jax.ShapeDtypeStruct(key_sums.shape, BF16)] * 2 + [jax.ShapeDtypeStruct((own, HD), BF16)] * 2
    return pl.pallas_call(
        finish_body,
        in_specs=[VMEM] * (2 + len(parts)),
        out_specs=[VMEM] * 4,
        out_shape=shapes,
        compiler_params=params(8),
        cost_estimate=cost("finish"),
        name="finish",
    )(*(pinned(x) for x in (key_sums, value_sums, *parts)))


def local(
    grad_out,
    out_weight,
    queries,
    attn_out,
    lse,
    keys,
    values,
    prefix_keys,
    prefix_values,
    fork_owner,
    fork_root,
    fork_offset,
):
    own_part = pack_call(keys, values, prefix_keys, prefix_values)
    forks = [fork_owner.reshape(-1), fork_root, fork_offset]
    own = prefix_keys.shape[0]
    if lax.axis_size("servers") == 4:
        pairs = [[(i, i ^ d) for i in range(4)] for d in range(4)]
        part_two = lax.ppermute(own_part, "servers", pairs[3])
        later_part, later_prompt = repeat_call(own_part)
        prompt_far = lax.ppermute(later_prompt, "servers", pairs[2])
        part_one = lax.ppermute(later_part, "servers", pairs[1])
        out_grad, lse_rows, delta, forks = out_grad_call(grad_out, out_weight, attn_out, lse, *forks)
        part_two, delta = lax.optimization_barrier((part_two, delta))
        part_far = lax.ppermute(part_two[: 2 * ROOT_ROWS], "servers", pairs[1])
        part, whole = (2 * ROOT_ROWS, HD), (2 * ROOT_ROWS + 2 * own, HD)
        near_ds, near_keys, send_two = near_call(forks, (queries, out_grad, lse_rows, delta), part_two)
        back_two = lax.ppermute(send_two, "servers", pairs[3])
        delta, near_ds = lax.optimization_barrier((delta, near_ds))
        prompt_ds, prompt_keys, prompt_sums, send_two_prompt = prompt_call(
            (queries, out_grad, lse_rows, delta), [own_part, part_one, prompt_far, part_two], 2 * own, True
        )
        far_ds, far_keys, own_sums, send_far, send_one = parent_call(
            forks,
            (queries, out_grad, lse_rows, delta),
            [own_part, part_far, part_one],
            (0, 2, 1),
            [kept(part, F32), kept(whole, BF16), kept(whole, BF16)],
            prompt_sums,
            "attend_far",
        )
        back_far = lax.ppermute(send_far, "servers", pairs[2])
        back_one = lax.ppermute(send_one, "servers", pairs[1])
        back_two_prompt = lax.ppermute(send_two_prompt, "servers", pairs[3])
        delta, far_ds = lax.optimization_barrier((delta, far_ds))
        shared = (queries, out_grad, lse_rows, delta)
        parents = (near_keys, near_ds, far_keys, far_ds)
        back = (own_sums, back_two)
        parts = [prompt_sums, back_far, back_one, back_two_prompt]
    else:
        count = lax.axis_size("servers")
        all_parts = lax.all_gather(own_part, "servers", axis=0, tiled=False)
        part = 2 * ROOT_ROWS
        all_roots = all_parts[:, :part].reshape(-1, HD)
        all_prompts = all_parts[:, part:].reshape(-1, HD)
        out_grad, lse_rows, delta, forks = out_grad_call(grad_out, out_weight, attn_out, lse, *forks)
        shared = (queries, out_grad, lse_rows, delta)
        prompt_ds, prompt_keys, prompt_sums = prompt_call(shared, [all_prompts], 2 * own, False)
        parent_ds, parent_keys, root_sums = parent_call(forks, shared, [all_roots])
        parents = (parent_keys, parent_ds)
        sends = jnp.concatenate(
            [root_sums.reshape(count, part, HD), prompt_sums.reshape(count, 2 * own, HD)], axis=1
        ).reshape(-1, HD)
        back = ()
        parts = [lax.psum_scatter(sends, "servers", scatter_dimension=0, tiled=True)]
    root_ds, child_ds, key_sums, value_sums = own_call(shared, keys, values)
    operands = (keys, root_ds, child_ds, prompt_keys, prompt_ds, *parents)
    grad_queries, *totals = query_call(*queries.shape, operands, back)
    parts = totals + parts
    grads = finish_call(key_sums, value_sums, parts, own)
    return (grad_queries, *grads)


def solution(mesh):
    placed = (
        P(("groups", "servers"), None),
        P(None, "heads"),
        P(("groups", "servers"), "heads"),
        P(("groups", "servers"), "heads"),
        P("heads", ("groups", "servers")),
        P(("groups", "servers"), "heads"),
        P(("groups", "servers"), "heads"),
        P(("groups", "servers"), "heads"),
        P(("groups", "servers"), "heads"),
        P("groups", None),
        P("groups"),
        P("groups"),
    )
    return jax.shard_map(
        local,
        mesh=mesh,
        in_specs=placed,
        out_specs=(P(("groups", "servers"), "heads"),) * 5,
        check_vma=False,
    )
```
